32 devices in a mesh: shard: 4 (over y, x), ctx: 4 (over z), tensor: 2 (over core).
Axes of the slice: x: 2, y: 2, z: 4, core: 2. Of those that a mesh axis runs over, the one named last changes fastest.
Arguments:
- tokens: bfloat16 [8, 1024, 2304], P('shard', 'ctx'), may hold values from -6 to 6
- lengths: int32 [8], P('shard'), may hold values from 256 to 1024, as said below
- span_order: int32 [8], replicated, may hold values from 0 to 7, each once
- attn_gain: bfloat16 [2304], P('shard'), may hold values from 0.5 to 1.5
- w_query: bfloat16 [2304, 2304], P('shard', 'tensor'), may hold values from -0.125 to 0.125
- w_key: bfloat16 [2304, 2304], P('shard', 'tensor'), may hold values from -0.125 to 0.125
- w_value: bfloat16 [2304, 2304], P('shard', 'tensor'), may hold values from -0.125 to 0.125
- w_out: bfloat16 [2304, 2304], P('tensor', 'shard'), may hold values from -4 to 4
- mlp_gain: bfloat16 [2304], P('shard'), may hold values from 0.5 to 1.5
- w_gate: bfloat16 [2304, 5760], P('shard', 'tensor'), may hold values from -0.125 to 0.125
- w_up: bfloat16 [2304, 5760], P('shard', 'tensor'), may hold values from -0.125 to 0.125
- w_down: bfloat16 [5760, 2304], P('tensor', 'shard'), may hold values from -0.4375 to 0.4375
- cotangent: bfloat16 [8, 1024, 2304], P('shard', 'ctx'), may hold values from -6 to 6
Outputs:
- layer_out: bfloat16 [8, 1024, 2304], P('shard', 'ctx')
- grad_tokens: float32 [8, 1024, 2304], P('shard', 'ctx')
- grad_attn_gain: float32 [2304], P('shard')
- grad_query: float32 [2304, 2304], P('shard', 'tensor')
- grad_key: float32 [2304, 2304], P('shard', 'tensor')
- grad_value: float32 [2304, 2304], P('shard', 'tensor')
- grad_out: float32 [2304, 2304], P('tensor', 'shard')
- grad_mlp_gain: float32 [2304], P('shard')
- grad_gate: float32 [2304, 5760], P('shard', 'tensor')
- grad_up: float32 [2304, 5760], P('shard', 'tensor')
- grad_down: float32 [5760, 2304], P('tensor', 'shard')
The draws below stay inside these ranges and needn't reach their ends.
Inputs may be any that keep to these rules, and one draw needn't show every extreme that they name: `lengths`: rows of a slot whose position is its length or more are padding; some slot is full and some slot holds exactly 256 tokens. `span_order`: each block place of a slot appears once.
All inputs are finite; a program needn't handle non-finite values.
Results may differ from the reference program's by a relative error of at most 0.015.
Values may be sent and summed in bfloat16 or wider, within the bound.
A program may use at most 272 MiB of HBM per device.

```python
import jax
import jax.numpy as jnp
from jax import lax

D = 2304
H = 36
HD = 64
FF = 5760
SLOT = 1024
MIN_LEN = 256
HQ = 2304
SLOTS = 8
SPANS = 8
SPAN = 128


def draw_lengths(key, part):
    key_draw, key_pick = jax.random.split(jax.random.fold_in(key, 11))
    drawn = jax.random.randint(key_draw, (SLOTS,), (MIN_LEN + SLOT) // 2, SLOT + 1)
    picked = jax.random.permutation(key_pick, SLOTS)
    drawn = drawn.at[picked[0]].set(SLOT)
    drawn = drawn.at[picked[1]].set(MIN_LEN)
    return drawn.astype(jnp.int32)


def raised(entries, stream_key, source, target, blocks, factor):
    def block_of(dim):
        return (jnp.arange(entries.shape[dim]) // (entries.shape[dim] // blocks)).reshape((-1,) + (1,) * (entries.ndim - 1 - dim))

    near = jax.random.permutation(stream_key, blocks)[block_of(target)]
    second = (block_of(target) + blocks // 2) % blocks
    return jnp.where((block_of(source) == near) | (block_of(source) == second), factor * entries, entries)


def block_scale(rng, shape, pieces, smallest, high):
    def one(position, shards_of):
        heights = jax.random.uniform(jax.random.fold_in(jax.random.fold_in(rng, 6), position), (shards_of,), jnp.float32, smallest / len(pieces), high / len(pieces))
        return jnp.repeat(jnp.exp(heights), shape[position] // shards_of).reshape((-1,) + (1,) * (len(shape) - position - 1))

    level = one(*pieces[0])
    for cut in pieces[1:]:
        level = level * one(*cut)
    return level


def bell_draw(stream_key, shape, deviation, bound, shards=(), kind=jnp.bfloat16):
    factor_of = block_scale(stream_key, shape, shards, -0.22, 0.18) if shards else 1.0
    values = jax.random.normal(stream_key, shape, jnp.float32) * deviation * factor_of
    return jnp.minimum(jnp.maximum(values, -bound), bound).astype(kind)


def gaussian_with(own_key, shape, scale, limit, cuts, heavy, kind=jnp.bfloat16):
    values = scale * jax.random.normal(own_key, shape, jnp.float32)
    if cuts:
        values = values * block_scale(own_key, shape, cuts, -0.22, 0.18)
    return jnp.clip(raised(values, jax.random.fold_in(own_key, 3), *heavy), -limit, limit).astype(kind)


def setup_inputs(seed: int = 0) -> dict:
    key_list = jax.random.split(jax.random.key(seed), 14)
    return {
        "tokens": bell_draw(key_list[0], (SLOTS, SLOT, D), 1.0, 6.0, ((0, 4), (1, 4))),
        "lengths": draw_lengths(jax.random.fold_in(key_list[13], 71), 0),
        "span_order": jax.random.permutation(key_list[2], SPANS).astype(jnp.int32),
        "attn_gain": jnp.clip(1.0 + 0.1 * jax.random.normal(key_list[3], (D,), jnp.float32), 0.5, 1.5).astype(jnp.bfloat16),
        "w_query": bell_draw(key_list[4], (D, HQ), D ** -0.5, 0.125, ((0, 4), (1, 2))),
        "w_key": bell_draw(key_list[5], (D, HQ), D ** -0.5, 0.125, ((0, 4), (1, 2))),
        "w_value": bell_draw(key_list[6], (D, HQ), D ** -0.5, 0.125, ((0, 4), (1, 2))),
        "w_out": bell_draw(key_list[7], (HQ, D), (max(1, HQ // 1024)) ** -0.5, 4.0, ((0, 2), (1, 4))),
        "mlp_gain": jnp.clip(1.0 + 0.1 * jax.random.normal(key_list[8], (D,), jnp.float32), 0.5, 1.5).astype(jnp.bfloat16),
        "w_gate": bell_draw(key_list[9], (D, FF), D ** -0.5, 0.125, ((0, 4), (1, 2))),
        "w_up": bell_draw(key_list[10], (D, FF), D ** -0.5, 0.125, ((0, 4), (1, 2))),
        "w_down": bell_draw(key_list[11], (FF, D), (max(1, FF // 32)) ** -0.5, 0.4375, ((0, 2), (1, 4))),
        "cotangent": gaussian_with(key_list[12], (SLOTS, SLOT, D), 1.0, 6.0, ((0, 4), (1, 4)), (1, 2, 4, 2.0)),
    }


NORM_EPS = 1e-05
ROPE_BASE = 10000.0
BRANCH_SCALE = 1.4 / 40.0 ** 0.5
PRECISE = lax.Precision.HIGHEST

@jax.custom_vjp
def low(v):
    return lax.optimization_barrier(v.astype(jnp.bfloat16)).astype(jnp.float32)

@jax.custom_vjp
def low_back(v):
    return v

def low_keep(v):
    return (low(v), None)

def low_pass(kept, grad):
    return (grad,)

def back_keep(v):
    return (v, None)

def back_low(kept, grad):
    return (low(grad),)
low.defvjp(low_keep, low_pass)
low_back.defvjp(back_keep, back_low)

def rms_norm(values_in, gain_vec):
    inverse = lax.rsqrt(lax.optimization_barrier(jnp.mean(values_in * values_in, axis=-1, keepdims=True)) + NORM_EPS)
    return values_in * inverse * gain_vec

def rotate(values_in, cos_table, sin_table):
    half_dim = values_in.shape[-1] // 2
    lead_part = values_in[..., :half_dim]
    tail_part = values_in[..., half_dim:]
    return jnp.concatenate([lead_part * cos_table - tail_part * sin_table, tail_part * cos_table + lead_part * sin_table], axis=-1)

def matmul(left_mat, right_mat):
    return jnp.dot(left_mat, right_mat, precision=PRECISE, preferred_element_type=jnp.float32)

def block_forward(params, tokens, positions, live_mask):
    attn_gain, w_query, w_key, w_value, w_out, mlp_gain, w_gate, w_up, w_down = params
    row_count = tokens.shape[0]
    frequency = ROPE_BASE ** (-(jnp.arange(HD // 2) * 2).astype(jnp.float32) / HD)
    angles = positions.astype(jnp.float32)[:, None] * frequency[None, :]
    cos_table = jnp.cos(angles)[:, None, :]
    sin_table = jnp.sin(angles)[:, None, :]
    first_in = low(rms_norm(tokens, attn_gain))
    query_rot = low(rotate(low_back(matmul(first_in, w_query)).reshape(row_count, H, HD), cos_table, sin_table))
    key_rot = low(rotate(low_back(matmul(first_in, w_key)).reshape(row_count, H, HD), cos_table, sin_table))
    value_low = low(low_back(matmul(first_in, w_value))).reshape(row_count, H, HD)
    scores = low_back(jnp.einsum('qhd,khd->hqk', query_rot, key_rot, precision=PRECISE) * HD ** (-0.5))
    allowed = (positions[None, :] <= positions[:, None]) & live_mask[None, :]
    scores = jnp.where(allowed[None], scores, -1e+30)
    row_top = lax.optimization_barrier(jnp.max(scores, axis=-1, keepdims=True))
    weights = jnp.exp(scores - row_top)
    probs_low = low(weights / lax.optimization_barrier(jnp.sum(weights, axis=-1, keepdims=True)))
    attend = low(low_back(jnp.einsum('hqk,khd->qhd', probs_low, value_low, precision=PRECISE))).reshape(row_count, H * HD)
    attn_out = low_back(matmul(attend, w_out))
    middle = tokens + BRANCH_SCALE * attn_out
    second_in = low(rms_norm(middle, mlp_gain))
    gate_proj = low_back(matmul(second_in, w_gate))
    up_proj = low_back(matmul(second_in, w_up))
    hidden = low(jax.nn.silu(gate_proj) * up_proj)
    mlp_out = low_back(matmul(hidden, w_down))
    return (middle + BRANCH_SCALE * mlp_out) * live_mask[:, None].astype(tokens.dtype)

def add_up(left_val, right_val):
    return left_val + right_val

def reference(tokens, lengths, span_order, attn_gain, w_query, w_key, w_value, w_out, mlp_gain, w_gate, w_up, w_down, cotangent):
    params = tuple((weight.astype(jnp.float32) for weight in (attn_gain, w_query, w_key, w_value, w_out, mlp_gain, w_gate, w_up, w_down)))
    offsets = jnp.arange(SPAN, dtype=jnp.int32)
    positions = (span_order[:, None].astype(jnp.int32) * SPAN + offsets[None, :]).reshape(SLOT).astype(jnp.int32)

    def one_slot(totals, slot_item):
        slot_tokens, length, slot_cot = slot_item
        live_mask = positions < length

        def forward(params_in, tokens_in):
            return block_forward(params_in, tokens_in, positions, live_mask)
        slot_out, pullback = jax.vjp(forward, params, slot_tokens.astype(jnp.float32))
        slot_grads, grad_in = pullback(slot_cot.astype(jnp.float32))
        totals = jax.tree.map(add_up, totals, slot_grads)
        return (totals, (slot_out.astype(jnp.bfloat16), grad_in))
    zero_grads = jax.tree.map(jnp.zeros_like, params)
    totals, (out_blocks, grad_blocks) = lax.scan(one_slot, zero_grads, (tokens, lengths, cotangent))
    return (out_blocks, grad_blocks, totals[0], totals[1], totals[2], totals[3], totals[4], totals[5], totals[6], totals[7], totals[8])
```

```python
import functools
import math

import jax
import jax.numpy as jnp
from jax import lax
from jax.sharding import PartitionSpec as P

HD = 64


NORM_EPS = 1e-05
ROPE_BASE = 10000.0
BRANCH_SCALE = 1.4 / math.sqrt(40.0)
CONTRACT_ROWS = (((0,), (0,)), ((), ()))
CONTRACT_COLS = (((1,), (1,)), ((), ()))


def row_product(left_mat, right_mat):
    return lax.dot_general(left_mat, right_mat, CONTRACT_ROWS, preferred_element_type=jnp.float32)


def col_product(left_mat, right_mat):
    return lax.dot_general(left_mat, right_mat, CONTRACT_COLS, preferred_element_type=jnp.float32)


def plain_product(left_mat, right_mat):
    return jnp.dot(left_mat, right_mat, preferred_element_type=jnp.float32)


def rope_tables(positions, head_dim):
    frequency = ROPE_BASE ** (-(jnp.arange(head_dim // 2) * 2).astype(jnp.float32) / head_dim)
    angles = positions.astype(jnp.float32)[:, None] * frequency[None, :]
    return (jnp.cos(angles)[:, None, :], jnp.sin(angles)[:, None, :])


def rotate(values_in, cos_table, sin_table, sign_dir):
    half_dim = values_in.shape[-1] // 2
    lead_part = values_in[..., :half_dim]
    tail_part = values_in[..., half_dim:]
    turned = sin_table * sign_dir
    return jnp.concatenate(
        [lead_part * cos_table - tail_part * turned, tail_part * cos_table + lead_part * turned],
        axis=-1,
    )


def norm_parts(values_in):
    inverse = lax.rsqrt(jnp.mean(values_in * values_in, axis=-1, keepdims=True) + NORM_EPS)
    return (values_in * inverse, inverse)


def norm_back(grad_in, normed, inverse, gain_vec):
    scaled = grad_in * gain_vec
    return inverse * (scaled - normed * jnp.mean(scaled * normed, axis=-1, keepdims=True))


def gather_all(
    tokens,
    lengths,
    span_order,
    attn_gain,
    w_query,
    w_key,
    w_value,
    w_out,
    mlp_gain,
    w_gate,
    w_up,
    w_down,
    cotangent,
):
    slot_count, row_count, width = tokens.shape
    local_heads = w_query.shape[1] // HD
    span_rows = row_count // 2
    offsets = jnp.arange(span_rows, dtype=jnp.int32)
    all_pos = (span_order[:, None] * span_rows + offsets[None, :]).reshape(-1)
    own_pos = lax.dynamic_slice_in_dim(all_pos, lax.axis_index("ctx") * row_count, row_count)
    cos_own, sin_own = rope_tables(own_pos, HD)
    causal = all_pos[None, :] <= own_pos[:, None]
    score_scale = HD ** (-0.5)

    def masked_scores(query_b, key_all, allowed):
        raw_scores = (
            jnp.einsum("qhd,khd->hqk", query_b, key_all, preferred_element_type=jnp.float32)
            * score_scale
        )
        return jnp.where(allowed[None], raw_scores, -1e30)

    out_blocks = []
    grad_blocks = []
    totals = None
    for slot_index in range(slot_count):
        length = lengths[slot_index]
        gain_one = lax.all_gather(attn_gain, "shard", axis=0, tiled=True)
        query_w = lax.all_gather(w_query, "shard", axis=0, tiled=True)
        key_w = lax.all_gather(w_key, "shard", axis=0, tiled=True)
        value_w = lax.all_gather(w_value, "shard", axis=0, tiled=True)
        out_w = lax.all_gather(w_out, "shard", axis=1, tiled=True)
        gain_two = lax.all_gather(mlp_gain, "shard", axis=0, tiled=True)
        gate_w = lax.all_gather(w_gate, "shard", axis=0, tiled=True)
        up_w = lax.all_gather(w_up, "shard", axis=0, tiled=True)
        down_w = lax.all_gather(w_down, "shard", axis=1, tiled=True)
        live_mask = (own_pos < length).astype(jnp.float32)[:, None]
        run_allowed = causal & (all_pos < length)[None, :]
        gain_a = gain_one.astype(jnp.float32)
        gain_b = gain_two.astype(jnp.float32)
        residual_in = tokens[slot_index].astype(jnp.float32)
        normed_one, inverse_one = norm_parts(residual_in)
        first_in = (normed_one * gain_a).astype(jnp.bfloat16)
        query_f = plain_product(first_in, query_w).reshape(row_count, local_heads, HD)
        key_f = plain_product(first_in, key_w).reshape(row_count, local_heads, HD)
        value_b = plain_product(first_in, value_w).astype(jnp.bfloat16)
        run_query_b = rotate(query_f, cos_own, sin_own, 1.0).astype(jnp.bfloat16)
        key_b = rotate(key_f, cos_own, sin_own, 1.0).astype(jnp.bfloat16).reshape(row_count, -1)
        run_key_all = lax.all_gather(key_b, "ctx", axis=0, tiled=True)
        value_all = lax.all_gather(value_b, "ctx", axis=0, tiled=True)
        run_key_all = run_key_all.reshape(-1, local_heads, HD)
        value_all = value_all.reshape(-1, local_heads, HD)
        scores = masked_scores(run_query_b, run_key_all, run_allowed)
        row_top = jnp.max(scores, axis=-1, keepdims=True)
        weights = jnp.exp(scores - row_top)
        row_total = jnp.sum(weights, axis=-1, keepdims=True)
        log_total = row_top + jnp.log(row_total)
        probs_low = (weights / row_total).astype(jnp.bfloat16)
        attend = (
            jnp.einsum("hqk,khd->qhd", probs_low, value_all, preferred_element_type=jnp.float32)
            .astype(jnp.bfloat16)
            .reshape(row_count, -1)
        )
        attn_out = lax.psum(plain_product(attend, out_w), "tensor")
        middle = residual_in + BRANCH_SCALE * attn_out
        normed_two, inverse_two = norm_parts(middle)
        second_in = (normed_two * gain_b).astype(jnp.bfloat16)
        gate_proj = plain_product(second_in, gate_w)
        up_proj = plain_product(second_in, up_w)
        gate_sig = jax.nn.sigmoid(gate_proj)
        gate_act = gate_proj * gate_sig
        hidden = (gate_act * up_proj).astype(jnp.bfloat16)
        mlp_out = lax.psum(plain_product(hidden, down_w).astype(jnp.bfloat16), "tensor").astype(
            jnp.float32
        )
        layer_rows = ((middle + BRANCH_SCALE * mlp_out) * live_mask).astype(jnp.bfloat16)
        grad_y = cotangent[slot_index].astype(jnp.float32) * live_mask
        grad_mlp = (BRANCH_SCALE * grad_y).astype(jnp.bfloat16)
        grad_down_w = row_product(hidden, grad_mlp)
        grad_hidden = col_product(grad_mlp, down_w)
        grad_gate_b = (
            grad_hidden * up_proj * gate_sig * (1.0 + gate_proj * (1.0 - gate_sig))
        ).astype(jnp.bfloat16)
        grad_up_b = (grad_hidden * gate_act).astype(jnp.bfloat16)
        grad_gate_w = row_product(second_in, grad_gate_b)
        grad_up_w = row_product(second_in, grad_up_b)
        grad_second = lax.psum(
            col_product(grad_gate_b, gate_w) + col_product(grad_up_b, up_w), "tensor"
        )
        grad_gain_two = jnp.sum(grad_second * normed_two, axis=0)
        grad_middle = grad_y + norm_back(grad_second, normed_two, inverse_two, gain_b)
        grad_attn = (BRANCH_SCALE * grad_middle).astype(jnp.bfloat16)
        grad_out_w = row_product(attend, grad_attn)
        grad_attend = (
            col_product(grad_attn, out_w).astype(jnp.bfloat16).reshape(row_count, local_heads, HD)
        )
        probs_new = jnp.exp(masked_scores(run_query_b, run_key_all, run_allowed) - log_total)
        grad_probs = jnp.einsum(
            "qhd,khd->hqk", grad_attend, value_all, preferred_element_type=jnp.float32
        )
        grad_scores = (
            probs_new * (grad_probs - jnp.sum(probs_new * grad_probs, axis=-1, keepdims=True))
        ).astype(jnp.bfloat16)
        grad_query_f = (
            jnp.einsum("hqk,khd->qhd", grad_scores, run_key_all, preferred_element_type=jnp.float32)
            * score_scale
        )
        grad_key_all = (
            jnp.einsum("hqk,qhd->khd", grad_scores, run_query_b, preferred_element_type=jnp.float32)
            * score_scale
        )
        grad_value_all = jnp.einsum(
            "hqk,qhd->khd",
            probs_new.astype(jnp.bfloat16),
            grad_attend,
            preferred_element_type=jnp.float32,
        )
        grad_key_own = lax.psum_scatter(
            grad_key_all.reshape(grad_key_all.shape[0], -1), "ctx", scatter_dimension=0, tiled=True
        )
        grad_value_own = lax.psum_scatter(
            grad_value_all.reshape(grad_value_all.shape[0], -1),
            "ctx",
            scatter_dimension=0,
            tiled=True,
        )
        grad_query_b = (
            rotate(grad_query_f, cos_own, sin_own, -1.0).astype(jnp.bfloat16).reshape(row_count, -1)
        )
        grad_key_b = (
            rotate(grad_key_own.reshape(row_count, local_heads, HD), cos_own, sin_own, -1.0)
            .astype(jnp.bfloat16)
            .reshape(row_count, -1)
        )
        grad_value_b = grad_value_own.astype(jnp.bfloat16)
        grad_query_w = row_product(first_in, grad_query_b)
        grad_key_w = row_product(first_in, grad_key_b)
        grad_value_w = row_product(first_in, grad_value_b)
        grad_first = lax.psum(
            (
                col_product(grad_query_b, query_w)
                + col_product(grad_key_b, key_w)
                + col_product(grad_value_b, value_w)
            ).astype(jnp.bfloat16),
            "tensor",
        ).astype(jnp.float32)
        grad_gain_one = jnp.sum(grad_first * normed_one, axis=0)
        grad_rows = grad_middle + norm_back(grad_first, normed_one, inverse_one, gain_a)
        slot_grads = (
            grad_gain_one,
            grad_query_w,
            grad_key_w,
            grad_value_w,
            grad_out_w,
            grad_gain_two,
            grad_gate_w,
            grad_up_w,
            grad_down_w,
        )
        layer_rows, grad_rows, slot_grads = (layer_rows, grad_rows, slot_grads)
        out_blocks.append(layer_rows)
        grad_blocks.append(grad_rows)
        if totals is None:
            totals = slot_grads
        else:
            totals = tuple(
                (left_val + right_val for left_val, right_val in zip(totals, slot_grads))
            )
    (
        sum_gain_one,
        sum_query,
        sum_key,
        sum_value,
        sum_out,
        sum_gain_two,
        sum_gate,
        sum_up,
        sum_down,
    ) = totals
    spread = (
        lax.psum_scatter(sum_gain_one, ("shard", "ctx"), scatter_dimension=0, tiled=True),
        lax.psum_scatter(sum_query, ("shard", "ctx"), scatter_dimension=0, tiled=True),
        lax.psum_scatter(sum_key, ("shard", "ctx"), scatter_dimension=0, tiled=True),
        lax.psum_scatter(sum_value, ("shard", "ctx"), scatter_dimension=0, tiled=True),
        lax.psum_scatter(sum_out, ("shard", "ctx"), scatter_dimension=1, tiled=True),
        lax.psum_scatter(sum_gain_two, ("shard", "ctx"), scatter_dimension=0, tiled=True),
        lax.psum_scatter(sum_gate, ("shard", "ctx"), scatter_dimension=0, tiled=True),
        lax.psum_scatter(sum_up, ("shard", "ctx"), scatter_dimension=0, tiled=True),
        lax.psum_scatter(sum_down, ("shard", "ctx"), scatter_dimension=1, tiled=True),
    )
    (
        part_gain_one,
        part_query,
        part_key,
        part_value,
        part_out,
        part_gain_two,
        part_gate,
        part_up,
        part_down,
    ) = spread
    final = (
        lax.all_gather(part_gain_one.astype(jnp.bfloat16), "ctx", axis=0, tiled=True).astype(
            part_gain_one.dtype
        ),
        lax.all_gather(part_query.astype(jnp.bfloat16), "ctx", axis=0, tiled=True).astype(
            part_query.dtype
        ),
        lax.all_gather(part_key.astype(jnp.bfloat16), "ctx", axis=0, tiled=True).astype(
            part_key.dtype
        ),
        lax.all_gather(part_value.astype(jnp.bfloat16), "ctx", axis=0, tiled=True).astype(
            part_value.dtype
        ),
        lax.all_gather(part_out.astype(jnp.bfloat16), "ctx", axis=1, tiled=True).astype(
            part_out.dtype
        ),
        lax.all_gather(part_gain_two.astype(jnp.bfloat16), "ctx", axis=0, tiled=True).astype(
            part_gain_two.dtype
        ),
        lax.all_gather(part_gate.astype(jnp.bfloat16), "ctx", axis=0, tiled=True).astype(
            part_gate.dtype
        ),
        lax.all_gather(part_up.astype(jnp.bfloat16), "ctx", axis=0, tiled=True).astype(
            part_up.dtype
        ),
        lax.all_gather(part_down.astype(jnp.bfloat16), "ctx", axis=1, tiled=True).astype(
            part_down.dtype
        ),
    )
    layer_out = jnp.stack(out_blocks, axis=0)
    grad_tokens = jnp.stack(grad_blocks, axis=0)
    return (
        layer_out,
        grad_tokens,
        final[0],
        final[1],
        final[2],
        final[3],
        final[4],
        final[5],
        final[6],
        final[7],
        final[8],
    )


def swap_pairs():
    return [(0, 1), (1, 0)]


def line_gather(block, axis, size):
    place = lax.axis_index(axis)
    ups = [block]
    downs = [block]
    for step in range(1, size):
        ups.append(lax.ppermute(ups[-1], axis, [(i, i + 1) for i in range(step - 1, size - 1)]))
        downs.append(lax.ppermute(downs[-1], axis, [(i, i - 1) for i in range(1, size - step + 1)]))
    return [block] + [
        jnp.where(place >= step, ups[step], downs[size - step]) for step in range(1, size)
    ]


def line_scatter(parts, axis, size):
    up = None
    down = None
    for step in range(1, size):
        up_part = parts[step]
        down_part = parts[size - step]
        if up is not None:
            up_part = (up_part.astype(jnp.float32) + up.astype(jnp.float32)).astype(jnp.bfloat16)
            down_part = (down_part.astype(jnp.float32) + down.astype(jnp.float32)).astype(
                jnp.bfloat16
            )
        up = lax.ppermute(up_part, axis, [(i, i + 1) for i in range(min(step, size - 1))])
        down = lax.ppermute(down_part, axis, [(i, i - 1) for i in range(max(size - step, 1), size)])
    return parts[0].astype(jnp.float32) + up.astype(jnp.float32) + down.astype(jnp.float32)


def column_split(
    shape,
    tokens,
    lengths,
    span_order,
    attn_gain,
    w_query,
    w_key,
    w_value,
    w_out,
    mlp_gain,
    w_gate,
    w_up,
    w_down,
    cotangent,
):
    shards, lines, cores = shape["shard"], shape["ctx"], shape["tensor"]
    line = lax.axis_index("ctx")
    core = lax.axis_index("tensor")
    per_half = lines // cores
    owner = core == line // per_half
    sub = line % per_half
    slot_count, row_count, width = tokens.shape
    all_rows = row_count * lines
    heads = w_query.shape[1] * cores // lines // HD
    head_cols = heads * HD
    unit_cols = w_gate.shape[1] * cores // lines

    def column_piece(weights):
        cut = [
            lax.dynamic_slice_in_dim(w, sub * (w.shape[1] // per_half), w.shape[1] // per_half, 1)
            for w in weights
        ]
        return jnp.concatenate(cut, axis=1) if len(cut) > 1 else cut[0]

    def row_piece(w):
        return lax.dynamic_slice_in_dim(w, sub * (w.shape[0] // per_half), w.shape[0] // per_half, 0)

    def to_pair(piece):
        rows = piece.shape[0] // cores
        keep = lax.dynamic_slice_in_dim(piece, core * rows, rows, 0)
        give = lax.dynamic_slice_in_dim(piece, (1 - core) * rows, rows, 0)
        got = lax.ppermute(give, "tensor", swap_pairs())
        return jnp.where(owner, keep, got)

    def gather_columns(weights):
        return lax.all_gather(to_pair(column_piece(weights)), ("shard", "tensor"), axis=0, tiled=True)

    def gather_rows(w):
        mine = to_pair(row_piece(w))
        got = lax.all_gather(mine, ("shard", "tensor"), axis=0, tiled=True)
        got = got.reshape(shards, cores * mine.shape[0], mine.shape[1])
        return jnp.transpose(got, (1, 0, 2)).reshape(cores * mine.shape[0], -1)

    def spread(piece):
        got = lax.all_gather(piece, ("ctx", "tensor"), axis=0, tiled=True)
        got = got.reshape(lines, cores, piece.shape[0], piece.shape[1])
        return lax.dynamic_slice_in_dim(got, core * per_half, per_half, 0)

    def reduce_columns(grad, count):
        piece = lax.psum_scatter(
            grad.astype(jnp.bfloat16), ("shard", "tensor"), scatter_dimension=0, tiled=True
        )
        got = spread(piece).astype(jnp.float32)
        each = grad.shape[1] // count
        return [
            jnp.transpose(got[..., k * each : (k + 1) * each], (1, 2, 0, 3)).reshape(
                width // shards, per_half * each
            )
            for k in range(count)
        ]

    def reduce_rows(grad):
        rows = grad.shape[0]
        grad = grad.astype(jnp.bfloat16).reshape(rows, shards, width // shards)
        grad = jnp.transpose(grad, (1, 0, 2)).reshape(shards * rows, width // shards)
        piece = lax.psum_scatter(grad, ("shard", "tensor"), scatter_dimension=0, tiled=True)
        return spread(piece).astype(jnp.float32).reshape(per_half * rows, width // shards)

    def line_all(block):
        return jnp.concatenate(line_gather(block, "ctx", lines), axis=0)

    def line_sum(partial):
        partial = partial.astype(jnp.bfloat16)
        parts = [partial[k * row_count : (k + 1) * row_count] for k in range(lines)]
        return line_scatter(parts, "ctx", lines)

    length = lengths[core]
    offsets = jnp.arange(row_count // 2, dtype=jnp.int32)
    stored_pos = (span_order[:, None] * (row_count // 2) + offsets[None, :]).reshape(lines, row_count)
    ring_pos = stored_pos[(line - jnp.arange(lines)) % lines].reshape(-1)
    own_pos = ring_pos[:row_count]
    cos_all, sin_all = rope_tables(ring_pos, HD)
    live_all = (ring_pos < length).astype(jnp.float32)[:, None]
    live_own = live_all[:row_count]
    allowed = (ring_pos[None, :] <= ring_pos[:, None]) & (ring_pos < length)[None, :]
    score_scale = HD ** (-0.5)

    gains = lax.all_gather(jnp.stack([attn_gain, mlp_gain]), "shard", axis=1, tiled=True)
    gain_a = gains[0].astype(jnp.float32)
    gain_b = gains[1].astype(jnp.float32)
    own_tokens = lax.dynamic_index_in_dim(tokens, core, 0, keepdims=False)
    own_cot = lax.dynamic_index_in_dim(cotangent, core, 0, keepdims=False)

    all_tokens = line_all(own_tokens)
    qkv_w = gather_columns([w_query, w_key, w_value])
    out_w = gather_rows(w_out)
    gate_up_w = gather_columns([w_gate, w_up])
    down_w = gather_rows(w_down)

    first_in = (norm_parts(all_tokens.astype(jnp.float32))[0] * gain_a).astype(jnp.bfloat16)
    qkv = plain_product(first_in, qkv_w)
    as_heads = lambda v: v.reshape(all_rows, heads, HD)
    query_b = rotate(as_heads(qkv[:, :head_cols]), cos_all, sin_all, 1.0).astype(jnp.bfloat16)
    key_b = rotate(as_heads(qkv[:, head_cols : 2 * head_cols]), cos_all, sin_all, 1.0).astype(
        jnp.bfloat16
    )
    value_b = as_heads(qkv[:, 2 * head_cols :]).astype(jnp.bfloat16)

    def masked_scores():
        raw_scores = (
            jnp.einsum("qhd,khd->hqk", query_b, key_b, preferred_element_type=jnp.float32)
            * score_scale
        )
        return jnp.where(allowed[None], raw_scores, -1e30)

    scores = masked_scores()
    row_top = jnp.max(scores, axis=-1, keepdims=True)
    weights = jnp.exp(scores - row_top)
    row_total = jnp.sum(weights, axis=-1, keepdims=True)
    log_total = row_top + jnp.log(row_total)
    probs_low = (weights / row_total).astype(jnp.bfloat16)
    attend = (
        jnp.einsum("hqk,khd->qhd", probs_low, value_b, preferred_element_type=jnp.float32)
        .astype(jnp.bfloat16)
        .reshape(all_rows, head_cols)
    )
    own_x = own_tokens.astype(jnp.float32)
    middle = own_x + BRANCH_SCALE * line_sum(plain_product(attend, out_w))
    normed_two, inverse_two = norm_parts(middle)
    second_in = line_all((normed_two * gain_b).astype(jnp.bfloat16))
    all_cot = line_all(own_cot).astype(jnp.float32) * live_all
    grad_mlp = (BRANCH_SCALE * all_cot).astype(jnp.bfloat16)

    gate_up = plain_product(second_in, gate_up_w)
    gate_proj = gate_up[:, :unit_cols]
    up_proj = gate_up[:, unit_cols:]
    gate_sig = jax.nn.sigmoid(gate_proj)
    gate_act = gate_proj * gate_sig
    hidden = (gate_act * up_proj).astype(jnp.bfloat16)
    grad_hidden = col_product(grad_mlp, down_w)
    grad_gate_b = (
        grad_hidden * up_proj * gate_sig * (1.0 + gate_proj * (1.0 - gate_sig))
    ).astype(jnp.bfloat16)
    grad_up_b = (grad_hidden * gate_act).astype(jnp.bfloat16)
    grad_gate_up = jnp.concatenate([grad_gate_b, grad_up_b], axis=1)
    grad_second = line_sum(col_product(grad_gate_up, gate_up_w))
    mlp_out = line_sum(plain_product(hidden, down_w))
    layer_rows = ((middle + BRANCH_SCALE * mlp_out) * live_own).astype(jnp.bfloat16)
    own_dy = own_cot.astype(jnp.float32) * live_own
    grad_gain_two = jnp.sum(grad_second * normed_two, axis=0)
    grad_middle = own_dy + norm_back(grad_second, normed_two, inverse_two, gain_b)
    grad_attn = line_all((BRANCH_SCALE * grad_middle).astype(jnp.bfloat16))

    final_down = reduce_rows(row_product(hidden, grad_mlp))
    final_gate, final_up = reduce_columns(row_product(second_in, grad_gate_up), 2)

    grad_attend = col_product(grad_attn, out_w).astype(jnp.bfloat16).reshape(all_rows, heads, HD)
    final_out = reduce_rows(row_product(attend, grad_attn))
    probs_new = jnp.exp(masked_scores() - log_total)
    grad_probs = jnp.einsum("qhd,khd->hqk", grad_attend, value_b, preferred_element_type=jnp.float32)
    grad_scores = (
        probs_new * (grad_probs - jnp.sum(probs_new * grad_probs, axis=-1, keepdims=True))
    ).astype(jnp.bfloat16)
    grad_query_f = (
        jnp.einsum("hqk,khd->qhd", grad_scores, key_b, preferred_element_type=jnp.float32)
        * score_scale
    )
    grad_key_f = (
        jnp.einsum("hqk,qhd->khd", grad_scores, query_b, preferred_element_type=jnp.float32)
        * score_scale
    )
    grad_value_f = jnp.einsum(
        "hqk,qhd->khd",
        probs_new.astype(jnp.bfloat16),
        grad_attend,
        preferred_element_type=jnp.float32,
    )
    as_columns = lambda v: v.astype(jnp.bfloat16).reshape(all_rows, head_cols)
    grad_qkv = jnp.concatenate(
        [
            as_columns(rotate(grad_query_f, cos_all, sin_all, -1.0)),
            as_columns(rotate(grad_key_f, cos_all, sin_all, -1.0)),
            as_columns(grad_value_f),
        ],
        axis=1,
    )
    grad_first = line_sum(col_product(grad_qkv, qkv_w))
    final_query, final_key, final_value = reduce_columns(row_product(first_in, grad_qkv), 3)
    normed_one, inverse_one = norm_parts(own_x)
    grad_gain_one = jnp.sum(grad_first * normed_one, axis=0)
    grad_rows = grad_middle + norm_back(grad_first, normed_one, inverse_one, gain_a)

    gain_sums = lax.psum(
        jnp.stack([grad_gain_one, grad_gain_two]), ("shard", "ctx", "tensor")
    )
    gain_sums = lax.dynamic_slice_in_dim(
        gain_sums, lax.axis_index("shard") * (width // shards), width // shards, 1
    )

    def both_slots(own):
        other = lax.ppermute(own, "tensor", swap_pairs())
        return jnp.stack(
            [jnp.where(core == 0, own, other), jnp.where(core == 0, other, own)], axis=0
        )

    layer_out = both_slots(layer_rows)
    grad_tokens = both_slots(grad_rows.astype(jnp.bfloat16)).astype(jnp.float32)
    return (
        layer_out,
        grad_tokens,
        gain_sums[0],
        final_query,
        final_key,
        final_value,
        final_out,
        gain_sums[1],
        final_gate,
        final_up,
        final_down,
    )


def local(shape, *arrays):
    shards, lines, cores = shape["shard"], shape["ctx"], shape["tensor"]
    tokens, w_query, w_gate = arrays[0], arrays[4], arrays[9]
    fits = (
        cores == 2
        and tokens.shape[0] == cores
        and lines % cores == 0
        and (w_query.shape[1] * cores) % (lines * HD) == 0
        and (w_gate.shape[1] * cores) % (lines * cores) == 0
        and w_query.shape[0] % cores == 0
    )
    if fits:
        return column_split(shape, *arrays)
    return gather_all(*arrays)


def solution(mesh):
    placed = (
        P("shard", "ctx", None),
        P("shard"),
        P(),
        P("shard"),
        P("shard", "tensor"),
        P("shard", "tensor"),
        P("shard", "tensor"),
        P("tensor", "shard"),
        P("shard"),
        P("shard", "tensor"),
        P("shard", "tensor"),
        P("tensor", "shard"),
        P("shard", "ctx", None),
    )
    return jax.shard_map(
        functools.partial(local, dict(mesh.shape)),
        mesh=mesh,
        in_specs=placed,
        out_specs=(
            P("shard", "ctx", None),
            P("shard", "ctx", None),
            P("shard"),
            P("shard", "tensor"),
            P("shard", "tensor"),
            P("shard", "tensor"),
            P("tensor", "shard"),
            P("shard"),
            P("shard", "tensor"),
            P("shard", "tensor"),
            P("tensor", "shard"),
        ),
        check_vma=False,
    )
```

```python
import functools
import math

import jax
import jax.numpy as jnp
from jax import lax
from jax.experimental import pallas as pl
from jax.experimental.pallas import tpu as pltpu
from jax.sharding import PartitionSpec as P

HD = 64


NORM_EPS = 1e-05
ROPE_BASE = 10000.0
BRANCH_SCALE = 1.4 / math.sqrt(40.0)
CONTRACT_ROWS = (((0,), (0,)), ((), ()))
CONTRACT_COLS = (((1,), (1,)), ((), ()))


def row_product(left_mat, right_mat):
    return lax.dot_general(left_mat, right_mat, CONTRACT_ROWS, preferred_element_type=jnp.float32)


def col_product(left_mat, right_mat):
    return lax.dot_general(left_mat, right_mat, CONTRACT_COLS, preferred_element_type=jnp.float32)


def plain_product(left_mat, right_mat):
    return jnp.dot(left_mat, right_mat, preferred_element_type=jnp.float32)


def rope_tables(positions, head_dim):
    frequency = ROPE_BASE ** (-(jnp.arange(head_dim // 2) * 2).astype(jnp.float32) / head_dim)
    angles = positions.astype(jnp.float32)[:, None] * frequency[None, :]
    return (jnp.cos(angles)[:, None, :], jnp.sin(angles)[:, None, :])


def rotate(values_in, cos_table, sin_table, sign_dir):
    half_dim = values_in.shape[-1] // 2
    lead_part = values_in[..., :half_dim]
    tail_part = values_in[..., half_dim:]
    turned = sin_table * sign_dir
    return jnp.concatenate(
        [lead_part * cos_table - tail_part * turned, tail_part * cos_table + lead_part * turned],
        axis=-1,
    )


def norm_parts(values_in):
    inverse = lax.rsqrt(jnp.mean(values_in * values_in, axis=-1, keepdims=True) + NORM_EPS)
    return (values_in * inverse, inverse)


def norm_back(grad_in, normed, inverse, gain_vec):
    scaled = grad_in * gain_vec
    return inverse * (scaled - normed * jnp.mean(scaled * normed, axis=-1, keepdims=True))


def gather_all(
    tokens,
    lengths,
    span_order,
    attn_gain,
    w_query,
    w_key,
    w_value,
    w_out,
    mlp_gain,
    w_gate,
    w_up,
    w_down,
    cotangent,
):
    slot_count, row_count, width = tokens.shape
    local_heads = w_query.shape[1] // HD
    span_rows = row_count // 2
    offsets = jnp.arange(span_rows, dtype=jnp.int32)
    all_pos = (span_order[:, None] * span_rows + offsets[None, :]).reshape(-1)
    own_pos = lax.dynamic_slice_in_dim(all_pos, lax.axis_index("ctx") * row_count, row_count)
    cos_own, sin_own = rope_tables(own_pos, HD)
    causal = all_pos[None, :] <= own_pos[:, None]
    score_scale = HD ** (-0.5)

    def masked_scores(query_b, key_all, allowed):
        raw_scores = (
            jnp.einsum("qhd,khd->hqk", query_b, key_all, preferred_element_type=jnp.float32)
            * score_scale
        )
        return jnp.where(allowed[None], raw_scores, -1e30)

    out_blocks = []
    grad_blocks = []
    totals = None
    for slot_index in range(slot_count):
        length = lengths[slot_index]
        gain_one = lax.all_gather(attn_gain, "shard", axis=0, tiled=True)
        query_w = lax.all_gather(w_query, "shard", axis=0, tiled=True)
        key_w = lax.all_gather(w_key, "shard", axis=0, tiled=True)
        value_w = lax.all_gather(w_value, "shard", axis=0, tiled=True)
        out_w = lax.all_gather(w_out, "shard", axis=1, tiled=True)
        gain_two = lax.all_gather(mlp_gain, "shard", axis=0, tiled=True)
        gate_w = lax.all_gather(w_gate, "shard", axis=0, tiled=True)
        up_w = lax.all_gather(w_up, "shard", axis=0, tiled=True)
        down_w = lax.all_gather(w_down, "shard", axis=1, tiled=True)
        live_mask = (own_pos < length).astype(jnp.float32)[:, None]
        run_allowed = causal & (all_pos < length)[None, :]
        gain_a = gain_one.astype(jnp.float32)
        gain_b = gain_two.astype(jnp.float32)
        residual_in = tokens[slot_index].astype(jnp.float32)
        normed_one, inverse_one = norm_parts(residual_in)
        first_in = (normed_one * gain_a).astype(jnp.bfloat16)
        query_f = plain_product(first_in, query_w).reshape(row_count, local_heads, HD)
        key_f = plain_product(first_in, key_w).reshape(row_count, local_heads, HD)
        value_b = plain_product(first_in, value_w).astype(jnp.bfloat16)
        run_query_b = rotate(query_f, cos_own, sin_own, 1.0).astype(jnp.bfloat16)
        key_b = rotate(key_f, cos_own, sin_own, 1.0).astype(jnp.bfloat16).reshape(row_count, -1)
        run_key_all = lax.all_gather(key_b, "ctx", axis=0, tiled=True)
        value_all = lax.all_gather(value_b, "ctx", axis=0, tiled=True)
        run_key_all = run_key_all.reshape(-1, local_heads, HD)
        value_all = value_all.reshape(-1, local_heads, HD)
        scores = masked_scores(run_query_b, run_key_all, run_allowed)
        row_top = jnp.max(scores, axis=-1, keepdims=True)
        weights = jnp.exp(scores - row_top)
        row_total = jnp.sum(weights, axis=-1, keepdims=True)
        log_total = row_top + jnp.log(row_total)
        probs_low = (weights / row_total).astype(jnp.bfloat16)
        attend = (
            jnp.einsum("hqk,khd->qhd", probs_low, value_all, preferred_element_type=jnp.float32)
            .astype(jnp.bfloat16)
            .reshape(row_count, -1)
        )
        attn_out = lax.psum(plain_product(attend, out_w), "tensor")
        middle = residual_in + BRANCH_SCALE * attn_out
        normed_two, inverse_two = norm_parts(middle)
        second_in = (normed_two * gain_b).astype(jnp.bfloat16)
        gate_proj = plain_product(second_in, gate_w)
        up_proj = plain_product(second_in, up_w)
        gate_sig = jax.nn.sigmoid(gate_proj)
        gate_act = gate_proj * gate_sig
        hidden = (gate_act * up_proj).astype(jnp.bfloat16)
        mlp_out = lax.psum(plain_product(hidden, down_w).astype(jnp.bfloat16), "tensor").astype(
            jnp.float32
        )
        layer_rows = ((middle + BRANCH_SCALE * mlp_out) * live_mask).astype(jnp.bfloat16)
        grad_y = cotangent[slot_index].astype(jnp.float32) * live_mask
        grad_mlp = (BRANCH_SCALE * grad_y).astype(jnp.bfloat16)
        grad_down_w = row_product(hidden, grad_mlp)
        grad_hidden = col_product(grad_mlp, down_w)
        grad_gate_b = (
            grad_hidden * up_proj * gate_sig * (1.0 + gate_proj * (1.0 - gate_sig))
        ).astype(jnp.bfloat16)
        grad_up_b = (grad_hidden * gate_act).astype(jnp.bfloat16)
        grad_gate_w = row_product(second_in, grad_gate_b)
        grad_up_w = row_product(second_in, grad_up_b)
        grad_second = lax.psum(
            col_product(grad_gate_b, gate_w) + col_product(grad_up_b, up_w), "tensor"
        )
        grad_gain_two = jnp.sum(grad_second * normed_two, axis=0)
        grad_middle = grad_y + norm_back(grad_second, normed_two, inverse_two, gain_b)
        grad_attn = (BRANCH_SCALE * grad_middle).astype(jnp.bfloat16)
        grad_out_w = row_product(attend, grad_attn)
        grad_attend = (
            col_product(grad_attn, out_w).astype(jnp.bfloat16).reshape(row_count, local_heads, HD)
        )
        probs_new = jnp.exp(masked_scores(run_query_b, run_key_all, run_allowed) - log_total)
        grad_probs = jnp.einsum(
            "qhd,khd->hqk", grad_attend, value_all, preferred_element_type=jnp.float32
        )
        grad_scores = (
            probs_new * (grad_probs - jnp.sum(probs_new * grad_probs, axis=-1, keepdims=True))
        ).astype(jnp.bfloat16)
        grad_query_f = (
            jnp.einsum("hqk,khd->qhd", grad_scores, run_key_all, preferred_element_type=jnp.float32)
            * score_scale
        )
        grad_key_all = (
            jnp.einsum("hqk,qhd->khd", grad_scores, run_query_b, preferred_element_type=jnp.float32)
            * score_scale
        )
        grad_value_all = jnp.einsum(
            "hqk,qhd->khd",
            probs_new.astype(jnp.bfloat16),
            grad_attend,
            preferred_element_type=jnp.float32,
        )
        grad_key_own = lax.psum_scatter(
            grad_key_all.reshape(grad_key_all.shape[0], -1), "ctx", scatter_dimension=0, tiled=True
        )
        grad_value_own = lax.psum_scatter(
            grad_value_all.reshape(grad_value_all.shape[0], -1),
            "ctx",
            scatter_dimension=0,
            tiled=True,
        )
        grad_query_b = (
            rotate(grad_query_f, cos_own, sin_own, -1.0).astype(jnp.bfloat16).reshape(row_count, -1)
        )
        grad_key_b = (
            rotate(grad_key_own.reshape(row_count, local_heads, HD), cos_own, sin_own, -1.0)
            .astype(jnp.bfloat16)
            .reshape(row_count, -1)
        )
        grad_value_b = grad_value_own.astype(jnp.bfloat16)
        grad_query_w = row_product(first_in, grad_query_b)
        grad_key_w = row_product(first_in, grad_key_b)
        grad_value_w = row_product(first_in, grad_value_b)
        grad_first = lax.psum(
            (
                col_product(grad_query_b, query_w)
                + col_product(grad_key_b, key_w)
                + col_product(grad_value_b, value_w)
            ).astype(jnp.bfloat16),
            "tensor",
        ).astype(jnp.float32)
        grad_gain_one = jnp.sum(grad_first * normed_one, axis=0)
        grad_rows = grad_middle + norm_back(grad_first, normed_one, inverse_one, gain_a)
        slot_grads = (
            grad_gain_one,
            grad_query_w,
            grad_key_w,
            grad_value_w,
            grad_out_w,
            grad_gain_two,
            grad_gate_w,
            grad_up_w,
            grad_down_w,
        )
        layer_rows, grad_rows, slot_grads = (layer_rows, grad_rows, slot_grads)
        out_blocks.append(layer_rows)
        grad_blocks.append(grad_rows)
        if totals is None:
            totals = slot_grads
        else:
            totals = tuple(
                (left_val + right_val for left_val, right_val in zip(totals, slot_grads))
            )
    (
        sum_gain_one,
        sum_query,
        sum_key,
        sum_value,
        sum_out,
        sum_gain_two,
        sum_gate,
        sum_up,
        sum_down,
    ) = totals
    spread = (
        lax.psum_scatter(sum_gain_one, ("shard", "ctx"), scatter_dimension=0, tiled=True),
        lax.psum_scatter(sum_query, ("shard", "ctx"), scatter_dimension=0, tiled=True),
        lax.psum_scatter(sum_key, ("shard", "ctx"), scatter_dimension=0, tiled=True),
        lax.psum_scatter(sum_value, ("shard", "ctx"), scatter_dimension=0, tiled=True),
        lax.psum_scatter(sum_out, ("shard", "ctx"), scatter_dimension=1, tiled=True),
        lax.psum_scatter(sum_gain_two, ("shard", "ctx"), scatter_dimension=0, tiled=True),
        lax.psum_scatter(sum_gate, ("shard", "ctx"), scatter_dimension=0, tiled=True),
        lax.psum_scatter(sum_up, ("shard", "ctx"), scatter_dimension=0, tiled=True),
        lax.psum_scatter(sum_down, ("shard", "ctx"), scatter_dimension=1, tiled=True),
    )
    (
        part_gain_one,
        part_query,
        part_key,
        part_value,
        part_out,
        part_gain_two,
        part_gate,
        part_up,
        part_down,
    ) = spread
    final = (
        lax.all_gather(part_gain_one.astype(jnp.bfloat16), "ctx", axis=0, tiled=True).astype(
            part_gain_one.dtype
        ),
        lax.all_gather(part_query.astype(jnp.bfloat16), "ctx", axis=0, tiled=True).astype(
            part_query.dtype
        ),
        lax.all_gather(part_key.astype(jnp.bfloat16), "ctx", axis=0, tiled=True).astype(
            part_key.dtype
        ),
        lax.all_gather(part_value.astype(jnp.bfloat16), "ctx", axis=0, tiled=True).astype(
            part_value.dtype
        ),
        lax.all_gather(part_out.astype(jnp.bfloat16), "ctx", axis=1, tiled=True).astype(
            part_out.dtype
        ),
        lax.all_gather(part_gain_two.astype(jnp.bfloat16), "ctx", axis=0, tiled=True).astype(
            part_gain_two.dtype
        ),
        lax.all_gather(part_gate.astype(jnp.bfloat16), "ctx", axis=0, tiled=True).astype(
            part_gate.dtype
        ),
        lax.all_gather(part_up.astype(jnp.bfloat16), "ctx", axis=0, tiled=True).astype(
            part_up.dtype
        ),
        lax.all_gather(part_down.astype(jnp.bfloat16), "ctx", axis=1, tiled=True).astype(
            part_down.dtype
        ),
    )
    layer_out = jnp.stack(out_blocks, axis=0)
    grad_tokens = jnp.stack(grad_blocks, axis=0)
    return (
        layer_out,
        grad_tokens,
        final[0],
        final[1],
        final[2],
        final[3],
        final[4],
        final[5],
        final[6],
        final[7],
        final[8],
    )


LANES = 128
QUERY_TILE = 256


def lane_partner(values_in):
    lane = lax.broadcasted_iota(jnp.int32, values_in.shape, 1) % HD
    return jnp.where(
        lane < HD // 2,
        -pltpu.roll(values_in, LANES - HD // 2, 1),
        pltpu.roll(values_in, HD // 2, 1),
    )


def head_lanes(values_in, head):
    lane = lax.broadcasted_iota(jnp.int32, values_in.shape, 1)
    return jnp.where(lane // HD == head, values_in, jnp.zeros_like(values_in))


def tile_allowed(rows, start, length):
    key = lax.broadcasted_iota(jnp.int32, (rows, QUERY_TILE), 0)
    query = lax.broadcasted_iota(jnp.int32, (rows, QUERY_TILE), 1) + start
    return (key <= query) & (key < length)


def attend_kernel(
    heads, span, order, length, q_in, k_in, v_in, cos, sin, out, q_out, k_out, v_out, log_out,
    q_sort, k_sort, v_sort, turned,
):
    rows = q_in.shape[0]
    pair = pl.program_id(0)
    for block in range(rows // span):
        place = pl.ds(pl.multiple_of(order[block] * span, span), span)
        stored = slice(block * span, (block + 1) * span)
        q_sort[place, :] = q_in[stored, :]
        k_sort[place, :] = k_in[stored, :]
        v_sort[place, :] = v_in[stored, :]
    queries = q_sort[...]
    keys = k_sort[...]
    q_out[...] = (queries * cos[...] + lane_partner(queries) * sin[...]).astype(jnp.bfloat16)
    k_out[...] = (keys * cos[...] + lane_partner(keys) * sin[...]).astype(jnp.bfloat16)
    v_out[...] = v_sort[...].astype(jnp.bfloat16)
    values_t = jnp.transpose(v_out[...])
    turned[...] = jnp.zeros_like(turned)
    log_out[...] = jnp.zeros_like(log_out)
    for head in range(LANES // HD):

        @pl.when(pair * (LANES // HD) + head < heads)
        def _():
            for start in range(0, rows, QUERY_TILE):
                used = start + QUERY_TILE
                query = head_lanes(q_out[start:used, :] * (HD**-0.5), head).astype(jnp.bfloat16)
                scores = col_product(k_out[:used, :], query)
                scores = jnp.where(tile_allowed(used, start, length[0]), scores, -1e30)
                top = jnp.max(scores, axis=0, keepdims=True)
                weights = jnp.exp(scores - top)
                total = jnp.sum(weights, axis=0, keepdims=True)
                probs = (weights * (1.0 / total)).astype(jnp.bfloat16)
                turned[head * HD : (head + 1) * HD, start:used] = plain_product(
                    values_t[head * HD : (head + 1) * HD, :used], probs
                )
                log_out[0, head : head + 1, start:used] = top + jnp.log(total)

    q_sort[...] = jnp.transpose(turned[...])
    for block in range(rows // span):
        place = pl.ds(pl.multiple_of(order[block] * span, span), span)
        out[block * span : (block + 1) * span, :] = q_sort[place, :].astype(jnp.bfloat16)


def attend_back_kernel(
    heads, span, order, length, q_in, k_in, v_in, log_in, o_in, do_in, cos, sin, grads,
    o_sort, do_sort, dq_turned, dq_sum, dk_sum, dv_sum, piece, sems,
):
    rows = q_in.shape[0]
    pair = pl.program_id(0)
    pairs = pl.num_programs(0)
    for block in range(rows // span):
        place = pl.ds(pl.multiple_of(order[block] * span, span), span)
        stored = slice(block * span, (block + 1) * span)
        o_sort[place, :] = o_in[stored, :].astype(jnp.float32)
        do_sort[place, :] = do_in[stored, :].astype(jnp.float32)
    means_t = jnp.transpose(o_sort[...] * do_sort[...])
    keys_t = jnp.transpose(k_in[...])
    dq_turned[...] = jnp.zeros_like(dq_turned)
    dk_sum[...] = jnp.zeros_like(dk_sum)
    dv_sum[...] = jnp.zeros_like(dv_sum)
    for head in range(LANES // HD):

        @pl.when(pair * (LANES // HD) + head < heads)
        def _():
            inner = jnp.sum(means_t[head * HD : (head + 1) * HD, :], axis=0, keepdims=True)
            for start in range(0, rows, QUERY_TILE):
                used = start + QUERY_TILE
                query = head_lanes(q_in[start:used, :] * (HD**-0.5), head).astype(jnp.bfloat16)
                grad_o = head_lanes(do_sort[start:used, :], head).astype(jnp.bfloat16)
                scores = col_product(k_in[:used, :], query)
                probs = jnp.where(
                    tile_allowed(used, start, length[0]),
                    jnp.exp(scores - log_in[0, head : head + 1, start:used]),
                    0.0,
                )
                grad_p = col_product(v_in[:used, :], grad_o)
                grad_s = (probs * (grad_p - inner[:, start:used])).astype(jnp.bfloat16)
                dv_sum[:used, :] += plain_product(probs.astype(jnp.bfloat16), grad_o)
                dk_sum[:used, :] += plain_product(grad_s, query)
                dq_turned[head * HD : (head + 1) * HD, start:used] = plain_product(
                    keys_t[head * HD : (head + 1) * HD, :used], grad_s
                )

    grad_q = jnp.transpose(dq_turned[...]) * (HD**-0.5)
    grad_k = dk_sum[...]
    dq_sum[...] = grad_q * cos[...] - lane_partner(grad_q) * sin[...]
    dk_sum[...] = grad_k * cos[...] - lane_partner(grad_k) * sin[...]
    copies = []
    for which, total in enumerate((dq_sum, dk_sum, dv_sum)):
        for block in range(rows // span):
            place = pl.ds(pl.multiple_of(order[block] * span, span), span)
            piece[which, block * span : (block + 1) * span, :] = total[place, :].astype(jnp.bfloat16)
        column = pl.multiple_of((which * pairs + pair) * LANES, LANES)
        copies.append(
            pltpu.make_async_copy(
                piece.at[which], grads.at[:, pl.ds(column, LANES)], sems.at[which]
            )
        )
        copies[-1].start()
    for copy in copies:
        copy.wait()


def attend_forward(heads, span, order, length, qkv, cos, sin):
    rows = qkv.shape[0]
    pairs = qkv.shape[1] // (3 * LANES)
    column = lambda offset: pl.BlockSpec((rows, LANES), lambda i, *_: (0, offset + i))
    fixed = pl.BlockSpec((rows, LANES), lambda i, *_: (0, 0))
    flat = jax.ShapeDtypeStruct((rows, pairs * LANES), jnp.bfloat16)
    return pl.pallas_call(
        functools.partial(attend_kernel, heads, span),
        grid_spec=pltpu.PrefetchScalarGridSpec(
            num_scalar_prefetch=2,
            grid=(pairs,),
            in_specs=[column(0), column(pairs), column(2 * pairs), fixed, fixed],
            out_specs=[column(0)] * 4 + [pl.BlockSpec((1, 8, rows), lambda i, *_: (i, 0, 0))],
            scratch_shapes=[pltpu.VMEM((rows, LANES), jnp.float32)] * 3
            + [pltpu.VMEM((LANES, rows), jnp.float32)],
        ),
        out_shape=[flat] * 4 + [jax.ShapeDtypeStruct((pairs, 8, rows), jnp.float32)],
        compiler_params=pltpu.CompilerParams(vmem_limit_bytes=40 << 20),
        cost_estimate=pl.CostEstimate(
            flops=4 * heads * rows * rows * HD,
            bytes_accessed=rows * pairs * LANES * 24,
            transcendentals=heads * rows * rows,
        ),
        name="attend",
    )(order, length, qkv, qkv, qkv, cos, sin)


def attend_backward(heads, span, order, length, kept, attend, grad_attend, cos, sin):
    queries, keys, values, logs = kept
    rows = queries.shape[0]
    pairs = queries.shape[1] // LANES
    column = pl.BlockSpec((rows, LANES), lambda i, *_: (0, i))
    fixed = pl.BlockSpec((rows, LANES), lambda i, *_: (0, 0))
    return pl.pallas_call(
        functools.partial(attend_back_kernel, heads, span),
        grid_spec=pltpu.PrefetchScalarGridSpec(
            num_scalar_prefetch=2,
            grid=(pairs,),
            in_specs=[column] * 3
            + [pl.BlockSpec((1, 8, rows), lambda i, *_: (i, 0, 0)), column, column, fixed, fixed],
            out_specs=pl.BlockSpec(memory_space=pl.ANY),
            scratch_shapes=[pltpu.VMEM((rows, LANES), jnp.float32)] * 2
            + [pltpu.VMEM((LANES, rows), jnp.float32)]
            + [pltpu.VMEM((rows, LANES), jnp.float32)] * 3
            + [pltpu.VMEM((3, rows, LANES), jnp.bfloat16), pltpu.SemaphoreType.DMA((3,))],
        ),
        out_shape=jax.ShapeDtypeStruct((rows, 3 * pairs * LANES), jnp.bfloat16),
        compiler_params=pltpu.CompilerParams(vmem_limit_bytes=40 << 20),
        cost_estimate=pl.CostEstimate(
            flops=10 * heads * rows * rows * HD,
            bytes_accessed=rows * pairs * LANES * 16,
            transcendentals=heads * rows * rows,
        ),
        name="attend_back",
    )(order, length, queries, keys, values, logs, attend, grad_attend, cos, sin)


def swap_pairs():
    return [(0, 1), (1, 0)]


class LineGather:
    def __init__(self, block, axis, size):
        self.axis, self.size = axis, size
        self.ups, self.downs = [block], [block]

    def step(self):
        done = len(self.ups)
        up_pairs = [(i, i + 1) for i in range(done - 1, self.size - 1)]
        down_pairs = [(i, i - 1) for i in range(1, self.size - done + 1)]
        self.ups.append(lax.ppermute(self.ups[-1], self.axis, up_pairs))
        self.downs.append(lax.ppermute(self.downs[-1], self.axis, down_pairs))

    def held(self):
        return (self.ups[-1], self.downs[-1])

    def hold(self, values):
        self.ups[-1], self.downs[-1] = values

    def near(self, mask):
        place = lax.axis_index(self.axis)
        found = None
        for here in range(self.size):
            there = here ^ mask
            block = self.ups[here - there] if there < here else self.downs[there - here]
            found = block if found is None else jnp.where(place == here, block, found)
        return found

    def before(self, count):
        if count == 0:
            return self.ups[0]
        place = lax.axis_index(self.axis)
        return jnp.where(place >= count, self.ups[count], self.downs[self.size - count])


class LineScatter:
    def __init__(self, parts, axis, size):
        self.axis, self.size, self.parts = axis, size, parts
        self.done = 0
        self.up = self.down = None

    def part(self, offsets):
        place = lax.axis_index(self.axis)
        masks = {}
        for here, there in offsets:
            masks.setdefault(here ^ there, []).append(here)
        found = None
        for mask, places in sorted(masks.items()):
            if found is None:
                found = self.parts[mask]
                continue
            chosen = functools.reduce(jnp.logical_or, [place == here for here in places])
            found = jnp.where(chosen, self.parts[mask], found)
        return found

    def step(self):
        self.done += 1
        gap = self.size - self.done
        ups = [(i, i + gap) for i in range(self.done)]
        downs = [(i, i - gap) for i in range(gap, self.size)]
        up, down = self.part(ups), self.part(downs)
        if self.done > 1:
            up = (up.astype(jnp.float32) + self.up.astype(jnp.float32)).astype(jnp.bfloat16)
            down = (down.astype(jnp.float32) + self.down.astype(jnp.float32)).astype(jnp.bfloat16)
        self.up = lax.ppermute(up, self.axis, [(i, i + 1) for i, _ in ups])
        self.down = lax.ppermute(down, self.axis, [(i, i - 1) for i, _ in downs])

    def held(self):
        return (self.up, self.down)

    def hold(self, values):
        self.up, self.down = values

    def total(self):
        return (
            self.parts[0].astype(jnp.float32)
            + self.up.astype(jnp.float32)
            + self.down.astype(jnp.float32)
        )


def stage(chains, *arrays):
    held = [chain.held() for chain in chains]
    held, arrays = lax.optimization_barrier((held, arrays))
    for chain, values in zip(chains, held):
        chain.hold(values)
    return arrays


def column_split(
    shape,
    tokens,
    lengths,
    span_order,
    attn_gain,
    w_query,
    w_key,
    w_value,
    w_out,
    mlp_gain,
    w_gate,
    w_up,
    w_down,
    cotangent,
):
    shards, lines, cores = shape["shard"], shape["ctx"], shape["tensor"]
    line = lax.axis_index("ctx")
    core = lax.axis_index("tensor")
    per_half = lines // cores
    owner = core == line // per_half
    sub = line % per_half
    slot_count, row_count, width = tokens.shape
    all_rows = row_count * lines
    heads = w_query.shape[1] * cores // lines // HD
    head_cols = heads * HD
    pad_cols = -(-head_cols // LANES) * LANES
    widen = lambda v, dim: jnp.pad(v, [(0, pad_cols - head_cols if d == dim else 0) for d in (0, 1)])
    unit_cols = w_gate.shape[1] * cores // lines

    def column_piece(weights, shape_up=lambda v: v):
        cut = [
            shape_up(
                lax.dynamic_slice_in_dim(w, sub * (w.shape[1] // per_half), w.shape[1] // per_half, 1)
            )
            for w in weights
        ]
        return jnp.concatenate(cut, axis=1) if len(cut) > 1 else cut[0]

    def row_piece(w):
        return lax.dynamic_slice_in_dim(w, sub * (w.shape[0] // per_half), w.shape[0] // per_half, 0)

    def to_pair(piece):
        rows = piece.shape[0] // cores
        keep = lax.dynamic_slice_in_dim(piece, core * rows, rows, 0)
        give = lax.dynamic_slice_in_dim(piece, (1 - core) * rows, rows, 0)
        got = lax.ppermute(give, "tensor", swap_pairs())
        return jnp.where(owner, keep, got)

    def gather_columns(piece):
        return lax.all_gather(to_pair(piece), ("shard", "tensor"), axis=0, tiled=True)

    def gather_rows(w):
        mine = to_pair(row_piece(w))
        got = lax.all_gather(mine, ("shard", "tensor"), axis=0, tiled=True)
        rows = cores * mine.shape[0]
        return jnp.concatenate([got[k * rows : (k + 1) * rows] for k in range(shards)], axis=1)

    def reduce_pair(grad):
        return lax.psum_scatter(grad, ("shard", "tensor"), scatter_dimension=0, tiled=True)

    def by_shard(grad):
        cols = width // shards
        return jnp.concatenate([grad[:, k * cols : (k + 1) * cols] for k in range(shards)], axis=0)

    def gathered_halves(chain):
        rows, cols = chain.ups[0].shape
        ring = jnp.stack([chain.before(k) for k in range(lines)])
        take = lambda half: jnp.stack(
            [
                lax.dynamic_index_in_dim(ring, (line - half * per_half - k) % lines, 0, False)
                for k in range(per_half)
            ]
        )
        other = lax.ppermute(take(1 - core), "tensor", swap_pairs())
        own = take(core)
        first = jnp.where(core == 0, own, other)
        second = jnp.where(core == 0, other, own)
        return [[first[k], second[k]] for k in range(per_half)]

    def spread_columns(chain, count, used):
        pieces = gathered_halves(chain)
        each = pieces[0][0].shape[1] // count
        cut = lambda k: jnp.concatenate(
            [
                jnp.concatenate([piece[:, k * each : k * each + used] for piece in row], axis=1)
                for row in zip(*pieces)
            ],
            axis=0,
        )
        return [cut(k).astype(jnp.float32) for k in range(count)]

    def spread_rows(chain):
        pieces = gathered_halves(chain)
        return jnp.concatenate([p for quarter in pieces for p in quarter], axis=0).astype(
            jnp.float32
        )

    def walk(block):
        return LineGather(block, "ctx", lines)

    def add_up(parts):
        return LineScatter(parts, "ctx", lines)

    def blocks_of(v):
        v = v.astype(jnp.bfloat16)
        return [v[k * row_count : (k + 1) * row_count] for k in range(v.shape[0] // row_count)]

    length = lengths[core]
    offsets = jnp.arange(row_count // 2, dtype=jnp.int32)
    stored_pos = (span_order[:, None] * (row_count // 2) + offsets[None, :]).reshape(lines, row_count)
    ring_pos = stored_pos[line ^ jnp.arange(lines)].reshape(-1)
    own_pos = ring_pos[:row_count]
    span = row_count // 2
    order = ring_pos[::span] // span
    frequency = ROPE_BASE ** (-(jnp.arange(HD // 2) * 2).astype(jnp.float32) / HD)
    angles = jnp.arange(all_rows, dtype=jnp.float32)[:, None] * jnp.tile(frequency, 2 * LANES // HD)
    cos_all, sin_all = jnp.cos(angles), jnp.sin(angles)
    live_all = (ring_pos < length).astype(jnp.float32)[:, None]
    live_own = live_all[:row_count]
    gains = lax.all_gather(jnp.stack([attn_gain, mlp_gain]), "shard", axis=1, tiled=True)
    gain_a = gains[0].astype(jnp.float32)
    gain_b = gains[1].astype(jnp.float32)
    own_tokens = lax.dynamic_index_in_dim(tokens, core, 0, keepdims=False)
    own_cot = lax.dynamic_index_in_dim(cotangent, core, 0, keepdims=False)

    qkv_w = gather_columns(column_piece([w_query, w_key, w_value], lambda v: widen(v, 1)))
    out_w = widen(gather_rows(w_out), 0)
    gate_up_w = gather_columns(column_piece([w_gate, w_up]))
    down_w = gather_rows(w_down)

    tokens_line = walk(own_tokens)
    for _ in range(lines - 1):
        tokens_line.step()
    all_tokens = jnp.concatenate([tokens_line.near(k) for k in range(lines)], axis=0)
    first_in = (norm_parts(all_tokens.astype(jnp.float32))[0] * gain_a).astype(jnp.bfloat16)
    first_in, own_cot = stage([], first_in, own_cot)

    cot_line = walk(own_cot)
    cot_line.step()
    qkv = plain_product(first_in, qkv_w)
    attend, *kept = attend_forward(heads, span, order, length.reshape(1), qkv, cos_all, sin_all)
    attn_part = plain_product(attend, out_w).astype(jnp.bfloat16)
    (attn_part,) = stage([cot_line], attn_part)

    attn_line = add_up(blocks_of(attn_part))
    attn_line.step()
    cot_line.step()
    stage([attn_line, cot_line])
    attn_line.step()
    cot_line.step()
    stage([attn_line, cot_line])
    attn_line.step()
    all_cot = jnp.concatenate([cot_line.near(k) for k in range(lines)], axis=0)
    grad_mlp = (BRANCH_SCALE * (all_cot.astype(jnp.float32) * live_all)).astype(jnp.bfloat16)
    half_rows = all_rows // 2
    grad_hidden = [
        col_product(grad_mlp[k * half_rows : (k + 1) * half_rows], down_w).astype(jnp.float32)
        for k in range(2)
    ]
    grad_hidden = stage([attn_line], *grad_hidden)
    own_x = own_tokens.astype(jnp.float32)
    middle = own_x + BRANCH_SCALE * attn_line.total()
    normed_two, inverse_two = norm_parts(middle)

    second_line = walk((normed_two * gain_b).astype(jnp.bfloat16))
    second_line.step()
    stage([second_line])

    def units(second_half, grad_half):
        gate_up = plain_product(second_half, gate_up_w)
        gate_proj = gate_up[:, :unit_cols]
        up_proj = gate_up[:, unit_cols:]
        gate_sig = jax.nn.sigmoid(gate_proj)
        gate_act = gate_proj * gate_sig
        hidden_half = (gate_act * up_proj).astype(jnp.bfloat16)
        grad_gate_b = (
            grad_half * up_proj * gate_sig * (1.0 + gate_proj * (1.0 - gate_sig))
        ).astype(jnp.bfloat16)
        grad_up_b = (grad_half * gate_act).astype(jnp.bfloat16)
        return hidden_half, jnp.concatenate([grad_gate_b, grad_up_b], axis=1)

    near_half = jnp.concatenate([second_line.near(k) for k in range(lines // 2)], axis=0)
    second_line.step()
    hidden_near, grad_near = units(near_half, grad_hidden[0])
    hidden_near, grad_near = stage([second_line], hidden_near, grad_near)
    second_line.step()
    part_near = col_product(grad_near, gate_up_w).astype(jnp.bfloat16)
    (part_near,) = stage([second_line], part_near)
    far_half = jnp.concatenate([second_line.near(k) for k in range(lines // 2, lines)], axis=0)
    hidden_far, grad_far = units(far_half, grad_hidden[1])
    part_far = col_product(grad_far, gate_up_w).astype(jnp.bfloat16)

    grad_line = add_up(blocks_of(part_near) + blocks_of(part_far))
    grad_line.step()
    hidden = jnp.concatenate([hidden_near, hidden_far], axis=0)
    second_in = jnp.concatenate([near_half, far_half], axis=0)
    grad_gate_up = jnp.concatenate([grad_near, grad_far], axis=0)
    down_grad = by_shard(row_product(hidden, grad_mlp).astype(jnp.bfloat16))
    (down_grad,) = stage([grad_line], down_grad)
    grad_line.step()
    down_piece = reduce_pair(down_grad)
    gate_up_grad = row_product(second_in, grad_gate_up).astype(jnp.bfloat16)
    (gate_up_grad,) = stage([grad_line], gate_up_grad)
    gate_up_piece = reduce_pair(gate_up_grad)
    grad_line.step()
    mlp_part = plain_product(hidden, down_w).astype(jnp.bfloat16)
    (mlp_part,) = stage([grad_line], mlp_part)
    grad_second = grad_line.total()

    own_dy = own_cot.astype(jnp.float32) * live_own
    grad_gain_two = jnp.sum(grad_second * normed_two, axis=0)
    grad_middle = own_dy + norm_back(grad_second, normed_two, inverse_two, gain_b)
    attn_grad_line = walk((BRANCH_SCALE * grad_middle).astype(jnp.bfloat16))
    attn_grad_line.step()
    stage([attn_grad_line])
    attn_grad_line.step()
    (down_piece,) = stage([attn_grad_line], down_piece)
    attn_grad_line.step()
    gate_up_piece, down_piece = stage([attn_grad_line], gate_up_piece, down_piece)
    grad_attn = jnp.concatenate([attn_grad_line.near(k) for k in range(lines)], axis=0)

    down_line = walk(down_piece)
    gate_up_line = walk(gate_up_piece)
    mlp_line = add_up(blocks_of(mlp_part))
    mlp_line.step()
    down_line.step()
    gate_up_line.step()
    out_grad = by_shard(row_product(attend, grad_attn)[:head_cols].astype(jnp.bfloat16))
    out_piece = reduce_pair(out_grad)
    grad_attend = col_product(grad_attn, out_w).astype(jnp.bfloat16)
    grad_qkv = attend_backward(
        heads, span, order, length.reshape(1), kept, attend, grad_attend, cos_all, sin_all
    )
    moving = [mlp_line, down_line, gate_up_line]
    (grad_qkv,) = stage(moving, grad_qkv)
    for chain in moving:
        chain.step()
    first_part = col_product(grad_qkv, qkv_w).astype(jnp.bfloat16)
    qkv_grad = row_product(first_in, grad_qkv).astype(jnp.bfloat16)
    first_part, qkv_grad, out_piece = stage(moving, first_part, qkv_grad, out_piece)
    qkv_piece = reduce_pair(qkv_grad)
    for chain in moving:
        chain.step()
    first_line = add_up(blocks_of(first_part))
    first_line.step()
    stage(moving + [first_line])
    first_line.step()
    layer_rows = ((middle + BRANCH_SCALE * mlp_line.total()) * live_own).astype(jnp.bfloat16)
    final_down = spread_rows(down_line)
    out_line = walk(out_piece)
    out_line.step()
    layer_rows, final_down, qkv_piece = stage(
        [first_line, out_line], layer_rows, final_down, qkv_piece
    )
    first_line.step()
    out_line.step()
    qkv_line = walk(qkv_piece)
    qkv_line.step()
    final_gate, final_up = spread_columns(gate_up_line, 2, unit_cols)
    final_gate, final_up = stage([first_line, out_line, qkv_line], final_gate, final_up)
    qkv_line.step()
    out_line.step()
    grad_first = first_line.total()
    normed_one, inverse_one = norm_parts(own_x)
    grad_gain_one = jnp.sum(grad_first * normed_one, axis=0)
    grad_rows = grad_middle + norm_back(grad_first, normed_one, inverse_one, gain_a)

    gain_sums = lax.psum(jnp.stack([grad_gain_one, grad_gain_two]), ("shard", "ctx", "tensor"))
    gain_sums, grad_rows = stage([qkv_line, out_line], gain_sums, grad_rows)
    qkv_line.step()
    final_out = spread_rows(out_line)
    stage([qkv_line])
    final_query, final_key, final_value = spread_columns(qkv_line, 3, head_cols)
    gain_sums = lax.dynamic_slice_in_dim(
        gain_sums, lax.axis_index("shard") * (width // shards), width // shards, 1
    )

    def both_slots(own):
        other = lax.ppermute(own, "tensor", swap_pairs())
        return jnp.stack(
            [jnp.where(core == 0, own, other), jnp.where(core == 0, other, own)], axis=0
        )

    layer_out = both_slots(layer_rows)
    grad_tokens = both_slots(grad_rows.astype(jnp.bfloat16)).astype(jnp.float32)
    return (
        layer_out,
        grad_tokens,
        gain_sums[0],
        final_query,
        final_key,
        final_value,
        final_out,
        gain_sums[1],
        final_gate,
        final_up,
        final_down,
    )


def local(shape, *arrays):
    shards, lines, cores = shape["shard"], shape["ctx"], shape["tensor"]
    tokens, w_query, w_gate = arrays[0], arrays[4], arrays[9]
    fits = (
        cores == 2
        and tokens.shape[0] == cores
        and lines % cores == 0
        and lines == 4
        and (w_query.shape[1] * cores) % (lines * HD) == 0
        and (w_gate.shape[1] * cores) % (lines * cores) == 0
        and w_query.shape[0] % cores == 0
    )
    if fits:
        return column_split(shape, *arrays)
    return gather_all(*arrays)


def solution(mesh):
    placed = (
        P("shard", "ctx", None),
        P("shard"),
        P(),
        P("shard"),
        P("shard", "tensor"),
        P("shard", "tensor"),
        P("shard", "tensor"),
        P("tensor", "shard"),
        P("shard"),
        P("shard", "tensor"),
        P("shard", "tensor"),
        P("tensor", "shard"),
        P("shard", "ctx", None),
    )
    return jax.shard_map(
        functools.partial(local, dict(mesh.shape)),
        mesh=mesh,
        in_specs=placed,
        out_specs=(
            P("shard", "ctx", None),
            P("shard", "ctx", None),
            P("shard"),
            P("shard", "tensor"),
            P("shard", "tensor"),
            P("shard", "tensor"),
            P("tensor", "shard"),
            P("shard"),
            P("shard", "tensor"),
            P("shard", "tensor"),
            P("tensor", "shard"),
        ),
        check_vma=False,
    )
```

```python
import functools
import math

import jax
import jax.numpy as jnp
from jax import lax
from jax.experimental import pallas as pl
from jax.experimental.pallas import tpu as pltpu
from jax.sharding import PartitionSpec as P

HD = 64


NORM_EPS = 1e-05
ROPE_BASE = 10000.0
BRANCH_SCALE = 1.4 / math.sqrt(40.0)
CONTRACT_ROWS = (((0,), (0,)), ((), ()))
CONTRACT_COLS = (((1,), (1,)), ((), ()))


def row_product(left_mat, right_mat):
    return lax.dot_general(left_mat, right_mat, CONTRACT_ROWS, preferred_element_type=jnp.float32)


def col_product(left_mat, right_mat):
    return lax.dot_general(left_mat, right_mat, CONTRACT_COLS, preferred_element_type=jnp.float32)


def plain_product(left_mat, right_mat):
    return jnp.dot(left_mat, right_mat, preferred_element_type=jnp.float32)


def rope_tables(positions, head_dim):
    frequency = ROPE_BASE ** (-(jnp.arange(head_dim // 2) * 2).astype(jnp.float32) / head_dim)
    angles = positions.astype(jnp.float32)[:, None] * frequency[None, :]
    return (jnp.cos(angles)[:, None, :], jnp.sin(angles)[:, None, :])


def rotate(values_in, cos_table, sin_table, sign_dir):
    half_dim = values_in.shape[-1] // 2
    lead_part = values_in[..., :half_dim]
    tail_part = values_in[..., half_dim:]
    turned = sin_table * sign_dir
    return jnp.concatenate(
        [lead_part * cos_table - tail_part * turned, tail_part * cos_table + lead_part * turned],
        axis=-1,
    )


def norm_parts(values_in):
    inverse = lax.rsqrt(jnp.mean(values_in * values_in, axis=-1, keepdims=True) + NORM_EPS)
    return (values_in * inverse, inverse)


def norm_back(grad_in, normed, inverse, gain_vec):
    scaled = grad_in * gain_vec
    return inverse * (scaled - normed * jnp.mean(scaled * normed, axis=-1, keepdims=True))


def gather_all(
    tokens,
    lengths,
    span_order,
    attn_gain,
    w_query,
    w_key,
    w_value,
    w_out,
    mlp_gain,
    w_gate,
    w_up,
    w_down,
    cotangent,
):
    slot_count, row_count, width = tokens.shape
    local_heads = w_query.shape[1] // HD
    span_rows = row_count // 2
    offsets = jnp.arange(span_rows, dtype=jnp.int32)
    all_pos = (span_order[:, None] * span_rows + offsets[None, :]).reshape(-1)
    own_pos = lax.dynamic_slice_in_dim(all_pos, lax.axis_index("ctx") * row_count, row_count)
    cos_own, sin_own = rope_tables(own_pos, HD)
    causal = all_pos[None, :] <= own_pos[:, None]
    score_scale = HD ** (-0.5)

    def masked_scores(query_b, key_all, allowed):
        raw_scores = (
            jnp.einsum("qhd,khd->hqk", query_b, key_all, preferred_element_type=jnp.float32)
            * score_scale
        )
        return jnp.where(allowed[None], raw_scores, -1e30)

    out_blocks = []
    grad_blocks = []
    totals = None
    for slot_index in range(slot_count):
        length = lengths[slot_index]
        gain_one = lax.all_gather(attn_gain, "shard", axis=0, tiled=True)
        query_w = lax.all_gather(w_query, "shard", axis=0, tiled=True)
        key_w = lax.all_gather(w_key, "shard", axis=0, tiled=True)
        value_w = lax.all_gather(w_value, "shard", axis=0, tiled=True)
        out_w = lax.all_gather(w_out, "shard", axis=1, tiled=True)
        gain_two = lax.all_gather(mlp_gain, "shard", axis=0, tiled=True)
        gate_w = lax.all_gather(w_gate, "shard", axis=0, tiled=True)
        up_w = lax.all_gather(w_up, "shard", axis=0, tiled=True)
        down_w = lax.all_gather(w_down, "shard", axis=1, tiled=True)
        live_mask = (own_pos < length).astype(jnp.float32)[:, None]
        run_allowed = causal & (all_pos < length)[None, :]
        gain_a = gain_one.astype(jnp.float32)
        gain_b = gain_two.astype(jnp.float32)
        residual_in = tokens[slot_index].astype(jnp.float32)
        normed_one, inverse_one = norm_parts(residual_in)
        first_in = (normed_one * gain_a).astype(jnp.bfloat16)
        query_f = plain_product(first_in, query_w).reshape(row_count, local_heads, HD)
        key_f = plain_product(first_in, key_w).reshape(row_count, local_heads, HD)
        value_b = plain_product(first_in, value_w).astype(jnp.bfloat16)
        run_query_b = rotate(query_f, cos_own, sin_own, 1.0).astype(jnp.bfloat16)
        key_b = rotate(key_f, cos_own, sin_own, 1.0).astype(jnp.bfloat16).reshape(row_count, -1)
        run_key_all = lax.all_gather(key_b, "ctx", axis=0, tiled=True)
        value_all = lax.all_gather(value_b, "ctx", axis=0, tiled=True)
        run_key_all = run_key_all.reshape(-1, local_heads, HD)
        value_all = value_all.reshape(-1, local_heads, HD)
        scores = masked_scores(run_query_b, run_key_all, run_allowed)
        row_top = jnp.max(scores, axis=-1, keepdims=True)
        weights = jnp.exp(scores - row_top)
        row_total = jnp.sum(weights, axis=-1, keepdims=True)
        log_total = row_top + jnp.log(row_total)
        probs_low = (weights / row_total).astype(jnp.bfloat16)
        attend = (
            jnp.einsum("hqk,khd->qhd", probs_low, value_all, preferred_element_type=jnp.float32)
            .astype(jnp.bfloat16)
            .reshape(row_count, -1)
        )
        attn_out = lax.psum(plain_product(attend, out_w), "tensor")
        middle = residual_in + BRANCH_SCALE * attn_out
        normed_two, inverse_two = norm_parts(middle)
        second_in = (normed_two * gain_b).astype(jnp.bfloat16)
        gate_proj = plain_product(second_in, gate_w)
        up_proj = plain_product(second_in, up_w)
        gate_sig = jax.nn.sigmoid(gate_proj)
        gate_act = gate_proj * gate_sig
        hidden = (gate_act * up_proj).astype(jnp.bfloat16)
        mlp_out = lax.psum(plain_product(hidden, down_w).astype(jnp.bfloat16), "tensor").astype(
            jnp.float32
        )
        layer_rows = ((middle + BRANCH_SCALE * mlp_out) * live_mask).astype(jnp.bfloat16)
        grad_y = cotangent[slot_index].astype(jnp.float32) * live_mask
        grad_mlp = (BRANCH_SCALE * grad_y).astype(jnp.bfloat16)
        grad_down_w = row_product(hidden, grad_mlp)
        grad_hidden = col_product(grad_mlp, down_w)
        grad_gate_b = (
            grad_hidden * up_proj * gate_sig * (1.0 + gate_proj * (1.0 - gate_sig))
        ).astype(jnp.bfloat16)
        grad_up_b = (grad_hidden * gate_act).astype(jnp.bfloat16)
        grad_gate_w = row_product(second_in, grad_gate_b)
        grad_up_w = row_product(second_in, grad_up_b)
        grad_second = lax.psum(
            col_product(grad_gate_b, gate_w) + col_product(grad_up_b, up_w), "tensor"
        )
        grad_gain_two = jnp.sum(grad_second * normed_two, axis=0)
        grad_middle = grad_y + norm_back(grad_second, normed_two, inverse_two, gain_b)
        grad_attn = (BRANCH_SCALE * grad_middle).astype(jnp.bfloat16)
        grad_out_w = row_product(attend, grad_attn)
        grad_attend = (
            col_product(grad_attn, out_w).astype(jnp.bfloat16).reshape(row_count, local_heads, HD)
        )
        probs_new = jnp.exp(masked_scores(run_query_b, run_key_all, run_allowed) - log_total)
        grad_probs = jnp.einsum(
            "qhd,khd->hqk", grad_attend, value_all, preferred_element_type=jnp.float32
        )
        grad_scores = (
            probs_new * (grad_probs - jnp.sum(probs_new * grad_probs, axis=-1, keepdims=True))
        ).astype(jnp.bfloat16)
        grad_query_f = (
            jnp.einsum("hqk,khd->qhd", grad_scores, run_key_all, preferred_element_type=jnp.float32)
            * score_scale
        )
        grad_key_all = (
            jnp.einsum("hqk,qhd->khd", grad_scores, run_query_b, preferred_element_type=jnp.float32)
            * score_scale
        )
        grad_value_all = jnp.einsum(
            "hqk,qhd->khd",
            probs_new.astype(jnp.bfloat16),
            grad_attend,
            preferred_element_type=jnp.float32,
        )
        grad_key_own = lax.psum_scatter(
            grad_key_all.reshape(grad_key_all.shape[0], -1), "ctx", scatter_dimension=0, tiled=True
        )
        grad_value_own = lax.psum_scatter(
            grad_value_all.reshape(grad_value_all.shape[0], -1),
            "ctx",
            scatter_dimension=0,
            tiled=True,
        )
        grad_query_b = (
            rotate(grad_query_f, cos_own, sin_own, -1.0).astype(jnp.bfloat16).reshape(row_count, -1)
        )
        grad_key_b = (
            rotate(grad_key_own.reshape(row_count, local_heads, HD), cos_own, sin_own, -1.0)
            .astype(jnp.bfloat16)
            .reshape(row_count, -1)
        )
        grad_value_b = grad_value_own.astype(jnp.bfloat16)
        grad_query_w = row_product(first_in, grad_query_b)
        grad_key_w = row_product(first_in, grad_key_b)
        grad_value_w = row_product(first_in, grad_value_b)
        grad_first = lax.psum(
            (
                col_product(grad_query_b, query_w)
                + col_product(grad_key_b, key_w)
                + col_product(grad_value_b, value_w)
            ).astype(jnp.bfloat16),
            "tensor",
        ).astype(jnp.float32)
        grad_gain_one = jnp.sum(grad_first * normed_one, axis=0)
        grad_rows = grad_middle + norm_back(grad_first, normed_one, inverse_one, gain_a)
        slot_grads = (
            grad_gain_one,
            grad_query_w,
            grad_key_w,
            grad_value_w,
            grad_out_w,
            grad_gain_two,
            grad_gate_w,
            grad_up_w,
            grad_down_w,
        )
        layer_rows, grad_rows, slot_grads = (layer_rows, grad_rows, slot_grads)
        out_blocks.append(layer_rows)
        grad_blocks.append(grad_rows)
        if totals is None:
            totals = slot_grads
        else:
            totals = tuple(
                (left_val + right_val for left_val, right_val in zip(totals, slot_grads))
            )
    (
        sum_gain_one,
        sum_query,
        sum_key,
        sum_value,
        sum_out,
        sum_gain_two,
        sum_gate,
        sum_up,
        sum_down,
    ) = totals
    spread = (
        lax.psum_scatter(sum_gain_one, ("shard", "ctx"), scatter_dimension=0, tiled=True),
        lax.psum_scatter(sum_query, ("shard", "ctx"), scatter_dimension=0, tiled=True),
        lax.psum_scatter(sum_key, ("shard", "ctx"), scatter_dimension=0, tiled=True),
        lax.psum_scatter(sum_value, ("shard", "ctx"), scatter_dimension=0, tiled=True),
        lax.psum_scatter(sum_out, ("shard", "ctx"), scatter_dimension=1, tiled=True),
        lax.psum_scatter(sum_gain_two, ("shard", "ctx"), scatter_dimension=0, tiled=True),
        lax.psum_scatter(sum_gate, ("shard", "ctx"), scatter_dimension=0, tiled=True),
        lax.psum_scatter(sum_up, ("shard", "ctx"), scatter_dimension=0, tiled=True),
        lax.psum_scatter(sum_down, ("shard", "ctx"), scatter_dimension=1, tiled=True),
    )
    (
        part_gain_one,
        part_query,
        part_key,
        part_value,
        part_out,
        part_gain_two,
        part_gate,
        part_up,
        part_down,
    ) = spread
    final = (
        lax.all_gather(part_gain_one.astype(jnp.bfloat16), "ctx", axis=0, tiled=True).astype(
            part_gain_one.dtype
        ),
        lax.all_gather(part_query.astype(jnp.bfloat16), "ctx", axis=0, tiled=True).astype(
            part_query.dtype
        ),
        lax.all_gather(part_key.astype(jnp.bfloat16), "ctx", axis=0, tiled=True).astype(
            part_key.dtype
        ),
        lax.all_gather(part_value.astype(jnp.bfloat16), "ctx", axis=0, tiled=True).astype(
            part_value.dtype
        ),
        lax.all_gather(part_out.astype(jnp.bfloat16), "ctx", axis=1, tiled=True).astype(
            part_out.dtype
        ),
        lax.all_gather(part_gain_two.astype(jnp.bfloat16), "ctx", axis=0, tiled=True).astype(
            part_gain_two.dtype
        ),
        lax.all_gather(part_gate.astype(jnp.bfloat16), "ctx", axis=0, tiled=True).astype(
            part_gate.dtype
        ),
        lax.all_gather(part_up.astype(jnp.bfloat16), "ctx", axis=0, tiled=True).astype(
            part_up.dtype
        ),
        lax.all_gather(part_down.astype(jnp.bfloat16), "ctx", axis=1, tiled=True).astype(
            part_down.dtype
        ),
    )
    layer_out = jnp.stack(out_blocks, axis=0)
    grad_tokens = jnp.stack(grad_blocks, axis=0)
    return (
        layer_out,
        grad_tokens,
        final[0],
        final[1],
        final[2],
        final[3],
        final[4],
        final[5],
        final[6],
        final[7],
        final[8],
    )


LANES = 128
QUERY_TILE = 256


def lane_partner(values_in):
    lane = lax.broadcasted_iota(jnp.int32, values_in.shape, 1) % HD
    return jnp.where(
        lane < HD // 2,
        -pltpu.roll(values_in, LANES - HD // 2, 1),
        pltpu.roll(values_in, HD // 2, 1),
    )


def head_lanes(values_in, head):
    lane = lax.broadcasted_iota(jnp.int32, values_in.shape, 1)
    return jnp.where(lane // HD == head, values_in, jnp.zeros_like(values_in))


def tile_allowed(rows, start, length):
    key = lax.broadcasted_iota(jnp.int32, (rows, QUERY_TILE), 0)
    query = lax.broadcasted_iota(jnp.int32, (rows, QUERY_TILE), 1) + start
    return (key <= query) & (key < length)


def attend_kernel(
    heads, span, order, length, q_in, k_in, v_in, cos, sin, out, q_out, k_out, v_out, log_out,
    q_sort, k_sort, v_sort, turned,
):
    rows = q_in.shape[0]
    pair = pl.program_id(0)
    for block in range(rows // span):
        place = pl.ds(pl.multiple_of(order[block] * span, span), span)
        stored = slice(block * span, (block + 1) * span)
        q_sort[place, :] = q_in[stored, :]
        k_sort[place, :] = k_in[stored, :]
        v_sort[place, :] = v_in[stored, :]
    queries = q_sort[...]
    keys = k_sort[...]
    q_out[...] = (queries * cos[...] + lane_partner(queries) * sin[...]).astype(jnp.bfloat16)
    k_out[...] = (keys * cos[...] + lane_partner(keys) * sin[...]).astype(jnp.bfloat16)
    v_out[...] = v_sort[...].astype(jnp.bfloat16)
    values_t = jnp.transpose(v_out[...])
    turned[...] = jnp.zeros_like(turned)
    log_out[...] = jnp.zeros_like(log_out)
    for head in range(LANES // HD):

        @pl.when(pair * (LANES // HD) + head < heads)
        def _():
            for start in range(0, rows, QUERY_TILE):
                used = start + QUERY_TILE
                query = head_lanes(q_out[start:used, :] * (HD**-0.5), head).astype(jnp.bfloat16)
                scores = col_product(k_out[:used, :], query)
                scores = jnp.where(tile_allowed(used, start, length[0]), scores, -1e30)
                top = jnp.max(scores, axis=0, keepdims=True)
                weights = jnp.exp(scores - top)
                total = jnp.sum(weights, axis=0, keepdims=True)
                probs = (weights * (1.0 / total)).astype(jnp.bfloat16)
                turned[head * HD : (head + 1) * HD, start:used] = plain_product(
                    values_t[head * HD : (head + 1) * HD, :used], probs
                )
                log_out[0, head : head + 1, start:used] = top + jnp.log(total)

    q_sort[...] = jnp.transpose(turned[...])
    for block in range(rows // span):
        place = pl.ds(pl.multiple_of(order[block] * span, span), span)
        out[block * span : (block + 1) * span, :] = q_sort[place, :].astype(jnp.bfloat16)


def attend_back_kernel(
    heads, span, order, length, q_in, k_in, v_in, log_in, o_in, do_in, cos, sin, grads,
    o_sort, do_sort, dq_turned, dq_sum, dk_sum, dv_sum, piece, sems,
):
    rows = q_in.shape[0]
    pair = pl.program_id(0)
    pairs = pl.num_programs(0)
    for block in range(rows // span):
        place = pl.ds(pl.multiple_of(order[block] * span, span), span)
        stored = slice(block * span, (block + 1) * span)
        o_sort[place, :] = o_in[stored, :].astype(jnp.float32)
        do_sort[place, :] = do_in[stored, :].astype(jnp.float32)
    means_t = jnp.transpose(o_sort[...] * do_sort[...])
    keys_t = jnp.transpose(k_in[...])
    dq_turned[...] = jnp.zeros_like(dq_turned)
    dk_sum[...] = jnp.zeros_like(dk_sum)
    dv_sum[...] = jnp.zeros_like(dv_sum)
    for head in range(LANES // HD):

        @pl.when(pair * (LANES // HD) + head < heads)
        def _():
            inner = jnp.sum(means_t[head * HD : (head + 1) * HD, :], axis=0, keepdims=True)
            for start in range(0, rows, QUERY_TILE):
                used = start + QUERY_TILE
                query = head_lanes(q_in[start:used, :] * (HD**-0.5), head).astype(jnp.bfloat16)
                grad_o = head_lanes(do_sort[start:used, :], head).astype(jnp.bfloat16)
                scores = col_product(k_in[:used, :], query)
                probs = jnp.where(
                    tile_allowed(used, start, length[0]),
                    jnp.exp(scores - log_in[0, head : head + 1, start:used]),
                    0.0,
                )
                grad_p = col_product(v_in[:used, :], grad_o)
                grad_s = (probs * (grad_p - inner[:, start:used])).astype(jnp.bfloat16)
                dv_sum[:used, :] += plain_product(probs.astype(jnp.bfloat16), grad_o)
                dk_sum[:used, :] += plain_product(grad_s, query)
                dq_turned[head * HD : (head + 1) * HD, start:used] = plain_product(
                    keys_t[head * HD : (head + 1) * HD, :used], grad_s
                )

    grad_q = jnp.transpose(dq_turned[...]) * (HD**-0.5)
    grad_k = dk_sum[...]
    dq_sum[...] = grad_q * cos[...] - lane_partner(grad_q) * sin[...]
    dk_sum[...] = grad_k * cos[...] - lane_partner(grad_k) * sin[...]
    copies = []
    for which, total in enumerate((dq_sum, dk_sum, dv_sum)):
        for block in range(rows // span):
            place = pl.ds(pl.multiple_of(order[block] * span, span), span)
            piece[which, block * span : (block + 1) * span, :] = total[place, :].astype(jnp.bfloat16)
        column = pl.multiple_of((which * pairs + pair) * LANES, LANES)
        copies.append(
            pltpu.make_async_copy(
                piece.at[which], grads.at[:, pl.ds(column, LANES)], sems.at[which]
            )
        )
        copies[-1].start()
    for copy in copies:
        copy.wait()


def attend_forward(heads, span, order, length, qkv, cos, sin):
    rows = qkv.shape[0]
    pairs = qkv.shape[1] // (3 * LANES)
    column = lambda offset: pl.BlockSpec((rows, LANES), lambda i, *_: (0, offset + i))
    fixed = pl.BlockSpec((rows, LANES), lambda i, *_: (0, 0))
    flat = jax.ShapeDtypeStruct((rows, pairs * LANES), jnp.bfloat16)
    return pl.pallas_call(
        functools.partial(attend_kernel, heads, span),
        grid_spec=pltpu.PrefetchScalarGridSpec(
            num_scalar_prefetch=2,
            grid=(pairs,),
            in_specs=[column(0), column(pairs), column(2 * pairs), fixed, fixed],
            out_specs=[column(0)] * 4 + [pl.BlockSpec((1, 8, rows), lambda i, *_: (i, 0, 0))],
            scratch_shapes=[pltpu.VMEM((rows, LANES), jnp.float32)] * 3
            + [pltpu.VMEM((LANES, rows), jnp.float32)],
        ),
        out_shape=[flat] * 4 + [jax.ShapeDtypeStruct((pairs, 8, rows), jnp.float32)],
        compiler_params=pltpu.CompilerParams(vmem_limit_bytes=40 << 20),
        cost_estimate=pl.CostEstimate(
            flops=4 * heads * rows * rows * HD,
            bytes_accessed=rows * pairs * LANES * 24,
            transcendentals=heads * rows * rows,
        ),
        name="attend",
    )(order, length, qkv, qkv, qkv, cos, sin)


def attend_backward(heads, span, order, length, kept, attend, grad_attend, cos, sin):
    queries, keys, values, logs = kept
    rows = queries.shape[0]
    pairs = queries.shape[1] // LANES
    column = pl.BlockSpec((rows, LANES), lambda i, *_: (0, i))
    fixed = pl.BlockSpec((rows, LANES), lambda i, *_: (0, 0))
    return pl.pallas_call(
        functools.partial(attend_back_kernel, heads, span),
        grid_spec=pltpu.PrefetchScalarGridSpec(
            num_scalar_prefetch=2,
            grid=(pairs,),
            in_specs=[column] * 3
            + [pl.BlockSpec((1, 8, rows), lambda i, *_: (i, 0, 0)), column, column, fixed, fixed],
            out_specs=pl.BlockSpec(memory_space=pl.ANY),
            scratch_shapes=[pltpu.VMEM((rows, LANES), jnp.float32)] * 2
            + [pltpu.VMEM((LANES, rows), jnp.float32)]
            + [pltpu.VMEM((rows, LANES), jnp.float32)] * 3
            + [pltpu.VMEM((3, rows, LANES), jnp.bfloat16), pltpu.SemaphoreType.DMA((3,))],
        ),
        out_shape=jax.ShapeDtypeStruct((rows, 3 * pairs * LANES), jnp.bfloat16),
        compiler_params=pltpu.CompilerParams(vmem_limit_bytes=40 << 20),
        cost_estimate=pl.CostEstimate(
            flops=10 * heads * rows * rows * HD,
            bytes_accessed=rows * pairs * LANES * 16,
            transcendentals=heads * rows * rows,
        ),
        name="attend_back",
    )(order, length, queries, keys, values, logs, attend, grad_attend, cos, sin)


def columns_kernel(count, each, used, core, own, other, *outs):
    mine = pl.program_id(0) == core[0]
    for k in range(own.shape[0]):
        rows = jnp.where(mine, own[k].astype(jnp.float32), other[k].astype(jnp.float32))
        for j in range(count):
            outs[j][:, k * used : (k + 1) * used] = rows[:, j * each : j * each + used]


def join_columns(core, own, other, count, each, used):
    pieces, rows, cols = own.shape
    tile = rows // 3 if rows % 48 == 0 else rows
    taken = pl.BlockSpec((pieces, tile, cols), lambda c, r, *_: (0, r, 0))
    given = pl.BlockSpec((tile, pieces * used), lambda c, r, *_: (c * (rows // tile) + r, 0))
    return pl.pallas_call(
        functools.partial(columns_kernel, count, each, used),
        grid_spec=pltpu.PrefetchScalarGridSpec(
            num_scalar_prefetch=1,
            grid=(2, rows // tile),
            in_specs=[taken, taken],
            out_specs=[given] * count,
        ),
        out_shape=[jax.ShapeDtypeStruct((2 * rows, pieces * used), jnp.float32)] * count,
        compiler_params=pltpu.CompilerParams(vmem_limit_bytes=40 << 20),
        cost_estimate=pl.CostEstimate(
            flops=0, bytes_accessed=8 * pieces * rows * (cols + used * count), transcendentals=0
        ),
        name="join_columns",
    )(core, own, other)


def turned_kernel(start, used, core, own, other, out, joined):
    rows = own.shape[1]
    first = core[0] == 0
    left = own[0, :, start : start + used].astype(jnp.float32)
    right = other[0, :, start : start + used].astype(jnp.float32)
    joined[:rows, :] = jnp.where(first, left, right)
    joined[rows:, :] = jnp.where(first, right, left)
    out[...] = jnp.transpose(joined[...])


def join_turned(core, own, other, start, used):
    pieces, rows, cols = own.shape
    taken = pl.BlockSpec((1, rows, cols), lambda k, *_: (k, 0, 0))
    return pl.pallas_call(
        functools.partial(turned_kernel, start, used),
        grid_spec=pltpu.PrefetchScalarGridSpec(
            num_scalar_prefetch=1,
            grid=(pieces,),
            in_specs=[taken, taken],
            out_specs=pl.BlockSpec((used, 2 * rows), lambda k, *_: (k, 0)),
            scratch_shapes=[pltpu.VMEM((2 * rows, used), jnp.float32)],
        ),
        out_shape=jax.ShapeDtypeStruct((pieces * used, 2 * rows), jnp.float32),
        compiler_params=pltpu.CompilerParams(vmem_limit_bytes=40 << 20),
        cost_estimate=pl.CostEstimate(
            flops=0, bytes_accessed=8 * pieces * rows * (cols + used), transcendentals=0
        ),
        name="join_turned",
    )(core, own, other)


def swap_pairs():
    return [(0, 1), (1, 0)]


class LineGather:
    def __init__(self, block, axis, size):
        self.axis, self.size = axis, size
        self.ups, self.downs = [block], [block]

    def step(self):
        done = len(self.ups)
        up_pairs = [(i, i + 1) for i in range(done - 1, self.size - 1)]
        down_pairs = [(i, i - 1) for i in range(1, self.size - done + 1)]
        self.ups.append(lax.ppermute(self.ups[-1], self.axis, up_pairs))
        self.downs.append(lax.ppermute(self.downs[-1], self.axis, down_pairs))

    def held(self):
        return (self.ups[-1], self.downs[-1])

    def hold(self, values):
        self.ups[-1], self.downs[-1] = values

    def near(self, mask):
        place = lax.axis_index(self.axis)
        found = None
        for here in range(self.size):
            there = here ^ mask
            block = self.ups[here - there] if there < here else self.downs[there - here]
            found = block if found is None else jnp.where(place == here, block, found)
        return found

    def at(self, target):
        place = lax.axis_index(self.axis)
        found = self.ups[0]
        for here in range(self.size):
            if here != target:
                block = self.ups[here - target] if target < here else self.downs[target - here]
                found = jnp.where(place == here, block, found)
        return found


class LineScatter:
    def __init__(self, parts, axis, size):
        self.axis, self.size, self.parts = axis, size, parts
        self.done = 0
        self.up = self.down = None

    def part(self, offsets):
        place = lax.axis_index(self.axis)
        masks = {}
        for here, there in offsets:
            masks.setdefault(here ^ there, []).append(here)
        found = None
        for mask, places in sorted(masks.items()):
            if found is None:
                found = self.parts[mask]
                continue
            chosen = functools.reduce(jnp.logical_or, [place == here for here in places])
            found = jnp.where(chosen, self.parts[mask], found)
        return found

    def step(self):
        self.done += 1
        gap = self.size - self.done
        ups = [(i, i + gap) for i in range(self.done)]
        downs = [(i, i - gap) for i in range(gap, self.size)]
        up, down = self.part(ups), self.part(downs)
        if self.done > 1:
            up = (up.astype(jnp.float32) + self.up.astype(jnp.float32)).astype(jnp.bfloat16)
            down = (down.astype(jnp.float32) + self.down.astype(jnp.float32)).astype(jnp.bfloat16)
        self.up = lax.ppermute(up, self.axis, [(i, i + 1) for i, _ in ups])
        self.down = lax.ppermute(down, self.axis, [(i, i - 1) for i, _ in downs])

    def held(self):
        return (self.up, self.down)

    def hold(self, values):
        self.up, self.down = values

    def total(self):
        return (
            self.parts[0].astype(jnp.float32)
            + self.up.astype(jnp.float32)
            + self.down.astype(jnp.float32)
        )


def stage(chains, *arrays):
    held = [chain.held() for chain in chains]
    held, arrays = lax.optimization_barrier((held, arrays))
    for chain, values in zip(chains, held):
        chain.hold(values)
    return arrays


def column_split(
    shape,
    tokens,
    lengths,
    span_order,
    attn_gain,
    w_query,
    w_key,
    w_value,
    w_out,
    mlp_gain,
    w_gate,
    w_up,
    w_down,
    cotangent,
):
    shards, lines, cores = shape["shard"], shape["ctx"], shape["tensor"]
    line = lax.axis_index("ctx")
    core = lax.axis_index("tensor")
    per_half = lines // cores
    owner = core == line // per_half
    sub = line % per_half
    slot_count, row_count, width = tokens.shape
    all_rows = row_count * lines
    heads = w_query.shape[1] * cores // lines // HD
    head_cols = heads * HD
    pad_cols = -(-head_cols // LANES) * LANES
    widen = lambda v, dim: jnp.pad(v, [(0, pad_cols - head_cols if d == dim else 0) for d in (0, 1)])
    unit_cols = w_gate.shape[1] * cores // lines

    def column_piece(weights, shape_up=lambda v: v):
        cut = [
            shape_up(
                lax.dynamic_slice_in_dim(w, sub * (w.shape[1] // per_half), w.shape[1] // per_half, 1)
            )
            for w in weights
        ]
        return jnp.concatenate(cut, axis=1) if len(cut) > 1 else cut[0]

    def turned_piece(w):
        rows = w.shape[0] // per_half
        return jnp.transpose(lax.dynamic_slice_in_dim(w, sub * rows, rows, 0))

    def to_pair(piece):
        rows = piece.shape[0] // cores
        keep = lax.dynamic_slice_in_dim(piece, core * rows, rows, 0)
        give = lax.dynamic_slice_in_dim(piece, (1 - core) * rows, rows, 0)
        got = lax.ppermute(give, "tensor", swap_pairs())
        return jnp.where(owner, keep, got)

    def gather_pair(mine):
        return lax.all_gather(mine, ("shard", "tensor"), axis=0, tiled=True)

    def reduce_pair(grad):
        return lax.psum_scatter(grad, ("shard", "tensor"), scatter_dimension=0, tiled=True)

    def gain_marks(weights, piece):
        used = weights.shape[1]
        total = jnp.sum(
            weights.astype(jnp.float32) * piece[:, :used].astype(jnp.float32), axis=1, keepdims=True
        )
        high = total.astype(jnp.bfloat16)
        low = (total - high.astype(jnp.float32)).astype(jnp.bfloat16)
        return jnp.concatenate([high, low], axis=1)

    def line_pieces(chain):
        found = [chain.at(q) for q in range(lines)]
        halves = [jnp.stack(found[h * per_half : (h + 1) * per_half]) for h in range(cores)]
        own = jnp.where(core == 0, halves[0], halves[1])
        give = jnp.where(core == 0, halves[1], halves[0])
        return own, lax.ppermute(give, "tensor", swap_pairs()), found

    def gain_total(found, column, gain):
        marks = sum(piece[:, column : column + 2].astype(jnp.float32) for piece in found)
        own = jnp.sum(marks, axis=1)
        other = lax.ppermute(own, "tensor", swap_pairs())
        total = jnp.concatenate(
            [jnp.where(core == 0, own, other), jnp.where(core == 0, other, own)]
        )
        return total / gain.astype(jnp.float32)

    def walk(block):
        return LineGather(block, "ctx", lines)

    def add_up(parts):
        return LineScatter(parts, "ctx", lines)

    def blocks_of(v):
        v = v.astype(jnp.bfloat16)
        return [v[k * row_count : (k + 1) * row_count] for k in range(v.shape[0] // row_count)]

    length = lengths[core]
    offsets = jnp.arange(row_count // 2, dtype=jnp.int32)
    stored_pos = (span_order[:, None] * (row_count // 2) + offsets[None, :]).reshape(lines, row_count)
    ring_pos = stored_pos[line ^ jnp.arange(lines)].reshape(-1)
    own_pos = ring_pos[:row_count]
    span = row_count // 2
    order = ring_pos[::span] // span
    frequency = ROPE_BASE ** (-(jnp.arange(HD // 2) * 2).astype(jnp.float32) / HD)
    angles = jnp.arange(all_rows, dtype=jnp.float32)[:, None] * jnp.tile(frequency, 2 * LANES // HD)
    cos_all, sin_all = jnp.cos(angles), jnp.sin(angles)
    live_all = (ring_pos < length).astype(jnp.float32)[:, None]
    live_own = live_all[:row_count]
    core_index = core.astype(jnp.int32).reshape(1)
    own_tokens = lax.dynamic_index_in_dim(tokens, core, 0, keepdims=False)
    own_cot = lax.dynamic_index_in_dim(cotangent, core, 0, keepdims=False)

    tokens_line = walk(own_tokens)
    tokens_line.step()
    qkv_mine = to_pair(column_piece([w_query, w_key, w_value], lambda v: widen(v, 1)))
    qkv_w = gather_pair(qkv_mine)
    w_out, w_gate, w_up, w_down, gain_pair = stage(
        [tokens_line], w_out, w_gate, w_up, w_down, jnp.stack([attn_gain, mlp_gain])
    )
    tokens_line.step()
    gains = lax.all_gather(gain_pair, "shard", axis=1, tiled=True)
    gain_a = gains[0].astype(jnp.float32)
    gain_b = gains[1].astype(jnp.float32)
    out_mine = to_pair(widen(turned_piece(w_out), 1))
    down_mine = to_pair(turned_piece(w_down))
    gate_up_mine = to_pair(column_piece([w_gate, w_up]))
    stage([tokens_line])
    tokens_line.step()
    out_mine, qkv_w = lax.optimization_barrier((out_mine, qkv_w))
    out_w = gather_pair(out_mine)
    own_cot, down_mine = stage([tokens_line], own_cot, down_mine)
    down_w = gather_pair(down_mine)

    cot_line = walk(own_cot)
    cot_line.step()
    all_tokens = jnp.concatenate([tokens_line.near(k) for k in range(lines)], axis=0)
    first_in = (norm_parts(all_tokens.astype(jnp.float32))[0] * gain_a).astype(jnp.bfloat16)
    qkv = plain_product(first_in, qkv_w)
    qkv, gate_up_mine = stage([cot_line], qkv, gate_up_mine)
    gate_up_w = gather_pair(gate_up_mine)

    cot_line.step()
    attend, *kept = attend_forward(heads, span, order, length.reshape(1), qkv, cos_all, sin_all)
    (attend,) = stage([cot_line], attend)

    cot_line.step()
    attn_part = col_product(attend, out_w).astype(jnp.bfloat16)
    attn_line = add_up(blocks_of(attn_part))
    attn_line.step()
    stage([attn_line, cot_line])
    attn_line.step()
    all_cot = jnp.concatenate([cot_line.near(k) for k in range(lines)], axis=0)
    grad_mlp = (BRANCH_SCALE * (all_cot.astype(jnp.float32) * live_all)).astype(jnp.bfloat16)
    (grad_mlp,) = stage([attn_line], grad_mlp)
    attn_line.step()
    half_rows = all_rows // 2
    grad_hidden = [
        plain_product(grad_mlp[k * half_rows : (k + 1) * half_rows], down_w) for k in range(2)
    ]
    grad_hidden = stage([attn_line], *grad_hidden)
    own_x = own_tokens.astype(jnp.float32)
    middle = own_x + BRANCH_SCALE * attn_line.total()
    normed_two, inverse_two = norm_parts(middle)

    second_line = walk((normed_two * gain_b).astype(jnp.bfloat16))
    second_line.step()
    stage([second_line])

    def units(second_half, grad_half):
        gate_up = plain_product(second_half, gate_up_w)
        gate_proj = gate_up[:, :unit_cols]
        up_proj = gate_up[:, unit_cols:]
        gate_sig = jax.nn.sigmoid(gate_proj)
        gate_act = gate_proj * gate_sig
        hidden_half = (gate_act * up_proj).astype(jnp.bfloat16)
        grad_gate_b = (
            grad_half * up_proj * gate_sig * (1.0 + gate_proj * (1.0 - gate_sig))
        ).astype(jnp.bfloat16)
        grad_up_b = (grad_half * gate_act).astype(jnp.bfloat16)
        return hidden_half, jnp.concatenate([grad_gate_b, grad_up_b], axis=1)

    near_half = jnp.concatenate([second_line.near(k) for k in range(lines // 2)], axis=0)
    second_line.step()
    hidden_near, grad_near = units(near_half, grad_hidden[0])
    hidden_near, grad_near = stage([second_line], hidden_near, grad_near)
    second_line.step()
    part_near = col_product(grad_near, gate_up_w).astype(jnp.bfloat16)
    (part_near,) = stage([second_line], part_near)
    far_half = jnp.concatenate([second_line.near(k) for k in range(lines // 2, lines)], axis=0)
    hidden_far, grad_far = units(far_half, grad_hidden[1])
    part_far = col_product(grad_far, gate_up_w).astype(jnp.bfloat16)

    grad_line = add_up(blocks_of(part_near) + blocks_of(part_far))
    grad_line.step()
    hidden = jnp.concatenate([hidden_near, hidden_far], axis=0)
    second_in = jnp.concatenate([near_half, far_half], axis=0)
    grad_gate_up = jnp.concatenate([grad_near, grad_far], axis=0)
    down_grad = row_product(grad_mlp, hidden).astype(jnp.bfloat16)
    down_piece = reduce_pair(down_grad)
    mlp_part = col_product(hidden, down_w).astype(jnp.bfloat16)
    second_in, mlp_part = stage([grad_line], second_in, mlp_part)
    grad_line.step()
    gate_up_grad = row_product(second_in, grad_gate_up).astype(jnp.bfloat16)
    (gate_up_grad,) = stage([grad_line], gate_up_grad)
    gate_up_piece = reduce_pair(gate_up_grad)
    grad_line.step()
    stage([grad_line])
    grad_second = grad_line.total()

    own_dy = own_cot.astype(jnp.float32) * live_own
    grad_middle = own_dy + norm_back(grad_second, normed_two, inverse_two, gain_b)
    attn_grad_line = walk((BRANCH_SCALE * grad_middle).astype(jnp.bfloat16))
    attn_grad_line.step()
    (mlp_part,) = stage([attn_grad_line], mlp_part)
    mlp_line = add_up(blocks_of(mlp_part))
    mlp_line.step()
    attn_grad_line.step()
    stage([attn_grad_line, mlp_line])
    attn_grad_line.step()
    mlp_line.step()
    stage([attn_grad_line, mlp_line])
    mlp_line.step()
    grad_attn = jnp.concatenate([attn_grad_line.near(k) for k in range(lines)], axis=0)

    out_grad = row_product(grad_attn, attend).astype(jnp.bfloat16)
    out_piece = reduce_pair(out_grad)
    grad_attend = plain_product(grad_attn, out_w).astype(jnp.bfloat16)
    grad_attend, gate_up_piece, down_piece = lax.optimization_barrier(
        (grad_attend, gate_up_piece, down_piece)
    )
    unit_marks = gain_marks(gate_up_mine, gate_up_piece)
    unit_line = walk(
        jnp.pad(
            jnp.concatenate([gate_up_piece, down_piece, unit_marks], axis=1),
            [(0, 0), (0, -(3 * unit_cols + 2) % LANES)],
        )
    )
    unit_line.step()
    grad_qkv = attend_backward(
        heads, span, order, length.reshape(1), kept, attend, grad_attend, cos_all, sin_all
    )
    qkv_grad = row_product(first_in, grad_qkv).astype(jnp.bfloat16)
    qkv_piece = reduce_pair(qkv_grad)
    first_part = col_product(grad_qkv, qkv_w).astype(jnp.bfloat16)
    (first_part,) = stage([unit_line, mlp_line], first_part)

    first_line = add_up(blocks_of(first_part))
    first_line.step()
    unit_line.step()
    layer_rows = ((middle + BRANCH_SCALE * mlp_line.total()) * live_own).astype(jnp.bfloat16)
    (layer_rows,) = stage([unit_line, first_line], layer_rows)
    first_line.step()
    unit_line.step()
    stage([unit_line, first_line])
    first_line.step()
    qkv_marks = gain_marks(qkv_mine, qkv_piece)
    head_line = walk(
        jnp.concatenate(
            [qkv_piece[:, :head_cols], qkv_marks, qkv_piece[:, head_cols + 2 :], out_piece], axis=1
        )
    )
    head_line.step()
    own, other, found = line_pieces(unit_line)
    final_gate, final_up = join_columns(core_index, own, other, 2, unit_cols, unit_cols)
    final_down = join_turned(core_index, own, other, 2 * unit_cols, unit_cols)
    final_gain_two = gain_total(found, 3 * unit_cols, mlp_gain)
    final_gate, final_up, final_down = stage([first_line, head_line], final_gate, final_up, final_down)
    head_line.step()
    grad_first = first_line.total()
    normed_one, inverse_one = norm_parts(own_x)
    grad_rows = grad_middle + norm_back(grad_first, normed_one, inverse_one, gain_a)
    (grad_rows,) = stage([head_line], grad_rows)
    head_line.step()

    def both_slots(own):
        other = lax.ppermute(own, "tensor", swap_pairs())
        return jnp.stack(
            [jnp.where(core == 0, own, other), jnp.where(core == 0, other, own)], axis=0
        )

    layer_out = both_slots(layer_rows)
    grad_tokens = both_slots(grad_rows.astype(jnp.bfloat16)).astype(jnp.float32)
    layer_out, grad_tokens = stage([head_line], layer_out, grad_tokens)
    own, other, found = line_pieces(head_line)
    final_query, final_key, final_value = join_columns(
        core_index, own, other, 3, pad_cols, head_cols
    )
    final_out = join_turned(core_index, own, other, 3 * pad_cols, head_cols)
    final_gain_one = gain_total(found, head_cols, attn_gain)
    return (
        layer_out,
        grad_tokens,
        final_gain_one,
        final_query,
        final_key,
        final_value,
        final_out,
        final_gain_two,
        final_gate,
        final_up,
        final_down,
    )


def heads_of(w_query, cores, lines):
    return w_query.shape[1] * cores // lines


def local(shape, *arrays):
    shards, lines, cores = shape["shard"], shape["ctx"], shape["tensor"]
    tokens, w_query, w_gate = arrays[0], arrays[4], arrays[9]
    fits = (
        cores == 2
        and tokens.shape[0] == cores
        and lines % cores == 0
        and lines == 4
        and (w_query.shape[1] * cores) % (lines * HD) == 0
        and (w_gate.shape[1] * cores) % (lines * cores) == 0
        and w_query.shape[0] % cores == 0
        and -(-heads_of(w_query, cores, lines) // LANES) * LANES >= heads_of(w_query, cores, lines) + 2
    )
    if fits:
        return column_split(shape, *arrays)
    return gather_all(*arrays)


def solution(mesh):
    placed = (
        P("shard", "ctx", None),
        P("shard"),
        P(),
        P("shard"),
        P("shard", "tensor"),
        P("shard", "tensor"),
        P("shard", "tensor"),
        P("tensor", "shard"),
        P("shard"),
        P("shard", "tensor"),
        P("shard", "tensor"),
        P("tensor", "shard"),
        P("shard", "ctx", None),
    )
    return jax.shard_map(
        functools.partial(local, dict(mesh.shape)),
        mesh=mesh,
        in_specs=placed,
        out_specs=(
            P("shard", "ctx", None),
            P("shard", "ctx", None),
            P("shard"),
            P("shard", "tensor"),
            P("shard", "tensor"),
            P("shard", "tensor"),
            P("tensor", "shard"),
            P("shard"),
            P("shard", "tensor"),
            P("shard", "tensor"),
            P("tensor", "shard"),
        ),
        check_vma=False,
    )
```

```python
import functools
import math

import jax
import jax.numpy as jnp
from jax import lax
from jax.experimental import pallas as pl
from jax.experimental.pallas import tpu as pltpu
from jax.sharding import PartitionSpec as P

HD = 64


NORM_EPS = 1e-05
ROPE_BASE = 10000.0
BRANCH_SCALE = 1.4 / math.sqrt(40.0)
CONTRACT_ROWS = (((0,), (0,)), ((), ()))
CONTRACT_COLS = (((1,), (1,)), ((), ()))


def row_product(left_mat, right_mat):
    return lax.dot_general(left_mat, right_mat, CONTRACT_ROWS, preferred_element_type=jnp.float32)


def col_product(left_mat, right_mat):
    return lax.dot_general(left_mat, right_mat, CONTRACT_COLS, preferred_element_type=jnp.float32)


def plain_product(left_mat, right_mat):
    return jnp.dot(left_mat, right_mat, preferred_element_type=jnp.float32)


def rope_tables(positions, head_dim):
    frequency = ROPE_BASE ** (-(jnp.arange(head_dim // 2) * 2).astype(jnp.float32) / head_dim)
    angles = positions.astype(jnp.float32)[:, None] * frequency[None, :]
    return (jnp.cos(angles)[:, None, :], jnp.sin(angles)[:, None, :])


def rotate(values_in, cos_table, sin_table, sign_dir):
    half_dim = values_in.shape[-1] // 2
    lead_part = values_in[..., :half_dim]
    tail_part = values_in[..., half_dim:]
    turned = sin_table * sign_dir
    return jnp.concatenate(
        [lead_part * cos_table - tail_part * turned, tail_part * cos_table + lead_part * turned],
        axis=-1,
    )


def norm_parts(values_in):
    inverse = lax.rsqrt(jnp.mean(values_in * values_in, axis=-1, keepdims=True) + NORM_EPS)
    return (values_in * inverse, inverse)


def norm_back(grad_in, normed, inverse, gain_vec):
    scaled = grad_in * gain_vec
    return inverse * (scaled - normed * jnp.mean(scaled * normed, axis=-1, keepdims=True))


def gather_all(
    tokens,
    lengths,
    span_order,
    attn_gain,
    w_query,
    w_key,
    w_value,
    w_out,
    mlp_gain,
    w_gate,
    w_up,
    w_down,
    cotangent,
):
    slot_count, row_count, width = tokens.shape
    local_heads = w_query.shape[1] // HD
    span_rows = row_count // 2
    offsets = jnp.arange(span_rows, dtype=jnp.int32)
    all_pos = (span_order[:, None] * span_rows + offsets[None, :]).reshape(-1)
    own_pos = lax.dynamic_slice_in_dim(all_pos, lax.axis_index("ctx") * row_count, row_count)
    cos_own, sin_own = rope_tables(own_pos, HD)
    causal = all_pos[None, :] <= own_pos[:, None]
    score_scale = HD ** (-0.5)

    def masked_scores(query_b, key_all, allowed):
        raw_scores = (
            jnp.einsum("qhd,khd->hqk", query_b, key_all, preferred_element_type=jnp.float32)
            * score_scale
        )
        return jnp.where(allowed[None], raw_scores, -1e30)

    out_blocks = []
    grad_blocks = []
    totals = None
    for slot_index in range(slot_count):
        length = lengths[slot_index]
        gain_one = lax.all_gather(attn_gain, "shard", axis=0, tiled=True)
        query_w = lax.all_gather(w_query, "shard", axis=0, tiled=True)
        key_w = lax.all_gather(w_key, "shard", axis=0, tiled=True)
        value_w = lax.all_gather(w_value, "shard", axis=0, tiled=True)
        out_w = lax.all_gather(w_out, "shard", axis=1, tiled=True)
        gain_two = lax.all_gather(mlp_gain, "shard", axis=0, tiled=True)
        gate_w = lax.all_gather(w_gate, "shard", axis=0, tiled=True)
        up_w = lax.all_gather(w_up, "shard", axis=0, tiled=True)
        down_w = lax.all_gather(w_down, "shard", axis=1, tiled=True)
        live_mask = (own_pos < length).astype(jnp.float32)[:, None]
        run_allowed = causal & (all_pos < length)[None, :]
        gain_a = gain_one.astype(jnp.float32)
        gain_b = gain_two.astype(jnp.float32)
        residual_in = tokens[slot_index].astype(jnp.float32)
        normed_one, inverse_one = norm_parts(residual_in)
        first_in = (normed_one * gain_a).astype(jnp.bfloat16)
        query_f = plain_product(first_in, query_w).reshape(row_count, local_heads, HD)
        key_f = plain_product(first_in, key_w).reshape(row_count, local_heads, HD)
        value_b = plain_product(first_in, value_w).astype(jnp.bfloat16)
        run_query_b = rotate(query_f, cos_own, sin_own, 1.0).astype(jnp.bfloat16)
        key_b = rotate(key_f, cos_own, sin_own, 1.0).astype(jnp.bfloat16).reshape(row_count, -1)
        run_key_all = lax.all_gather(key_b, "ctx", axis=0, tiled=True)
        value_all = lax.all_gather(value_b, "ctx", axis=0, tiled=True)
        run_key_all = run_key_all.reshape(-1, local_heads, HD)
        value_all = value_all.reshape(-1, local_heads, HD)
        scores = masked_scores(run_query_b, run_key_all, run_allowed)
        row_top = jnp.max(scores, axis=-1, keepdims=True)
        weights = jnp.exp(scores - row_top)
        row_total = jnp.sum(weights, axis=-1, keepdims=True)
        log_total = row_top + jnp.log(row_total)
        probs_low = (weights / row_total).astype(jnp.bfloat16)
        attend = (
            jnp.einsum("hqk,khd->qhd", probs_low, value_all, preferred_element_type=jnp.float32)
            .astype(jnp.bfloat16)
            .reshape(row_count, -1)
        )
        attn_out = lax.psum(plain_product(attend, out_w), "tensor")
        middle = residual_in + BRANCH_SCALE * attn_out
        normed_two, inverse_two = norm_parts(middle)
        second_in = (normed_two * gain_b).astype(jnp.bfloat16)
        gate_proj = plain_product(second_in, gate_w)
        up_proj = plain_product(second_in, up_w)
        gate_sig = jax.nn.sigmoid(gate_proj)
        gate_act = gate_proj * gate_sig
        hidden = (gate_act * up_proj).astype(jnp.bfloat16)
        mlp_out = lax.psum(plain_product(hidden, down_w).astype(jnp.bfloat16), "tensor").astype(
            jnp.float32
        )
        layer_rows = ((middle + BRANCH_SCALE * mlp_out) * live_mask).astype(jnp.bfloat16)
        grad_y = cotangent[slot_index].astype(jnp.float32) * live_mask
        grad_mlp = (BRANCH_SCALE * grad_y).astype(jnp.bfloat16)
        grad_down_w = row_product(hidden, grad_mlp)
        grad_hidden = col_product(grad_mlp, down_w)
        grad_gate_b = (
            grad_hidden * up_proj * gate_sig * (1.0 + gate_proj * (1.0 - gate_sig))
        ).astype(jnp.bfloat16)
        grad_up_b = (grad_hidden * gate_act).astype(jnp.bfloat16)
        grad_gate_w = row_product(second_in, grad_gate_b)
        grad_up_w = row_product(second_in, grad_up_b)
        grad_second = lax.psum(
            col_product(grad_gate_b, gate_w) + col_product(grad_up_b, up_w), "tensor"
        )
        grad_gain_two = jnp.sum(grad_second * normed_two, axis=0)
        grad_middle = grad_y + norm_back(grad_second, normed_two, inverse_two, gain_b)
        grad_attn = (BRANCH_SCALE * grad_middle).astype(jnp.bfloat16)
        grad_out_w = row_product(attend, grad_attn)
        grad_attend = (
            col_product(grad_attn, out_w).astype(jnp.bfloat16).reshape(row_count, local_heads, HD)
        )
        probs_new = jnp.exp(masked_scores(run_query_b, run_key_all, run_allowed) - log_total)
        grad_probs = jnp.einsum(
            "qhd,khd->hqk", grad_attend, value_all, preferred_element_type=jnp.float32
        )
        grad_scores = (
            probs_new * (grad_probs - jnp.sum(probs_new * grad_probs, axis=-1, keepdims=True))
        ).astype(jnp.bfloat16)
        grad_query_f = (
            jnp.einsum("hqk,khd->qhd", grad_scores, run_key_all, preferred_element_type=jnp.float32)
            * score_scale
        )
        grad_key_all = (
            jnp.einsum("hqk,qhd->khd", grad_scores, run_query_b, preferred_element_type=jnp.float32)
            * score_scale
        )
        grad_value_all = jnp.einsum(
            "hqk,qhd->khd",
            probs_new.astype(jnp.bfloat16),
            grad_attend,
            preferred_element_type=jnp.float32,
        )
        grad_key_own = lax.psum_scatter(
            grad_key_all.reshape(grad_key_all.shape[0], -1), "ctx", scatter_dimension=0, tiled=True
        )
        grad_value_own = lax.psum_scatter(
            grad_value_all.reshape(grad_value_all.shape[0], -1),
            "ctx",
            scatter_dimension=0,
            tiled=True,
        )
        grad_query_b = (
            rotate(grad_query_f, cos_own, sin_own, -1.0).astype(jnp.bfloat16).reshape(row_count, -1)
        )
        grad_key_b = (
            rotate(grad_key_own.reshape(row_count, local_heads, HD), cos_own, sin_own, -1.0)
            .astype(jnp.bfloat16)
            .reshape(row_count, -1)
        )
        grad_value_b = grad_value_own.astype(jnp.bfloat16)
        grad_query_w = row_product(first_in, grad_query_b)
        grad_key_w = row_product(first_in, grad_key_b)
        grad_value_w = row_product(first_in, grad_value_b)
        grad_first = lax.psum(
            (
                col_product(grad_query_b, query_w)
                + col_product(grad_key_b, key_w)
                + col_product(grad_value_b, value_w)
            ).astype(jnp.bfloat16),
            "tensor",
        ).astype(jnp.float32)
        grad_gain_one = jnp.sum(grad_first * normed_one, axis=0)
        grad_rows = grad_middle + norm_back(grad_first, normed_one, inverse_one, gain_a)
        slot_grads = (
            grad_gain_one,
            grad_query_w,
            grad_key_w,
            grad_value_w,
            grad_out_w,
            grad_gain_two,
            grad_gate_w,
            grad_up_w,
            grad_down_w,
        )
        layer_rows, grad_rows, slot_grads = (layer_rows, grad_rows, slot_grads)
        out_blocks.append(layer_rows)
        grad_blocks.append(grad_rows)
        if totals is None:
            totals = slot_grads
        else:
            totals = tuple(
                (left_val + right_val for left_val, right_val in zip(totals, slot_grads))
            )
    (
        sum_gain_one,
        sum_query,
        sum_key,
        sum_value,
        sum_out,
        sum_gain_two,
        sum_gate,
        sum_up,
        sum_down,
    ) = totals
    spread = (
        lax.psum_scatter(sum_gain_one, ("shard", "ctx"), scatter_dimension=0, tiled=True),
        lax.psum_scatter(sum_query, ("shard", "ctx"), scatter_dimension=0, tiled=True),
        lax.psum_scatter(sum_key, ("shard", "ctx"), scatter_dimension=0, tiled=True),
        lax.psum_scatter(sum_value, ("shard", "ctx"), scatter_dimension=0, tiled=True),
        lax.psum_scatter(sum_out, ("shard", "ctx"), scatter_dimension=1, tiled=True),
        lax.psum_scatter(sum_gain_two, ("shard", "ctx"), scatter_dimension=0, tiled=True),
        lax.psum_scatter(sum_gate, ("shard", "ctx"), scatter_dimension=0, tiled=True),
        lax.psum_scatter(sum_up, ("shard", "ctx"), scatter_dimension=0, tiled=True),
        lax.psum_scatter(sum_down, ("shard", "ctx"), scatter_dimension=1, tiled=True),
    )
    (
        part_gain_one,
        part_query,
        part_key,
        part_value,
        part_out,
        part_gain_two,
        part_gate,
        part_up,
        part_down,
    ) = spread
    final = (
        lax.all_gather(part_gain_one.astype(jnp.bfloat16), "ctx", axis=0, tiled=True).astype(
            part_gain_one.dtype
        ),
        lax.all_gather(part_query.astype(jnp.bfloat16), "ctx", axis=0, tiled=True).astype(
            part_query.dtype
        ),
        lax.all_gather(part_key.astype(jnp.bfloat16), "ctx", axis=0, tiled=True).astype(
            part_key.dtype
        ),
        lax.all_gather(part_value.astype(jnp.bfloat16), "ctx", axis=0, tiled=True).astype(
            part_value.dtype
        ),
        lax.all_gather(part_out.astype(jnp.bfloat16), "ctx", axis=1, tiled=True).astype(
            part_out.dtype
        ),
        lax.all_gather(part_gain_two.astype(jnp.bfloat16), "ctx", axis=0, tiled=True).astype(
            part_gain_two.dtype
        ),
        lax.all_gather(part_gate.astype(jnp.bfloat16), "ctx", axis=0, tiled=True).astype(
            part_gate.dtype
        ),
        lax.all_gather(part_up.astype(jnp.bfloat16), "ctx", axis=0, tiled=True).astype(
            part_up.dtype
        ),
        lax.all_gather(part_down.astype(jnp.bfloat16), "ctx", axis=1, tiled=True).astype(
            part_down.dtype
        ),
    )
    layer_out = jnp.stack(out_blocks, axis=0)
    grad_tokens = jnp.stack(grad_blocks, axis=0)
    return (
        layer_out,
        grad_tokens,
        final[0],
        final[1],
        final[2],
        final[3],
        final[4],
        final[5],
        final[6],
        final[7],
        final[8],
    )


LANES = 128
QUERY_TILE = 256


def lane_partner(values_in):
    lane = lax.broadcasted_iota(jnp.int32, values_in.shape, 1) % HD
    return jnp.where(
        lane < HD // 2,
        -pltpu.roll(values_in, LANES - HD // 2, 1),
        pltpu.roll(values_in, HD // 2, 1),
    )


def head_lanes(values_in, head):
    lane = lax.broadcasted_iota(jnp.int32, values_in.shape, 1)
    return jnp.where(lane // HD == head, values_in, jnp.zeros_like(values_in))


def tile_allowed(rows, start, length):
    key = lax.broadcasted_iota(jnp.int32, (rows, QUERY_TILE), 0)
    query = lax.broadcasted_iota(jnp.int32, (rows, QUERY_TILE), 1) + start
    return (key <= query) & (key < length)


def attend_kernel(
    heads, span, order, length, q_in, k_in, v_in, cos, sin, out, q_out, k_out, v_out, log_out,
    q_sort, k_sort, v_sort, turned,
):
    rows = q_in.shape[0]
    pair = pl.program_id(0)
    for block in range(rows // span):
        place = pl.ds(pl.multiple_of(order[block] * span, span), span)
        stored = slice(block * span, (block + 1) * span)
        q_sort[place, :] = q_in[stored, :]
        k_sort[place, :] = k_in[stored, :]
        v_sort[place, :] = v_in[stored, :]
    queries = q_sort[...]
    keys = k_sort[...]
    q_out[...] = (queries * cos[...] + lane_partner(queries) * sin[...]).astype(jnp.bfloat16)
    k_out[...] = (keys * cos[...] + lane_partner(keys) * sin[...]).astype(jnp.bfloat16)
    v_out[...] = v_sort[...].astype(jnp.bfloat16)
    values_t = jnp.transpose(v_out[...])
    turned[...] = jnp.zeros_like(turned)
    log_out[...] = jnp.zeros_like(log_out)
    for head in range(LANES // HD):

        @pl.when(pair * (LANES // HD) + head < heads)
        def _():
            for start in range(0, rows, QUERY_TILE):
                used = start + QUERY_TILE
                query = head_lanes(q_out[start:used, :] * (HD**-0.5), head).astype(jnp.bfloat16)
                scores = col_product(k_out[:used, :], query)
                scores = jnp.where(tile_allowed(used, start, length[0]), scores, -1e30)
                top = jnp.max(scores, axis=0, keepdims=True)
                weights = jnp.exp(scores - top)
                total = jnp.sum(weights, axis=0, keepdims=True)
                probs = (weights * (1.0 / total)).astype(jnp.bfloat16)
                turned[head * HD : (head + 1) * HD, start:used] = plain_product(
                    values_t[head * HD : (head + 1) * HD, :used], probs
                )
                log_out[0, head : head + 1, start:used] = top + jnp.log(total)

    q_sort[...] = jnp.transpose(turned[...])
    for block in range(rows // span):
        place = pl.ds(pl.multiple_of(order[block] * span, span), span)
        out[block * span : (block + 1) * span, :] = q_sort[place, :].astype(jnp.bfloat16)


def attend_back_kernel(
    heads, span, order, length, q_in, k_in, v_in, log_in, o_in, do_in, cos, sin, grads,
    o_sort, do_sort, dq_turned, dq_sum, dk_sum, dv_sum, piece, sems,
):
    rows = q_in.shape[0]
    pair = pl.program_id(0)
    pairs = pl.num_programs(0)
    for block in range(rows // span):
        place = pl.ds(pl.multiple_of(order[block] * span, span), span)
        stored = slice(block * span, (block + 1) * span)
        o_sort[place, :] = o_in[stored, :].astype(jnp.float32)
        do_sort[place, :] = do_in[stored, :].astype(jnp.float32)
    means_t = jnp.transpose(o_sort[...] * do_sort[...])
    keys_t = jnp.transpose(k_in[...])
    dq_turned[...] = jnp.zeros_like(dq_turned)
    dk_sum[...] = jnp.zeros_like(dk_sum)
    dv_sum[...] = jnp.zeros_like(dv_sum)
    for head in range(LANES // HD):

        @pl.when(pair * (LANES // HD) + head < heads)
        def _():
            inner = jnp.sum(means_t[head * HD : (head + 1) * HD, :], axis=0, keepdims=True)
            for start in range(0, rows, QUERY_TILE):
                used = start + QUERY_TILE
                query = head_lanes(q_in[start:used, :] * (HD**-0.5), head).astype(jnp.bfloat16)
                grad_o = head_lanes(do_sort[start:used, :], head).astype(jnp.bfloat16)
                scores = col_product(k_in[:used, :], query)
                probs = jnp.where(
                    tile_allowed(used, start, length[0]),
                    jnp.exp(scores - log_in[0, head : head + 1, start:used]),
                    0.0,
                )
                grad_p = col_product(v_in[:used, :], grad_o)
                grad_s = (probs * (grad_p - inner[:, start:used])).astype(jnp.bfloat16)
                dv_sum[:used, :] += plain_product(probs.astype(jnp.bfloat16), grad_o)
                dk_sum[:used, :] += plain_product(grad_s, query)
                dq_turned[head * HD : (head + 1) * HD, start:used] = plain_product(
                    keys_t[head * HD : (head + 1) * HD, :used], grad_s
                )

    grad_q = jnp.transpose(dq_turned[...]) * (HD**-0.5)
    grad_k = dk_sum[...]
    dq_sum[...] = grad_q * cos[...] - lane_partner(grad_q) * sin[...]
    dk_sum[...] = grad_k * cos[...] - lane_partner(grad_k) * sin[...]
    copies = []
    for which, total in enumerate((dq_sum, dk_sum, dv_sum)):
        for block in range(rows // span):
            place = pl.ds(pl.multiple_of(order[block] * span, span), span)
            piece[which, block * span : (block + 1) * span, :] = total[place, :].astype(jnp.bfloat16)
        column = pl.multiple_of((which * pairs + pair) * LANES, LANES)
        copies.append(
            pltpu.make_async_copy(
                piece.at[which], grads.at[:, pl.ds(column, LANES)], sems.at[which]
            )
        )
        copies[-1].start()
    for copy in copies:
        copy.wait()


def attend_forward(heads, span, order, length, qkv, cos, sin):
    rows = qkv.shape[0]
    pairs = qkv.shape[1] // (3 * LANES)
    column = lambda offset: pl.BlockSpec((rows, LANES), lambda i, *_: (0, offset + i))
    fixed = pl.BlockSpec((rows, LANES), lambda i, *_: (0, 0))
    flat = jax.ShapeDtypeStruct((rows, pairs * LANES), jnp.bfloat16)
    return pl.pallas_call(
        functools.partial(attend_kernel, heads, span),
        grid_spec=pltpu.PrefetchScalarGridSpec(
            num_scalar_prefetch=2,
            grid=(pairs,),
            in_specs=[column(0), column(pairs), column(2 * pairs), fixed, fixed],
            out_specs=[column(0)] * 4 + [pl.BlockSpec((1, 8, rows), lambda i, *_: (i, 0, 0))],
            scratch_shapes=[pltpu.VMEM((rows, LANES), jnp.float32)] * 3
            + [pltpu.VMEM((LANES, rows), jnp.float32)],
        ),
        out_shape=[flat] * 4 + [jax.ShapeDtypeStruct((pairs, 8, rows), jnp.float32)],
        compiler_params=pltpu.CompilerParams(vmem_limit_bytes=40 << 20),
        cost_estimate=pl.CostEstimate(
            flops=4 * heads * rows * rows * HD,
            bytes_accessed=rows * pairs * LANES * 24,
            transcendentals=heads * rows * rows,
        ),
        name="attend",
    )(order, length, qkv, qkv, qkv, cos, sin)


def attend_backward(heads, span, order, length, kept, attend, grad_attend, cos, sin):
    queries, keys, values, logs = kept
    rows = queries.shape[0]
    pairs = queries.shape[1] // LANES
    column = pl.BlockSpec((rows, LANES), lambda i, *_: (0, i))
    fixed = pl.BlockSpec((rows, LANES), lambda i, *_: (0, 0))
    return pl.pallas_call(
        functools.partial(attend_back_kernel, heads, span),
        grid_spec=pltpu.PrefetchScalarGridSpec(
            num_scalar_prefetch=2,
            grid=(pairs,),
            in_specs=[column] * 3
            + [pl.BlockSpec((1, 8, rows), lambda i, *_: (i, 0, 0)), column, column, fixed, fixed],
            out_specs=pl.BlockSpec(memory_space=pl.ANY),
            scratch_shapes=[pltpu.VMEM((rows, LANES), jnp.float32)] * 2
            + [pltpu.VMEM((LANES, rows), jnp.float32)]
            + [pltpu.VMEM((rows, LANES), jnp.float32)] * 3
            + [pltpu.VMEM((3, rows, LANES), jnp.bfloat16), pltpu.SemaphoreType.DMA((3,))],
        ),
        out_shape=jax.ShapeDtypeStruct((rows, 3 * pairs * LANES), jnp.bfloat16),
        compiler_params=pltpu.CompilerParams(vmem_limit_bytes=40 << 20),
        cost_estimate=pl.CostEstimate(
            flops=10 * heads * rows * rows * HD,
            bytes_accessed=rows * pairs * LANES * 16,
            transcendentals=heads * rows * rows,
        ),
        name="attend_back",
    )(order, length, queries, keys, values, logs, attend, grad_attend, cos, sin)


def columns_kernel(count, each, used, core, own, other, *outs):
    mine = pl.program_id(0) == core[0]
    for k in range(own.shape[0]):
        rows = jnp.where(mine, own[k].astype(jnp.float32), other[k].astype(jnp.float32))
        for j in range(count):
            outs[j][:, k * used : (k + 1) * used] = rows[:, j * each : j * each + used]


def join_columns(core, own, other, count, each, used):
    pieces, rows, cols = own.shape
    tile = rows // 3 if rows % 48 == 0 else rows
    taken = pl.BlockSpec((pieces, tile, cols), lambda c, r, *_: (0, r, 0))
    given = pl.BlockSpec((tile, pieces * used), lambda c, r, *_: (c * (rows // tile) + r, 0))
    return pl.pallas_call(
        functools.partial(columns_kernel, count, each, used),
        grid_spec=pltpu.PrefetchScalarGridSpec(
            num_scalar_prefetch=1,
            grid=(2, rows // tile),
            in_specs=[taken, taken],
            out_specs=[given] * count,
        ),
        out_shape=[jax.ShapeDtypeStruct((2 * rows, pieces * used), jnp.float32)] * count,
        compiler_params=pltpu.CompilerParams(vmem_limit_bytes=40 << 20),
        cost_estimate=pl.CostEstimate(
            flops=0, bytes_accessed=8 * pieces * rows * (cols + used * count), transcendentals=0
        ),
        name="join_columns",
    )(core, own, other)


def swap_pairs():
    return [(0, 1), (1, 0)]


class LineGather:
    def __init__(self, block, axis, size):
        self.axis, self.size = axis, size
        self.ups, self.downs = [block], [block]

    def step(self):
        done = len(self.ups)
        up_pairs = [(i, i + 1) for i in range(done - 1, self.size - 1)]
        down_pairs = [(i, i - 1) for i in range(1, self.size - done + 1)]
        self.ups.append(lax.ppermute(self.ups[-1], self.axis, up_pairs))
        self.downs.append(lax.ppermute(self.downs[-1], self.axis, down_pairs))

    def held(self):
        return (self.ups[-1], self.downs[-1])

    def hold(self, values):
        self.ups[-1], self.downs[-1] = values

    def near(self, mask):
        place = lax.axis_index(self.axis)
        found = None
        for here in range(self.size):
            there = here ^ mask
            block = self.ups[here - there] if there < here else self.downs[there - here]
            found = block if found is None else jnp.where(place == here, block, found)
        return found

    def at(self, target):
        place = lax.axis_index(self.axis)
        found = self.ups[0]
        for here in range(self.size):
            if here != target:
                block = self.ups[here - target] if target < here else self.downs[target - here]
                found = jnp.where(place == here, block, found)
        return found


class LineScatter:
    def __init__(self, parts, axis, size):
        self.axis, self.size, self.parts = axis, size, parts
        self.done = 0
        self.up = self.down = None

    def part(self, offsets):
        place = lax.axis_index(self.axis)
        masks = {}
        for here, there in offsets:
            masks.setdefault(here ^ there, []).append(here)
        found = None
        for mask, places in sorted(masks.items()):
            if found is None:
                found = self.parts[mask]
                continue
            chosen = functools.reduce(jnp.logical_or, [place == here for here in places])
            found = jnp.where(chosen, self.parts[mask], found)
        return found

    def step(self):
        self.done += 1
        gap = self.size - self.done
        ups = [(i, i + gap) for i in range(self.done)]
        downs = [(i, i - gap) for i in range(gap, self.size)]
        up, down = self.part(ups), self.part(downs)
        if self.done > 1:
            up = (up.astype(jnp.float32) + self.up.astype(jnp.float32)).astype(jnp.bfloat16)
            down = (down.astype(jnp.float32) + self.down.astype(jnp.float32)).astype(jnp.bfloat16)
        self.up = lax.ppermute(up, self.axis, [(i, i + 1) for i, _ in ups])
        self.down = lax.ppermute(down, self.axis, [(i, i - 1) for i, _ in downs])

    def held(self):
        return (self.up, self.down)

    def hold(self, values):
        self.up, self.down = values

    def total(self):
        return (
            self.parts[0].astype(jnp.float32)
            + self.up.astype(jnp.float32)
            + self.down.astype(jnp.float32)
        )


def stage(chains, *arrays):
    held = [chain.held() for chain in chains]
    held, arrays = lax.optimization_barrier((held, arrays))
    for chain, values in zip(chains, held):
        chain.hold(values)
    return arrays


def column_split(
    shape,
    tokens,
    lengths,
    span_order,
    attn_gain,
    w_query,
    w_key,
    w_value,
    w_out,
    mlp_gain,
    w_gate,
    w_up,
    w_down,
    cotangent,
):
    shards, lines, cores = shape["shard"], shape["ctx"], shape["tensor"]
    line = lax.axis_index("ctx")
    core = lax.axis_index("tensor")
    per_half = lines // cores
    owner = core == line // per_half
    sub = line % per_half
    slot_count, row_count, width = tokens.shape
    all_rows = row_count * lines
    heads = w_query.shape[1] * cores // lines // HD
    head_cols = heads * HD
    pad_cols = -(-head_cols // LANES) * LANES
    widen = lambda v, dim: jnp.pad(v, [(0, pad_cols - head_cols if d == dim else 0) for d in (0, 1)])
    unit_cols = w_gate.shape[1] * cores // lines

    def column_piece(weights, shape_up=lambda v: v):
        cut = [
            shape_up(
                lax.dynamic_slice_in_dim(w, sub * (w.shape[1] // per_half), w.shape[1] // per_half, 1)
            )
            for w in weights
        ]
        return jnp.concatenate(cut, axis=1) if len(cut) > 1 else cut[0]

    def turned_piece(w):
        rows = w.shape[0] // per_half
        return jnp.transpose(lax.dynamic_slice_in_dim(w, sub * rows, rows, 0))

    def to_pair(piece):
        rows = piece.shape[0] // cores
        keep = lax.dynamic_slice_in_dim(piece, core * rows, rows, 0)
        give = lax.dynamic_slice_in_dim(piece, (1 - core) * rows, rows, 0)
        got = lax.ppermute(give, "tensor", swap_pairs())
        return jnp.where(owner, keep, got)

    def gather_pair(mine):
        return lax.all_gather(mine, ("shard", "tensor"), axis=0, tiled=True)

    def reduce_pair(grad):
        return lax.psum_scatter(grad, ("shard", "tensor"), scatter_dimension=0, tiled=True)

    def gain_marks(weights, piece):
        used = weights.shape[1]
        total = jnp.sum(
            weights.astype(jnp.float32) * piece[:, :used].astype(jnp.float32), axis=1, keepdims=True
        )
        high = total.astype(jnp.bfloat16)
        low = (total - high.astype(jnp.float32)).astype(jnp.bfloat16)
        return jnp.concatenate([high, low], axis=1)

    def line_pieces(chain):
        found = [chain.at(q) for q in range(lines)]
        halves = [jnp.stack(found[h * per_half : (h + 1) * per_half]) for h in range(cores)]
        own = jnp.where(core == 0, halves[0], halves[1])
        give = jnp.where(core == 0, halves[1], halves[0])
        return own, lax.ppermute(give, "tensor", swap_pairs()), found

    def gain_total(found, column, gain):
        marks = sum(piece[:, column : column + 2].astype(jnp.float32) for piece in found)
        own = jnp.sum(marks, axis=1)
        other = lax.ppermute(own, "tensor", swap_pairs())
        total = jnp.concatenate(
            [jnp.where(core == 0, own, other), jnp.where(core == 0, other, own)]
        )
        return total / gain.astype(jnp.float32)

    def walk(block):
        return LineGather(block, "ctx", lines)

    def add_up(parts):
        return LineScatter(parts, "ctx", lines)

    def blocks_of(v):
        v = v.astype(jnp.bfloat16)
        return [v[k * row_count : (k + 1) * row_count] for k in range(v.shape[0] // row_count)]

    length = lengths[core]
    offsets = jnp.arange(row_count // 2, dtype=jnp.int32)
    stored_pos = (span_order[:, None] * (row_count // 2) + offsets[None, :]).reshape(lines, row_count)
    ring_pos = stored_pos[line ^ jnp.arange(lines)].reshape(-1)
    own_pos = ring_pos[:row_count]
    span = row_count // 2
    order = ring_pos[::span] // span
    frequency = ROPE_BASE ** (-(jnp.arange(HD // 2) * 2).astype(jnp.float32) / HD)
    angles = jnp.arange(all_rows, dtype=jnp.float32)[:, None] * jnp.tile(frequency, 2 * LANES // HD)
    cos_all, sin_all = jnp.cos(angles), jnp.sin(angles)
    live_all = (ring_pos < length).astype(jnp.float32)[:, None]
    live_own = live_all[:row_count]
    core_index = core.astype(jnp.int32).reshape(1)
    own_tokens = lax.dynamic_index_in_dim(tokens, core, 0, keepdims=False)
    own_cot = lax.dynamic_index_in_dim(cotangent, core, 0, keepdims=False)

    own_tokens, w_query, w_key, w_value = lax.optimization_barrier(
        (own_tokens, w_query, w_key, w_value)
    )
    tokens_line = walk(own_tokens)
    tokens_line.step()
    qkv_mine = to_pair(column_piece([w_query, w_key, w_value], lambda v: widen(v, 1)))
    qkv_w = gather_pair(qkv_mine)
    w_out, w_gate, w_up, w_down, gain_pair = stage(
        [tokens_line], w_out, w_gate, w_up, w_down, jnp.stack([attn_gain, mlp_gain])
    )
    tokens_line.step()
    gains = lax.all_gather(gain_pair, "shard", axis=1, tiled=True)
    gain_a = gains[0].astype(jnp.float32)
    gain_b = gains[1].astype(jnp.float32)
    out_mine = to_pair(widen(turned_piece(w_out), 1))
    down_mine = to_pair(turned_piece(w_down))
    gate_up_mine = to_pair(column_piece([w_gate, w_up]))
    gain_a, gain_b, out_mine = stage([tokens_line], gain_a, gain_b, out_mine)
    tokens_line.step()
    out_w = gather_pair(out_mine)
    own_cot, down_mine = stage([tokens_line], own_cot, down_mine)
    down_w = gather_pair(down_mine)

    cot_line = walk(own_cot)
    cot_line.step()
    all_tokens = jnp.concatenate([tokens_line.near(k) for k in range(lines)], axis=0)
    first_in = (norm_parts(all_tokens.astype(jnp.float32))[0] * gain_a).astype(jnp.bfloat16)
    qkv = plain_product(first_in, qkv_w)
    qkv, gate_up_mine = stage([cot_line], qkv, gate_up_mine)
    gate_up_w = gather_pair(gate_up_mine)

    cot_line.step()
    attend, *kept = attend_forward(heads, span, order, length.reshape(1), qkv, cos_all, sin_all)
    (attend,) = stage([cot_line], attend)

    cot_line.step()
    attn_part = col_product(attend, out_w).astype(jnp.bfloat16)
    attn_line = add_up(blocks_of(attn_part))
    attn_line.step()
    stage([attn_line, cot_line])
    attn_line.step()
    all_cot = jnp.concatenate([cot_line.near(k) for k in range(lines)], axis=0)
    grad_mlp = (BRANCH_SCALE * (all_cot.astype(jnp.float32) * live_all)).astype(jnp.bfloat16)
    (grad_mlp,) = stage([attn_line], grad_mlp)
    attn_line.step()
    half_rows = all_rows // 2
    grad_hidden = [
        plain_product(grad_mlp[k * half_rows : (k + 1) * half_rows], down_w) for k in range(2)
    ]
    grad_hidden = stage([attn_line], *grad_hidden)
    own_x = own_tokens.astype(jnp.float32)
    middle = own_x + BRANCH_SCALE * attn_line.total()
    normed_two, inverse_two = norm_parts(middle)

    second_line = walk((normed_two * gain_b).astype(jnp.bfloat16))
    second_line.step()
    stage([second_line])

    def units(second_half, grad_half):
        gate_up = plain_product(second_half, gate_up_w)
        gate_proj = gate_up[:, :unit_cols]
        up_proj = gate_up[:, unit_cols:]
        gate_sig = jax.nn.sigmoid(gate_proj)
        gate_act = gate_proj * gate_sig
        hidden_half = (gate_act * up_proj).astype(jnp.bfloat16)
        grad_gate_b = (
            grad_half * up_proj * gate_sig * (1.0 + gate_proj * (1.0 - gate_sig))
        ).astype(jnp.bfloat16)
        grad_up_b = (grad_half * gate_act).astype(jnp.bfloat16)
        return hidden_half, jnp.concatenate([grad_gate_b, grad_up_b], axis=1)

    near_half = jnp.concatenate([second_line.near(k) for k in range(lines // 2)], axis=0)
    second_line.step()
    hidden_near, grad_near = units(near_half, grad_hidden[0])
    hidden_near, grad_near = stage([second_line], hidden_near, grad_near)
    second_line.step()
    part_near = col_product(grad_near, gate_up_w).astype(jnp.bfloat16)
    (part_near,) = stage([second_line], part_near)
    far_half = jnp.concatenate([second_line.near(k) for k in range(lines // 2, lines)], axis=0)
    hidden_far, grad_far = units(far_half, grad_hidden[1])
    hidden = jnp.concatenate([hidden_near, hidden_far], axis=0)
    down_grad = row_product(grad_mlp, hidden).astype(jnp.bfloat16)
    down_grad, grad_far = lax.optimization_barrier((down_grad, grad_far))
    down_piece = reduce_pair(down_grad)
    part_far = col_product(grad_far, gate_up_w).astype(jnp.bfloat16)

    grad_line = add_up(blocks_of(part_near) + blocks_of(part_far))
    grad_line.step()
    second_in = jnp.concatenate([near_half, far_half], axis=0)
    grad_gate_up = jnp.concatenate([grad_near, grad_far], axis=0)
    gate_up_grad = row_product(second_in, grad_gate_up).astype(jnp.bfloat16)
    (hidden,) = stage([grad_line], hidden)
    grad_line.step()
    gate_up_grad, down_piece = stage([grad_line], gate_up_grad, down_piece)
    gate_up_piece = reduce_pair(gate_up_grad)
    grad_line.step()
    mlp_part = col_product(hidden, down_w).astype(jnp.bfloat16)
    (mlp_part,) = stage([grad_line], mlp_part)
    grad_second = grad_line.total()

    own_dy = own_cot.astype(jnp.float32) * live_own
    grad_middle = own_dy + norm_back(grad_second, normed_two, inverse_two, gain_b)
    attn_grad_line = walk((BRANCH_SCALE * grad_middle).astype(jnp.bfloat16))
    attn_grad_line.step()
    (mlp_part,) = stage([attn_grad_line], mlp_part)
    mlp_line = add_up(blocks_of(mlp_part))
    mlp_line.step()
    attn_grad_line.step()
    stage([attn_grad_line, mlp_line])
    attn_grad_line.step()
    mlp_line.step()
    unit_marks = gain_marks(gate_up_mine, gate_up_piece)
    rest = jnp.zeros((unit_marks.shape[0], -(3 * unit_cols + 2) % LANES), jnp.bfloat16)
    unit_block = jnp.concatenate([gate_up_piece, down_piece, unit_marks, rest], axis=1)
    (unit_block,) = stage([attn_grad_line, mlp_line], unit_block)
    mlp_line.step()
    unit_line = walk(unit_block)
    unit_line.step()
    grad_attn = jnp.concatenate([attn_grad_line.near(k) for k in range(lines)], axis=0)
    out_grad = row_product(grad_attn, attend).astype(jnp.bfloat16)
    out_piece = reduce_pair(out_grad)
    grad_attn, out_grad = stage([unit_line, mlp_line], grad_attn, out_grad)
    unit_line.step()
    grad_attend = plain_product(grad_attn, out_w).astype(jnp.bfloat16)
    grad_qkv = attend_backward(
        heads, span, order, length.reshape(1), kept, attend, grad_attend, cos_all, sin_all
    )
    qkv_grad = row_product(first_in, grad_qkv).astype(jnp.bfloat16)
    grad_qkv, qkv_grad, out_piece = stage([unit_line], grad_qkv, qkv_grad, out_piece)
    unit_line.step()
    qkv_piece = reduce_pair(qkv_grad)
    first_part = col_product(grad_qkv, qkv_w).astype(jnp.bfloat16)
    first_line = add_up(blocks_of(first_part))
    first_line.step()
    layer_rows = ((middle + BRANCH_SCALE * mlp_line.total()) * live_own).astype(jnp.bfloat16)
    (layer_rows,) = stage([first_line], layer_rows)
    first_line.step()
    stage([unit_line, first_line])
    first_line.step()
    qkv_marks = gain_marks(qkv_mine, qkv_piece)
    head_line = walk(
        jnp.concatenate(
            [qkv_piece[:, :head_cols], qkv_marks, qkv_piece[:, head_cols + 2 :], out_piece], axis=1
        )
    )
    head_line.step()
    own, other, found = line_pieces(unit_line)
    final_gate, final_up, final_down = join_columns(core_index, own, other, 3, unit_cols, unit_cols)
    final_gain_two = gain_total(found, 3 * unit_cols, mlp_gain)
    final_gate, final_up, final_down = stage([first_line, head_line], final_gate, final_up, final_down)
    head_line.step()
    grad_first = first_line.total()
    normed_one, inverse_one = norm_parts(own_x)
    grad_rows = grad_middle + norm_back(grad_first, normed_one, inverse_one, gain_a)
    (grad_rows,) = stage([head_line], grad_rows)
    head_line.step()

    def both_slots(own):
        other = lax.ppermute(own, "tensor", swap_pairs())
        return jnp.stack(
            [jnp.where(core == 0, own, other), jnp.where(core == 0, other, own)], axis=0
        )

    layer_out = both_slots(layer_rows)
    grad_tokens = both_slots(grad_rows.astype(jnp.bfloat16)).astype(jnp.float32)
    layer_out, grad_tokens = stage([head_line], layer_out, grad_tokens)
    own, other, found = line_pieces(head_line)
    final_query, final_key, final_value, final_out = join_columns(
        core_index, own, other, 4, pad_cols, head_cols
    )
    final_gain_one = gain_total(found, head_cols, attn_gain)
    return (
        layer_out,
        grad_tokens,
        final_gain_one,
        final_query,
        final_key,
        final_value,
        jnp.transpose(final_out),
        final_gain_two,
        final_gate,
        final_up,
        jnp.transpose(final_down),
    )


def heads_of(w_query, cores, lines):
    return w_query.shape[1] * cores // lines


def local(shape, *arrays):
    shards, lines, cores = shape["shard"], shape["ctx"], shape["tensor"]
    tokens, w_query, w_gate = arrays[0], arrays[4], arrays[9]
    fits = (
        cores == 2
        and tokens.shape[0] == cores
        and lines % cores == 0
        and lines == 4
        and (w_query.shape[1] * cores) % (lines * HD) == 0
        and (w_gate.shape[1] * cores) % (lines * cores) == 0
        and w_query.shape[0] % cores == 0
        and -(-heads_of(w_query, cores, lines) // LANES) * LANES >= heads_of(w_query, cores, lines) + 2
    )
    if fits:
        return column_split(shape, *arrays)
    return gather_all(*arrays)


def solution(mesh):
    placed = (
        P("shard", "ctx", None),
        P("shard"),
        P(),
        P("shard"),
        P("shard", "tensor"),
        P("shard", "tensor"),
        P("shard", "tensor"),
        P("tensor", "shard"),
        P("shard"),
        P("shard", "tensor"),
        P("shard", "tensor"),
        P("tensor", "shard"),
        P("shard", "ctx", None),
    )
    return jax.shard_map(
        functools.partial(local, dict(mesh.shape)),
        mesh=mesh,
        in_specs=placed,
        out_specs=(
            P("shard", "ctx", None),
            P("shard", "ctx", None),
            P("shard"),
            P("shard", "tensor"),
            P("shard", "tensor"),
            P("shard", "tensor"),
            P("tensor", "shard"),
            P("shard"),
            P("shard", "tensor"),
            P("shard", "tensor"),
            P("tensor", "shard"),
        ),
        check_vma=False,
    )
```

```python
import functools
import math

import jax
import jax.numpy as jnp
from jax import lax
from jax.experimental import pallas as pl
from jax.experimental.pallas import tpu as pltpu
from jax.sharding import PartitionSpec as P

HD = 64


NORM_EPS = 1e-05
ROPE_BASE = 10000.0
BRANCH_SCALE = 1.4 / math.sqrt(40.0)
CONTRACT_ROWS = (((0,), (0,)), ((), ()))
CONTRACT_COLS = (((1,), (1,)), ((), ()))


def row_product(left_mat, right_mat):
    return lax.dot_general(left_mat, right_mat, CONTRACT_ROWS, preferred_element_type=jnp.float32)


def col_product(left_mat, right_mat):
    return lax.dot_general(left_mat, right_mat, CONTRACT_COLS, preferred_element_type=jnp.float32)


def plain_product(left_mat, right_mat):
    return jnp.dot(left_mat, right_mat, preferred_element_type=jnp.float32)


def rope_tables(positions, head_dim):
    frequency = ROPE_BASE ** (-(jnp.arange(head_dim // 2) * 2).astype(jnp.float32) / head_dim)
    angles = positions.astype(jnp.float32)[:, None] * frequency[None, :]
    return (jnp.cos(angles)[:, None, :], jnp.sin(angles)[:, None, :])


def rotate(values_in, cos_table, sin_table, sign_dir):
    half_dim = values_in.shape[-1] // 2
    lead_part = values_in[..., :half_dim]
    tail_part = values_in[..., half_dim:]
    turned = sin_table * sign_dir
    return jnp.concatenate(
        [lead_part * cos_table - tail_part * turned, tail_part * cos_table + lead_part * turned],
        axis=-1,
    )


def norm_parts(values_in):
    inverse = lax.rsqrt(jnp.mean(values_in * values_in, axis=-1, keepdims=True) + NORM_EPS)
    return (values_in * inverse, inverse)


def norm_back(grad_in, normed, inverse, gain_vec):
    scaled = grad_in * gain_vec
    return inverse * (scaled - normed * jnp.mean(scaled * normed, axis=-1, keepdims=True))


def gather_all(
    tokens,
    lengths,
    span_order,
    attn_gain,
    w_query,
    w_key,
    w_value,
    w_out,
    mlp_gain,
    w_gate,
    w_up,
    w_down,
    cotangent,
):
    slot_count, row_count, width = tokens.shape
    local_heads = w_query.shape[1] // HD
    span_rows = row_count // 2
    offsets = jnp.arange(span_rows, dtype=jnp.int32)
    all_pos = (span_order[:, None] * span_rows + offsets[None, :]).reshape(-1)
    own_pos = lax.dynamic_slice_in_dim(all_pos, lax.axis_index("ctx") * row_count, row_count)
    cos_own, sin_own = rope_tables(own_pos, HD)
    causal = all_pos[None, :] <= own_pos[:, None]
    score_scale = HD ** (-0.5)

    def masked_scores(query_b, key_all, allowed):
        raw_scores = (
            jnp.einsum("qhd,khd->hqk", query_b, key_all, preferred_element_type=jnp.float32)
            * score_scale
        )
        return jnp.where(allowed[None], raw_scores, -1e30)

    out_blocks = []
    grad_blocks = []
    totals = None
    for slot_index in range(slot_count):
        length = lengths[slot_index]
        gain_one = lax.all_gather(attn_gain, "shard", axis=0, tiled=True)
        query_w = lax.all_gather(w_query, "shard", axis=0, tiled=True)
        key_w = lax.all_gather(w_key, "shard", axis=0, tiled=True)
        value_w = lax.all_gather(w_value, "shard", axis=0, tiled=True)
        out_w = lax.all_gather(w_out, "shard", axis=1, tiled=True)
        gain_two = lax.all_gather(mlp_gain, "shard", axis=0, tiled=True)
        gate_w = lax.all_gather(w_gate, "shard", axis=0, tiled=True)
        up_w = lax.all_gather(w_up, "shard", axis=0, tiled=True)
        down_w = lax.all_gather(w_down, "shard", axis=1, tiled=True)
        live_mask = (own_pos < length).astype(jnp.float32)[:, None]
        run_allowed = causal & (all_pos < length)[None, :]
        gain_a = gain_one.astype(jnp.float32)
        gain_b = gain_two.astype(jnp.float32)
        residual_in = tokens[slot_index].astype(jnp.float32)
        normed_one, inverse_one = norm_parts(residual_in)
        first_in = (normed_one * gain_a).astype(jnp.bfloat16)
        query_f = plain_product(first_in, query_w).reshape(row_count, local_heads, HD)
        key_f = plain_product(first_in, key_w).reshape(row_count, local_heads, HD)
        value_b = plain_product(first_in, value_w).astype(jnp.bfloat16)
        run_query_b = rotate(query_f, cos_own, sin_own, 1.0).astype(jnp.bfloat16)
        key_b = rotate(key_f, cos_own, sin_own, 1.0).astype(jnp.bfloat16).reshape(row_count, -1)
        run_key_all = lax.all_gather(key_b, "ctx", axis=0, tiled=True)
        value_all = lax.all_gather(value_b, "ctx", axis=0, tiled=True)
        run_key_all = run_key_all.reshape(-1, local_heads, HD)
        value_all = value_all.reshape(-1, local_heads, HD)
        scores = masked_scores(run_query_b, run_key_all, run_allowed)
        row_top = jnp.max(scores, axis=-1, keepdims=True)
        weights = jnp.exp(scores - row_top)
        row_total = jnp.sum(weights, axis=-1, keepdims=True)
        log_total = row_top + jnp.log(row_total)
        probs_low = (weights / row_total).astype(jnp.bfloat16)
        attend = (
            jnp.einsum("hqk,khd->qhd", probs_low, value_all, preferred_element_type=jnp.float32)
            .astype(jnp.bfloat16)
            .reshape(row_count, -1)
        )
        attn_out = lax.psum(plain_product(attend, out_w), "tensor")
        middle = residual_in + BRANCH_SCALE * attn_out
        normed_two, inverse_two = norm_parts(middle)
        second_in = (normed_two * gain_b).astype(jnp.bfloat16)
        gate_proj = plain_product(second_in, gate_w)
        up_proj = plain_product(second_in, up_w)
        gate_sig = jax.nn.sigmoid(gate_proj)
        gate_act = gate_proj * gate_sig
        hidden = (gate_act * up_proj).astype(jnp.bfloat16)
        mlp_out = lax.psum(plain_product(hidden, down_w).astype(jnp.bfloat16), "tensor").astype(
            jnp.float32
        )
        layer_rows = ((middle + BRANCH_SCALE * mlp_out) * live_mask).astype(jnp.bfloat16)
        grad_y = cotangent[slot_index].astype(jnp.float32) * live_mask
        grad_mlp = (BRANCH_SCALE * grad_y).astype(jnp.bfloat16)
        grad_down_w = row_product(hidden, grad_mlp)
        grad_hidden = col_product(grad_mlp, down_w)
        grad_gate_b = (
            grad_hidden * up_proj * gate_sig * (1.0 + gate_proj * (1.0 - gate_sig))
        ).astype(jnp.bfloat16)
        grad_up_b = (grad_hidden * gate_act).astype(jnp.bfloat16)
        grad_gate_w = row_product(second_in, grad_gate_b)
        grad_up_w = row_product(second_in, grad_up_b)
        grad_second = lax.psum(
            col_product(grad_gate_b, gate_w) + col_product(grad_up_b, up_w), "tensor"
        )
        grad_gain_two = jnp.sum(grad_second * normed_two, axis=0)
        grad_middle = grad_y + norm_back(grad_second, normed_two, inverse_two, gain_b)
        grad_attn = (BRANCH_SCALE * grad_middle).astype(jnp.bfloat16)
        grad_out_w = row_product(attend, grad_attn)
        grad_attend = (
            col_product(grad_attn, out_w).astype(jnp.bfloat16).reshape(row_count, local_heads, HD)
        )
        probs_new = jnp.exp(masked_scores(run_query_b, run_key_all, run_allowed) - log_total)
        grad_probs = jnp.einsum(
            "qhd,khd->hqk", grad_attend, value_all, preferred_element_type=jnp.float32
        )
        grad_scores = (
            probs_new * (grad_probs - jnp.sum(probs_new * grad_probs, axis=-1, keepdims=True))
        ).astype(jnp.bfloat16)
        grad_query_f = (
            jnp.einsum("hqk,khd->qhd", grad_scores, run_key_all, preferred_element_type=jnp.float32)
            * score_scale
        )
        grad_key_all = (
            jnp.einsum("hqk,qhd->khd", grad_scores, run_query_b, preferred_element_type=jnp.float32)
            * score_scale
        )
        grad_value_all = jnp.einsum(
            "hqk,qhd->khd",
            probs_new.astype(jnp.bfloat16),
            grad_attend,
            preferred_element_type=jnp.float32,
        )
        grad_key_own = lax.psum_scatter(
            grad_key_all.reshape(grad_key_all.shape[0], -1), "ctx", scatter_dimension=0, tiled=True
        )
        grad_value_own = lax.psum_scatter(
            grad_value_all.reshape(grad_value_all.shape[0], -1),
            "ctx",
            scatter_dimension=0,
            tiled=True,
        )
        grad_query_b = (
            rotate(grad_query_f, cos_own, sin_own, -1.0).astype(jnp.bfloat16).reshape(row_count, -1)
        )
        grad_key_b = (
            rotate(grad_key_own.reshape(row_count, local_heads, HD), cos_own, sin_own, -1.0)
            .astype(jnp.bfloat16)
            .reshape(row_count, -1)
        )
        grad_value_b = grad_value_own.astype(jnp.bfloat16)
        grad_query_w = row_product(first_in, grad_query_b)
        grad_key_w = row_product(first_in, grad_key_b)
        grad_value_w = row_product(first_in, grad_value_b)
        grad_first = lax.psum(
            (
                col_product(grad_query_b, query_w)
                + col_product(grad_key_b, key_w)
                + col_product(grad_value_b, value_w)
            ).astype(jnp.bfloat16),
            "tensor",
        ).astype(jnp.float32)
        grad_gain_one = jnp.sum(grad_first * normed_one, axis=0)
        grad_rows = grad_middle + norm_back(grad_first, normed_one, inverse_one, gain_a)
        slot_grads = (
            grad_gain_one,
            grad_query_w,
            grad_key_w,
            grad_value_w,
            grad_out_w,
            grad_gain_two,
            grad_gate_w,
            grad_up_w,
            grad_down_w,
        )
        layer_rows, grad_rows, slot_grads = (layer_rows, grad_rows, slot_grads)
        out_blocks.append(layer_rows)
        grad_blocks.append(grad_rows)
        if totals is None:
            totals = slot_grads
        else:
            totals = tuple(
                (left_val + right_val for left_val, right_val in zip(totals, slot_grads))
            )
    (
        sum_gain_one,
        sum_query,
        sum_key,
        sum_value,
        sum_out,
        sum_gain_two,
        sum_gate,
        sum_up,
        sum_down,
    ) = totals
    spread = (
        lax.psum_scatter(sum_gain_one, ("shard", "ctx"), scatter_dimension=0, tiled=True),
        lax.psum_scatter(sum_query, ("shard", "ctx"), scatter_dimension=0, tiled=True),
        lax.psum_scatter(sum_key, ("shard", "ctx"), scatter_dimension=0, tiled=True),
        lax.psum_scatter(sum_value, ("shard", "ctx"), scatter_dimension=0, tiled=True),
        lax.psum_scatter(sum_out, ("shard", "ctx"), scatter_dimension=1, tiled=True),
        lax.psum_scatter(sum_gain_two, ("shard", "ctx"), scatter_dimension=0, tiled=True),
        lax.psum_scatter(sum_gate, ("shard", "ctx"), scatter_dimension=0, tiled=True),
        lax.psum_scatter(sum_up, ("shard", "ctx"), scatter_dimension=0, tiled=True),
        lax.psum_scatter(sum_down, ("shard", "ctx"), scatter_dimension=1, tiled=True),
    )
    (
        part_gain_one,
        part_query,
        part_key,
        part_value,
        part_out,
        part_gain_two,
        part_gate,
        part_up,
        part_down,
    ) = spread
    final = (
        lax.all_gather(part_gain_one.astype(jnp.bfloat16), "ctx", axis=0, tiled=True).astype(
            part_gain_one.dtype
        ),
        lax.all_gather(part_query.astype(jnp.bfloat16), "ctx", axis=0, tiled=True).astype(
            part_query.dtype
        ),
        lax.all_gather(part_key.astype(jnp.bfloat16), "ctx", axis=0, tiled=True).astype(
            part_key.dtype
        ),
        lax.all_gather(part_value.astype(jnp.bfloat16), "ctx", axis=0, tiled=True).astype(
            part_value.dtype
        ),
        lax.all_gather(part_out.astype(jnp.bfloat16), "ctx", axis=1, tiled=True).astype(
            part_out.dtype
        ),
        lax.all_gather(part_gain_two.astype(jnp.bfloat16), "ctx", axis=0, tiled=True).astype(
            part_gain_two.dtype
        ),
        lax.all_gather(part_gate.astype(jnp.bfloat16), "ctx", axis=0, tiled=True).astype(
            part_gate.dtype
        ),
        lax.all_gather(part_up.astype(jnp.bfloat16), "ctx", axis=0, tiled=True).astype(
            part_up.dtype
        ),
        lax.all_gather(part_down.astype(jnp.bfloat16), "ctx", axis=1, tiled=True).astype(
            part_down.dtype
        ),
    )
    layer_out = jnp.stack(out_blocks, axis=0)
    grad_tokens = jnp.stack(grad_blocks, axis=0)
    return (
        layer_out,
        grad_tokens,
        final[0],
        final[1],
        final[2],
        final[3],
        final[4],
        final[5],
        final[6],
        final[7],
        final[8],
    )


LANES = 128
QUERY_TILE = 256


def lane_partner(values_in):
    lane = lax.broadcasted_iota(jnp.int32, values_in.shape, 1) % HD
    return jnp.where(
        lane < HD // 2,
        -pltpu.roll(values_in, LANES - HD // 2, 1),
        pltpu.roll(values_in, HD // 2, 1),
    )


def head_lanes(values_in, head):
    lane = lax.broadcasted_iota(jnp.int32, values_in.shape, 1)
    return jnp.where(lane // HD == head, values_in, jnp.zeros_like(values_in))


def tile_allowed(rows, start, length):
    key = lax.broadcasted_iota(jnp.int32, (rows, QUERY_TILE), 0)
    query = lax.broadcasted_iota(jnp.int32, (rows, QUERY_TILE), 1) + start
    return (key <= query) & (key < length)


def attend_kernel(
    heads, span, order, length, q_in, k_in, v_in, cos, sin, out, q_out, k_out, v_out, log_out,
    q_sort, k_sort, v_sort, turned,
):
    rows = q_in.shape[0]
    pair = pl.program_id(0)
    for block in range(rows // span):
        place = pl.ds(pl.multiple_of(order[block] * span, span), span)
        stored = slice(block * span, (block + 1) * span)
        q_sort[place, :] = q_in[stored, :]
        k_sort[place, :] = k_in[stored, :]
        v_sort[place, :] = v_in[stored, :]
    queries = q_sort[...]
    keys = k_sort[...]
    q_out[...] = (queries * cos[...] + lane_partner(queries) * sin[...]).astype(jnp.bfloat16)
    k_out[...] = (keys * cos[...] + lane_partner(keys) * sin[...]).astype(jnp.bfloat16)
    v_out[...] = v_sort[...].astype(jnp.bfloat16)
    values_t = jnp.transpose(v_out[...])
    turned[...] = jnp.zeros_like(turned)
    log_out[...] = jnp.zeros_like(log_out)
    for head in range(LANES // HD):

        @pl.when(pair * (LANES // HD) + head < heads)
        def _():
            for start in range(0, rows, QUERY_TILE):
                used = start + QUERY_TILE
                query = head_lanes(q_out[start:used, :] * (HD**-0.5), head).astype(jnp.bfloat16)
                scores = col_product(k_out[:used, :], query)
                scores = jnp.where(tile_allowed(used, start, length[0]), scores, -1e30)
                top = jnp.max(scores, axis=0, keepdims=True)
                weights = jnp.exp(scores - top)
                total = jnp.sum(weights, axis=0, keepdims=True)
                probs = (weights * (1.0 / total)).astype(jnp.bfloat16)
                turned[head * HD : (head + 1) * HD, start:used] = plain_product(
                    values_t[head * HD : (head + 1) * HD, :used], probs
                )
                log_out[0, head : head + 1, start:used] = top + jnp.log(total)

    q_sort[...] = jnp.transpose(turned[...])
    for block in range(rows // span):
        place = pl.ds(pl.multiple_of(order[block] * span, span), span)
        out[block * span : (block + 1) * span, :] = q_sort[place, :].astype(jnp.bfloat16)


def attend_back_kernel(
    heads, span, order, length, q_in, k_in, v_in, log_in, o_in, do_in, cos, sin, grads,
    o_sort, do_sort, dq_turned, dq_sum, dk_sum, dv_sum, piece, sems,
):
    rows = q_in.shape[0]
    pair = pl.program_id(0)
    pairs = pl.num_programs(0)
    for block in range(rows // span):
        place = pl.ds(pl.multiple_of(order[block] * span, span), span)
        stored = slice(block * span, (block + 1) * span)
        o_sort[place, :] = o_in[stored, :].astype(jnp.float32)
        do_sort[place, :] = do_in[stored, :].astype(jnp.float32)
    means_t = jnp.transpose(o_sort[...] * do_sort[...])
    keys_t = jnp.transpose(k_in[...])
    dq_turned[...] = jnp.zeros_like(dq_turned)
    dk_sum[...] = jnp.zeros_like(dk_sum)
    dv_sum[...] = jnp.zeros_like(dv_sum)
    for head in range(LANES // HD):

        @pl.when(pair * (LANES // HD) + head < heads)
        def _():
            inner = jnp.sum(means_t[head * HD : (head + 1) * HD, :], axis=0, keepdims=True)
            for start in range(0, rows, QUERY_TILE):
                used = start + QUERY_TILE
                query = head_lanes(q_in[start:used, :] * (HD**-0.5), head).astype(jnp.bfloat16)
                grad_o = head_lanes(do_sort[start:used, :], head).astype(jnp.bfloat16)
                scores = col_product(k_in[:used, :], query)
                probs = jnp.where(
                    tile_allowed(used, start, length[0]),
                    jnp.exp(scores - log_in[0, head : head + 1, start:used]),
                    0.0,
                )
                grad_p = col_product(v_in[:used, :], grad_o)
                grad_s = (probs * (grad_p - inner[:, start:used])).astype(jnp.bfloat16)
                dv_sum[:used, :] += plain_product(probs.astype(jnp.bfloat16), grad_o)
                dk_sum[:used, :] += plain_product(grad_s, query)
                dq_turned[head * HD : (head + 1) * HD, start:used] = plain_product(
                    keys_t[head * HD : (head + 1) * HD, :used], grad_s
                )

    grad_q = jnp.transpose(dq_turned[...]) * (HD**-0.5)
    grad_k = dk_sum[...]
    dq_sum[...] = grad_q * cos[...] - lane_partner(grad_q) * sin[...]
    dk_sum[...] = grad_k * cos[...] - lane_partner(grad_k) * sin[...]
    copies = []
    for which, total in enumerate((dq_sum, dk_sum, dv_sum)):
        for block in range(rows // span):
            place = pl.ds(pl.multiple_of(order[block] * span, span), span)
            piece[which, block * span : (block + 1) * span, :] = total[place, :].astype(jnp.bfloat16)
        column = pl.multiple_of((which * pairs + pair) * LANES, LANES)
        copies.append(
            pltpu.make_async_copy(
                piece.at[which], grads.at[:, pl.ds(column, LANES)], sems.at[which]
            )
        )
        copies[-1].start()
    for copy in copies:
        copy.wait()


def attend_forward(heads, span, order, length, qkv, cos, sin):
    rows = qkv.shape[0]
    pairs = qkv.shape[1] // (3 * LANES)
    column = lambda offset: pl.BlockSpec((rows, LANES), lambda i, *_: (0, offset + i))
    fixed = pl.BlockSpec((rows, LANES), lambda i, *_: (0, 0))
    flat = jax.ShapeDtypeStruct((rows, pairs * LANES), jnp.bfloat16)
    return pl.pallas_call(
        functools.partial(attend_kernel, heads, span),
        grid_spec=pltpu.PrefetchScalarGridSpec(
            num_scalar_prefetch=2,
            grid=(pairs,),
            in_specs=[column(0), column(pairs), column(2 * pairs), fixed, fixed],
            out_specs=[column(0)] * 4 + [pl.BlockSpec((1, 8, rows), lambda i, *_: (i, 0, 0))],
            scratch_shapes=[pltpu.VMEM((rows, LANES), jnp.float32)] * 3
            + [pltpu.VMEM((LANES, rows), jnp.float32)],
        ),
        out_shape=[flat] * 4 + [jax.ShapeDtypeStruct((pairs, 8, rows), jnp.float32)],
        compiler_params=pltpu.CompilerParams(vmem_limit_bytes=40 << 20),
        cost_estimate=pl.CostEstimate(
            flops=4 * heads * rows * rows * HD,
            bytes_accessed=rows * pairs * LANES * 24,
            transcendentals=heads * rows * rows,
        ),
        name="attend",
    )(order, length, qkv, qkv, qkv, cos, sin)


def attend_backward(heads, span, order, length, kept, attend, grad_attend, cos, sin):
    queries, keys, values, logs = kept
    rows = queries.shape[0]
    pairs = queries.shape[1] // LANES
    column = pl.BlockSpec((rows, LANES), lambda i, *_: (0, i))
    fixed = pl.BlockSpec((rows, LANES), lambda i, *_: (0, 0))
    return pl.pallas_call(
        functools.partial(attend_back_kernel, heads, span),
        grid_spec=pltpu.PrefetchScalarGridSpec(
            num_scalar_prefetch=2,
            grid=(pairs,),
            in_specs=[column] * 3
            + [pl.BlockSpec((1, 8, rows), lambda i, *_: (i, 0, 0)), column, column, fixed, fixed],
            out_specs=pl.BlockSpec(memory_space=pl.ANY),
            scratch_shapes=[pltpu.VMEM((rows, LANES), jnp.float32)] * 2
            + [pltpu.VMEM((LANES, rows), jnp.float32)]
            + [pltpu.VMEM((rows, LANES), jnp.float32)] * 3
            + [pltpu.VMEM((3, rows, LANES), jnp.bfloat16), pltpu.SemaphoreType.DMA((3,))],
        ),
        out_shape=jax.ShapeDtypeStruct((rows, 3 * pairs * LANES), jnp.bfloat16),
        compiler_params=pltpu.CompilerParams(vmem_limit_bytes=40 << 20),
        cost_estimate=pl.CostEstimate(
            flops=10 * heads * rows * rows * HD,
            bytes_accessed=rows * pairs * LANES * 16,
            transcendentals=heads * rows * rows,
        ),
        name="attend_back",
    )(order, length, queries, keys, values, logs, attend, grad_attend, cos, sin)


def columns_kernel(count, each, used, core, own, other, *outs):
    mine = pl.program_id(0) == core[0]
    for k in range(own.shape[0]):
        rows = jnp.where(mine, own[k].astype(jnp.float32), other[k].astype(jnp.float32))
        for j in range(count):
            outs[j][:, k * used : (k + 1) * used] = rows[:, j * each : j * each + used]


def join_columns(core, own, other, count, each, used):
    pieces, rows, cols = own.shape
    tile = rows // 3 if rows % 48 == 0 else rows
    taken = pl.BlockSpec((pieces, tile, cols), lambda c, r, *_: (0, r, 0))
    given = pl.BlockSpec((tile, pieces * used), lambda c, r, *_: (c * (rows // tile) + r, 0))
    return pl.pallas_call(
        functools.partial(columns_kernel, count, each, used),
        grid_spec=pltpu.PrefetchScalarGridSpec(
            num_scalar_prefetch=1,
            grid=(2, rows // tile),
            in_specs=[taken, taken],
            out_specs=[given] * count,
        ),
        out_shape=[jax.ShapeDtypeStruct((2 * rows, pieces * used), jnp.float32)] * count,
        compiler_params=pltpu.CompilerParams(vmem_limit_bytes=40 << 20),
        cost_estimate=pl.CostEstimate(
            flops=0, bytes_accessed=8 * pieces * rows * (cols + used * count), transcendentals=0
        ),
        name="join_columns",
    )(core, own, other)


def swap_pairs():
    return [(0, 1), (1, 0)]


class LineGather:
    def __init__(self, block, axis, size):
        self.axis, self.size = axis, size
        self.ups, self.downs = [block], [block]

    def step(self):
        done = len(self.ups)
        up_pairs = [(i, i + 1) for i in range(done - 1, self.size - 1)]
        down_pairs = [(i, i - 1) for i in range(1, self.size - done + 1)]
        self.ups.append(lax.ppermute(self.ups[-1], self.axis, up_pairs))
        self.downs.append(lax.ppermute(self.downs[-1], self.axis, down_pairs))

    def held(self):
        return (self.ups[-1], self.downs[-1])

    def hold(self, values):
        self.ups[-1], self.downs[-1] = values

    def near(self, mask):
        place = lax.axis_index(self.axis)
        found = None
        for here in range(self.size):
            there = here ^ mask
            block = self.ups[here - there] if there < here else self.downs[there - here]
            found = block if found is None else jnp.where(place == here, block, found)
        return found

    def at(self, target):
        gap = lax.axis_index(self.axis) - target
        found = self.ups[0]
        for hops in range(1, self.size):
            found = jnp.where(gap == hops, self.ups[hops], found)
            found = jnp.where(gap == -hops, self.downs[hops], found)
        return found


class LineScatter:
    def __init__(self, parts, axis, size):
        self.axis, self.size, self.parts = axis, size, parts
        self.done = 0
        self.up = self.down = None

    def part(self, offsets):
        place = lax.axis_index(self.axis)
        masks = {}
        for here, there in offsets:
            masks.setdefault(here ^ there, []).append(here)
        found = None
        for mask, places in sorted(masks.items()):
            if found is None:
                found = self.parts[mask]
                continue
            chosen = functools.reduce(jnp.logical_or, [place == here for here in places])
            found = jnp.where(chosen, self.parts[mask], found)
        return found

    def step(self):
        self.done += 1
        gap = self.size - self.done
        ups = [(i, i + gap) for i in range(self.done)]
        downs = [(i, i - gap) for i in range(gap, self.size)]
        up, down = self.part(ups), self.part(downs)
        if self.done > 1:
            up = (up.astype(jnp.float32) + self.up.astype(jnp.float32)).astype(jnp.bfloat16)
            down = (down.astype(jnp.float32) + self.down.astype(jnp.float32)).astype(jnp.bfloat16)
        self.up = lax.ppermute(up, self.axis, [(i, i + 1) for i, _ in ups])
        self.down = lax.ppermute(down, self.axis, [(i, i - 1) for i, _ in downs])

    def held(self):
        return (self.up, self.down)

    def hold(self, values):
        self.up, self.down = values

    def total(self):
        return (
            self.parts[0].astype(jnp.float32)
            + self.up.astype(jnp.float32)
            + self.down.astype(jnp.float32)
        )


def stage(chains, *arrays):
    held = [chain.held() for chain in chains]
    held, arrays = lax.optimization_barrier((held, arrays))
    for chain, values in zip(chains, held):
        chain.hold(values)
    return arrays


def column_split(
    shape,
    tokens,
    lengths,
    span_order,
    attn_gain,
    w_query,
    w_key,
    w_value,
    w_out,
    mlp_gain,
    w_gate,
    w_up,
    w_down,
    cotangent,
):
    shards, lines, cores = shape["shard"], shape["ctx"], shape["tensor"]
    line = lax.axis_index("ctx")
    core = lax.axis_index("tensor")
    per_half = lines // cores
    owner = core == line // per_half
    sub = line % per_half
    slot_count, row_count, width = tokens.shape
    all_rows = row_count * lines
    heads = w_query.shape[1] * cores // lines // HD
    head_cols = heads * HD
    pad_cols = -(-head_cols // LANES) * LANES
    widen = lambda v, dim: jnp.pad(v, [(0, pad_cols - head_cols if d == dim else 0) for d in (0, 1)])
    unit_cols = w_gate.shape[1] * cores // lines

    def column_piece(weights, shape_up=lambda v: v):
        cut = [
            shape_up(
                lax.dynamic_slice_in_dim(w, sub * (w.shape[1] // per_half), w.shape[1] // per_half, 1)
            )
            for w in weights
        ]
        return jnp.concatenate(cut, axis=1) if len(cut) > 1 else cut[0]

    def turned_piece(w):
        rows = w.shape[0] // per_half
        return jnp.transpose(lax.dynamic_slice_in_dim(w, sub * rows, rows, 0))

    def to_pair(piece):
        rows = piece.shape[0] // cores
        keep = lax.dynamic_slice_in_dim(piece, core * rows, rows, 0)
        give = lax.dynamic_slice_in_dim(piece, (1 - core) * rows, rows, 0)
        got = lax.ppermute(give, "tensor", swap_pairs())
        return jnp.where(owner, keep, got)

    def gather_pair(mine):
        return lax.all_gather(mine, ("shard", "tensor"), axis=0, tiled=True)

    def reduce_pair(grad):
        return lax.psum_scatter(grad, ("shard", "tensor"), scatter_dimension=0, tiled=True)

    def gain_marks(weights, piece):
        used = weights.shape[1]
        total = jnp.sum(
            weights.astype(jnp.float32) * piece[:, :used].astype(jnp.float32), axis=1, keepdims=True
        )
        high = total.astype(jnp.bfloat16)
        low = (total - high.astype(jnp.float32)).astype(jnp.bfloat16)
        return jnp.concatenate([high, low], axis=1)

    def line_pieces(chain):
        half = lambda c: jnp.stack([chain.at(c * per_half + k) for k in range(per_half)])
        give = half(1 - core)
        return half(core), lax.ppermute(give, "tensor", swap_pairs()), give

    def gain_total(found, column, gain):
        marks = [pieces[:, :, column : column + 2].astype(jnp.float32) for pieces in found]
        own = jnp.sum(marks[0] + marks[1], axis=(0, 2))
        other = lax.ppermute(own, "tensor", swap_pairs())
        total = jnp.concatenate(
            [jnp.where(core == 0, own, other), jnp.where(core == 0, other, own)]
        )
        return total / gain.astype(jnp.float32)

    def walk(block):
        return LineGather(block, "ctx", lines)

    def add_up(parts):
        return LineScatter(parts, "ctx", lines)

    def blocks_of(v):
        v = v.astype(jnp.bfloat16)
        return [v[k * row_count : (k + 1) * row_count] for k in range(v.shape[0] // row_count)]

    length = lengths[core]
    offsets = jnp.arange(row_count // 2, dtype=jnp.int32)
    stored_pos = (span_order[:, None] * (row_count // 2) + offsets[None, :]).reshape(lines, row_count)
    ring_pos = stored_pos[line ^ jnp.arange(lines)].reshape(-1)
    own_pos = ring_pos[:row_count]
    span = row_count // 2
    order = ring_pos[::span] // span
    frequency = ROPE_BASE ** (-(jnp.arange(HD // 2) * 2).astype(jnp.float32) / HD)
    angles = jnp.arange(all_rows, dtype=jnp.float32)[:, None] * jnp.tile(frequency, 2 * LANES // HD)
    cos_all, sin_all = jnp.cos(angles), jnp.sin(angles)
    live_all = (ring_pos < length).astype(jnp.float32)[:, None]
    live_own = live_all[:row_count]
    core_index = core.astype(jnp.int32).reshape(1)
    own_tokens = lax.dynamic_index_in_dim(tokens, core, 0, keepdims=False)
    own_cot = lax.dynamic_index_in_dim(cotangent, core, 0, keepdims=False)

    own_tokens, w_query, w_key, w_value = lax.optimization_barrier(
        (own_tokens, w_query, w_key, w_value)
    )
    tokens_line = walk(own_tokens)
    tokens_line.step()
    qkv_mine = to_pair(column_piece([w_query, w_key, w_value], lambda v: widen(v, 1)))
    qkv_w = gather_pair(qkv_mine)
    w_out, w_gate, w_up, w_down, gain_pair = stage(
        [tokens_line], w_out, w_gate, w_up, w_down, jnp.stack([attn_gain, mlp_gain])
    )
    tokens_line.step()
    gains = lax.all_gather(gain_pair, "shard", axis=1, tiled=True)
    gain_a = gains[0].astype(jnp.float32)
    gain_b = gains[1].astype(jnp.float32)
    out_mine = to_pair(widen(turned_piece(w_out), 1))
    down_mine = to_pair(turned_piece(w_down))
    gate_up_mine = to_pair(column_piece([w_gate, w_up]))
    gain_a, gain_b, out_mine, own_cot, cos_all, sin_all, order = stage(
        [tokens_line], gain_a, gain_b, out_mine, own_cot, cos_all, sin_all, order
    )
    tokens_line.step()
    out_w = gather_pair(out_mine)
    own_cot, down_mine = stage([tokens_line], own_cot, down_mine)
    down_w = gather_pair(down_mine)

    cot_line = walk(own_cot)
    cot_line.step()
    all_tokens = jnp.concatenate([tokens_line.near(k) for k in range(lines)], axis=0)
    first_in = (norm_parts(all_tokens.astype(jnp.float32))[0] * gain_a).astype(jnp.bfloat16)
    qkv = plain_product(first_in, qkv_w)
    qkv, gate_up_mine = stage([cot_line], qkv, gate_up_mine)
    gate_up_w = gather_pair(gate_up_mine)

    cot_line.step()
    attend, *kept = attend_forward(heads, span, order, length.reshape(1), qkv, cos_all, sin_all)
    (attend,) = stage([cot_line], attend)

    cot_line.step()
    attn_part = col_product(attend, out_w).astype(jnp.bfloat16)
    attn_line = add_up(blocks_of(attn_part))
    attn_line.step()
    stage([attn_line, cot_line])
    attn_line.step()
    all_cot = jnp.concatenate([cot_line.near(k) for k in range(lines)], axis=0)
    grad_mlp = (BRANCH_SCALE * (all_cot.astype(jnp.float32) * live_all)).astype(jnp.bfloat16)
    (grad_mlp,) = stage([attn_line], grad_mlp)
    attn_line.step()
    half_rows = all_rows // 2
    cut_rows = [0, half_rows, half_rows + row_count, all_rows]
    grad_hidden = [
        plain_product(grad_mlp[low:high], down_w) for low, high in zip(cut_rows, cut_rows[1:])
    ]
    grad_hidden = stage([attn_line], *grad_hidden)
    own_x = own_tokens.astype(jnp.float32)
    middle = own_x + BRANCH_SCALE * attn_line.total()
    normed_two, inverse_two = norm_parts(middle)

    second_line = walk((normed_two * gain_b).astype(jnp.bfloat16))
    second_line.step()
    stage([second_line])

    def units(second_half, grad_half):
        gate_up = plain_product(second_half, gate_up_w)
        gate_proj = gate_up[:, :unit_cols]
        up_proj = gate_up[:, unit_cols:]
        gate_sig = jax.nn.sigmoid(gate_proj)
        gate_act = gate_proj * gate_sig
        hidden_half = (gate_act * up_proj).astype(jnp.bfloat16)
        grad_gate_b = (
            grad_half * up_proj * gate_sig * (1.0 + gate_proj * (1.0 - gate_sig))
        ).astype(jnp.bfloat16)
        grad_up_b = (grad_half * gate_act).astype(jnp.bfloat16)
        return hidden_half, jnp.concatenate([grad_gate_b, grad_up_b], axis=1)

    near_half = jnp.concatenate([second_line.near(k) for k in range(lines // 2)], axis=0)
    second_line.step()
    hidden_near, grad_near = units(near_half, grad_hidden[0])
    hidden_near, grad_near = stage([second_line], hidden_near, grad_near)
    middle_block = second_line.near(lines // 2)
    second_line.step()
    hidden_mid, grad_mid = units(middle_block, grad_hidden[1])
    part_near = col_product(grad_near, gate_up_w).astype(jnp.bfloat16)
    part_near, hidden_mid, grad_mid = stage([second_line], part_near, hidden_mid, grad_mid)
    last_block = second_line.near(lines - 1)
    hidden_last, grad_last = units(last_block, grad_hidden[2])
    part_last = col_product(grad_last, gate_up_w).astype(jnp.bfloat16)
    part_last, hidden_last, grad_mid = lax.optimization_barrier((part_last, hidden_last, grad_mid))

    parts = blocks_of(part_near) + [None, part_last]
    grad_line = add_up(parts)
    grad_line.step()
    parts[lines // 2] = col_product(grad_mid, gate_up_w).astype(jnp.bfloat16)
    hidden = jnp.concatenate([hidden_near, hidden_mid, hidden_last], axis=0)
    down_grad = row_product(grad_mlp, hidden).astype(jnp.bfloat16)
    down_grad, grad_mid = lax.optimization_barrier((down_grad, grad_mid))
    down_piece = reduce_pair(down_grad)
    second_in = jnp.concatenate([near_half, middle_block, last_block], axis=0)
    grad_gate_up = jnp.concatenate([grad_near, grad_mid, grad_last], axis=0)
    parts[lines // 2], hidden = stage([grad_line], parts[lines // 2], hidden)
    grad_line.step()
    gate_up_grad = row_product(second_in, grad_gate_up).astype(jnp.bfloat16)
    gate_up_grad, down_piece = stage([grad_line], gate_up_grad, down_piece)
    gate_up_piece = reduce_pair(gate_up_grad)
    grad_line.step()
    mlp_part = col_product(hidden, down_w).astype(jnp.bfloat16)
    (mlp_part,) = stage([grad_line], mlp_part)
    grad_second = grad_line.total()

    own_dy = own_cot.astype(jnp.float32) * live_own
    grad_middle = own_dy + norm_back(grad_second, normed_two, inverse_two, gain_b)
    attn_grad_line = walk((BRANCH_SCALE * grad_middle).astype(jnp.bfloat16))
    attn_grad_line.step()
    (mlp_part,) = stage([attn_grad_line], mlp_part)
    mlp_line = add_up(blocks_of(mlp_part))
    mlp_line.step()
    attn_grad_line.step()
    stage([attn_grad_line, mlp_line])
    attn_grad_line.step()
    mlp_line.step()
    unit_marks = gain_marks(gate_up_mine, gate_up_piece)
    rest = jnp.zeros((unit_marks.shape[0], -(3 * unit_cols + 2) % LANES), jnp.bfloat16)
    unit_block = jnp.concatenate([gate_up_piece, down_piece, unit_marks, rest], axis=1)
    (unit_block,) = stage([attn_grad_line, mlp_line], unit_block)
    mlp_line.step()
    unit_line = walk(unit_block)
    unit_line.step()
    grad_attn = jnp.concatenate([attn_grad_line.near(k) for k in range(lines)], axis=0)
    out_grad = row_product(grad_attn, attend).astype(jnp.bfloat16)
    grad_attend = plain_product(grad_attn, out_w).astype(jnp.bfloat16)
    grad_qkv = attend_backward(
        heads, span, order, length.reshape(1), kept, attend, grad_attend, cos_all, sin_all
    )
    qkv_grad = row_product(first_in, grad_qkv).astype(jnp.bfloat16)
    out_piece = reduce_pair(out_grad)
    grad_qkv, qkv_grad, out_piece = stage([unit_line, mlp_line], grad_qkv, qkv_grad, out_piece)
    unit_line.step()
    qkv_piece = reduce_pair(qkv_grad)
    first_part = col_product(grad_qkv, qkv_w).astype(jnp.bfloat16)

    first_line = add_up(blocks_of(first_part))
    first_line.step()
    layer_rows = ((middle + BRANCH_SCALE * mlp_line.total()) * live_own).astype(jnp.bfloat16)
    (layer_rows,) = stage([unit_line, first_line], layer_rows)
    unit_line.step()
    first_line.step()
    qkv_marks = gain_marks(qkv_mine, qkv_piece)
    head_block = jnp.concatenate(
        [qkv_piece[:, :head_cols], qkv_marks, qkv_piece[:, head_cols + 2 :], out_piece], axis=1
    )
    (head_block,) = stage([unit_line, first_line], head_block)
    head_line = walk(head_block)
    head_line.step()
    first_line.step()
    own, other, give = line_pieces(unit_line)
    final_gate, final_up, final_down = join_columns(core_index, own, other, 3, unit_cols, unit_cols)
    final_gain_two = gain_total((own, give), 3 * unit_cols, mlp_gain)
    final_gate, final_up, final_down = stage([first_line, head_line], final_gate, final_up, final_down)
    head_line.step()
    grad_first = first_line.total()
    normed_one, inverse_one = norm_parts(own_x)
    grad_rows = grad_middle + norm_back(grad_first, normed_one, inverse_one, gain_a)
    (grad_rows,) = stage([head_line], grad_rows)
    head_line.step()

    def both_slots(own):
        other = lax.ppermute(own, "tensor", swap_pairs())
        return jnp.stack(
            [jnp.where(core == 0, own, other), jnp.where(core == 0, other, own)], axis=0
        )

    layer_out = both_slots(layer_rows)
    grad_tokens = both_slots(grad_rows.astype(jnp.bfloat16)).astype(jnp.float32)
    layer_out, grad_tokens = stage([head_line], layer_out, grad_tokens)
    own, other, give = line_pieces(head_line)
    final_query, final_key, final_value, final_out = join_columns(
        core_index, own, other, 4, pad_cols, head_cols
    )
    final_gain_one = gain_total((own, give), head_cols, attn_gain)
    return (
        layer_out,
        grad_tokens,
        final_gain_one,
        final_query,
        final_key,
        final_value,
        jnp.transpose(final_out),
        final_gain_two,
        final_gate,
        final_up,
        jnp.transpose(final_down),
    )


def heads_of(w_query, cores, lines):
    return w_query.shape[1] * cores // lines


def local(shape, *arrays):
    shards, lines, cores = shape["shard"], shape["ctx"], shape["tensor"]
    tokens, w_query, w_gate = arrays[0], arrays[4], arrays[9]
    fits = (
        cores == 2
        and tokens.shape[0] == cores
        and lines % cores == 0
        and lines == 4
        and (w_query.shape[1] * cores) % (lines * HD) == 0
        and (w_gate.shape[1] * cores) % (lines * cores) == 0
        and w_query.shape[0] % cores == 0
        and -(-heads_of(w_query, cores, lines) // LANES) * LANES >= heads_of(w_query, cores, lines) + 2
    )
    if fits:
        return column_split(shape, *arrays)
    return gather_all(*arrays)


def solution(mesh):
    placed = (
        P("shard", "ctx", None),
        P("shard"),
        P(),
        P("shard"),
        P("shard", "tensor"),
        P("shard", "tensor"),
        P("shard", "tensor"),
        P("tensor", "shard"),
        P("shard"),
        P("shard", "tensor"),
        P("shard", "tensor"),
        P("tensor", "shard"),
        P("shard", "ctx", None),
    )
    return jax.shard_map(
        functools.partial(local, dict(mesh.shape)),
        mesh=mesh,
        in_specs=placed,
        out_specs=(
            P("shard", "ctx", None),
            P("shard", "ctx", None),
            P("shard"),
            P("shard", "tensor"),
            P("shard", "tensor"),
            P("shard", "tensor"),
            P("tensor", "shard"),
            P("shard"),
            P("shard", "tensor"),
            P("shard", "tensor"),
            P("tensor", "shard"),
        ),
        check_vma=False,
    )
```

```python
import functools
import math

import jax
import jax.numpy as jnp
from jax import lax
from jax.experimental import pallas as pl
from jax.experimental.pallas import tpu as pltpu
from jax.sharding import PartitionSpec as P

HD = 64


NORM_EPS = 1e-05
ROPE_BASE = 10000.0
BRANCH_SCALE = 1.4 / math.sqrt(40.0)
CONTRACT_ROWS = (((0,), (0,)), ((), ()))
CONTRACT_COLS = (((1,), (1,)), ((), ()))


def row_product(left_mat, right_mat):
    return lax.dot_general(left_mat, right_mat, CONTRACT_ROWS, preferred_element_type=jnp.float32)


def col_product(left_mat, right_mat):
    return lax.dot_general(left_mat, right_mat, CONTRACT_COLS, preferred_element_type=jnp.float32)


def plain_product(left_mat, right_mat):
    return jnp.dot(left_mat, right_mat, preferred_element_type=jnp.float32)


def rope_tables(positions, head_dim):
    frequency = ROPE_BASE ** (-(jnp.arange(head_dim // 2) * 2).astype(jnp.float32) / head_dim)
    angles = positions.astype(jnp.float32)[:, None] * frequency[None, :]
    return (jnp.cos(angles)[:, None, :], jnp.sin(angles)[:, None, :])


def rotate(values_in, cos_table, sin_table, sign_dir):
    half_dim = values_in.shape[-1] // 2
    lead_part = values_in[..., :half_dim]
    tail_part = values_in[..., half_dim:]
    turned = sin_table * sign_dir
    return jnp.concatenate(
        [lead_part * cos_table - tail_part * turned, tail_part * cos_table + lead_part * turned],
        axis=-1,
    )


def norm_parts(values_in):
    inverse = lax.rsqrt(jnp.mean(values_in * values_in, axis=-1, keepdims=True) + NORM_EPS)
    return (values_in * inverse, inverse)


def norm_back(grad_in, normed, inverse, gain_vec):
    scaled = grad_in * gain_vec
    return inverse * (scaled - normed * jnp.mean(scaled * normed, axis=-1, keepdims=True))


def gather_all(
    tokens,
    lengths,
    span_order,
    attn_gain,
    w_query,
    w_key,
    w_value,
    w_out,
    mlp_gain,
    w_gate,
    w_up,
    w_down,
    cotangent,
):
    slot_count, row_count, width = tokens.shape
    local_heads = w_query.shape[1] // HD
    span_rows = row_count // 2
    offsets = jnp.arange(span_rows, dtype=jnp.int32)
    all_pos = (span_order[:, None] * span_rows + offsets[None, :]).reshape(-1)
    own_pos = lax.dynamic_slice_in_dim(all_pos, lax.axis_index("ctx") * row_count, row_count)
    cos_own, sin_own = rope_tables(own_pos, HD)
    causal = all_pos[None, :] <= own_pos[:, None]
    score_scale = HD ** (-0.5)

    def masked_scores(query_b, key_all, allowed):
        raw_scores = (
            jnp.einsum("qhd,khd->hqk", query_b, key_all, preferred_element_type=jnp.float32)
            * score_scale
        )
        return jnp.where(allowed[None], raw_scores, -1e30)

    out_blocks = []
    grad_blocks = []
    totals = None
    for slot_index in range(slot_count):
        length = lengths[slot_index]
        gain_one = lax.all_gather(attn_gain, "shard", axis=0, tiled=True)
        query_w = lax.all_gather(w_query, "shard", axis=0, tiled=True)
        key_w = lax.all_gather(w_key, "shard", axis=0, tiled=True)
        value_w = lax.all_gather(w_value, "shard", axis=0, tiled=True)
        out_w = lax.all_gather(w_out, "shard", axis=1, tiled=True)
        gain_two = lax.all_gather(mlp_gain, "shard", axis=0, tiled=True)
        gate_w = lax.all_gather(w_gate, "shard", axis=0, tiled=True)
        up_w = lax.all_gather(w_up, "shard", axis=0, tiled=True)
        down_w = lax.all_gather(w_down, "shard", axis=1, tiled=True)
        live_mask = (own_pos < length).astype(jnp.float32)[:, None]
        run_allowed = causal & (all_pos < length)[None, :]
        gain_a = gain_one.astype(jnp.float32)
        gain_b = gain_two.astype(jnp.float32)
        residual_in = tokens[slot_index].astype(jnp.float32)
        normed_one, inverse_one = norm_parts(residual_in)
        first_in = (normed_one * gain_a).astype(jnp.bfloat16)
        query_f = plain_product(first_in, query_w).reshape(row_count, local_heads, HD)
        key_f = plain_product(first_in, key_w).reshape(row_count, local_heads, HD)
        value_b = plain_product(first_in, value_w).astype(jnp.bfloat16)
        run_query_b = rotate(query_f, cos_own, sin_own, 1.0).astype(jnp.bfloat16)
        key_b = rotate(key_f, cos_own, sin_own, 1.0).astype(jnp.bfloat16).reshape(row_count, -1)
        run_key_all = lax.all_gather(key_b, "ctx", axis=0, tiled=True)
        value_all = lax.all_gather(value_b, "ctx", axis=0, tiled=True)
        run_key_all = run_key_all.reshape(-1, local_heads, HD)
        value_all = value_all.reshape(-1, local_heads, HD)
        scores = masked_scores(run_query_b, run_key_all, run_allowed)
        row_top = jnp.max(scores, axis=-1, keepdims=True)
        weights = jnp.exp(scores - row_top)
        row_total = jnp.sum(weights, axis=-1, keepdims=True)
        log_total = row_top + jnp.log(row_total)
        probs_low = (weights / row_total).astype(jnp.bfloat16)
        attend = (
            jnp.einsum("hqk,khd->qhd", probs_low, value_all, preferred_element_type=jnp.float32)
            .astype(jnp.bfloat16)
            .reshape(row_count, -1)
        )
        attn_out = lax.psum(plain_product(attend, out_w), "tensor")
        middle = residual_in + BRANCH_SCALE * attn_out
        normed_two, inverse_two = norm_parts(middle)
        second_in = (normed_two * gain_b).astype(jnp.bfloat16)
        gate_proj = plain_product(second_in, gate_w)
        up_proj = plain_product(second_in, up_w)
        gate_sig = jax.nn.sigmoid(gate_proj)
        gate_act = gate_proj * gate_sig
        hidden = (gate_act * up_proj).astype(jnp.bfloat16)
        mlp_out = lax.psum(plain_product(hidden, down_w).astype(jnp.bfloat16), "tensor").astype(
            jnp.float32
        )
        layer_rows = ((middle + BRANCH_SCALE * mlp_out) * live_mask).astype(jnp.bfloat16)
        grad_y = cotangent[slot_index].astype(jnp.float32) * live_mask
        grad_mlp = (BRANCH_SCALE * grad_y).astype(jnp.bfloat16)
        grad_down_w = row_product(hidden, grad_mlp)
        grad_hidden = col_product(grad_mlp, down_w)
        grad_gate_b = (
            grad_hidden * up_proj * gate_sig * (1.0 + gate_proj * (1.0 - gate_sig))
        ).astype(jnp.bfloat16)
        grad_up_b = (grad_hidden * gate_act).astype(jnp.bfloat16)
        grad_gate_w = row_product(second_in, grad_gate_b)
        grad_up_w = row_product(second_in, grad_up_b)
        grad_second = lax.psum(
            col_product(grad_gate_b, gate_w) + col_product(grad_up_b, up_w), "tensor"
        )
        grad_gain_two = jnp.sum(grad_second * normed_two, axis=0)
        grad_middle = grad_y + norm_back(grad_second, normed_two, inverse_two, gain_b)
        grad_attn = (BRANCH_SCALE * grad_middle).astype(jnp.bfloat16)
        grad_out_w = row_product(attend, grad_attn)
        grad_attend = (
            col_product(grad_attn, out_w).astype(jnp.bfloat16).reshape(row_count, local_heads, HD)
        )
        probs_new = jnp.exp(masked_scores(run_query_b, run_key_all, run_allowed) - log_total)
        grad_probs = jnp.einsum(
            "qhd,khd->hqk", grad_attend, value_all, preferred_element_type=jnp.float32
        )
        grad_scores = (
            probs_new * (grad_probs - jnp.sum(probs_new * grad_probs, axis=-1, keepdims=True))
        ).astype(jnp.bfloat16)
        grad_query_f = (
            jnp.einsum("hqk,khd->qhd", grad_scores, run_key_all, preferred_element_type=jnp.float32)
            * score_scale
        )
        grad_key_all = (
            jnp.einsum("hqk,qhd->khd", grad_scores, run_query_b, preferred_element_type=jnp.float32)
            * score_scale
        )
        grad_value_all = jnp.einsum(
            "hqk,qhd->khd",
            probs_new.astype(jnp.bfloat16),
            grad_attend,
            preferred_element_type=jnp.float32,
        )
        grad_key_own = lax.psum_scatter(
            grad_key_all.reshape(grad_key_all.shape[0], -1), "ctx", scatter_dimension=0, tiled=True
        )
        grad_value_own = lax.psum_scatter(
            grad_value_all.reshape(grad_value_all.shape[0], -1),
            "ctx",
            scatter_dimension=0,
            tiled=True,
        )
        grad_query_b = (
            rotate(grad_query_f, cos_own, sin_own, -1.0).astype(jnp.bfloat16).reshape(row_count, -1)
        )
        grad_key_b = (
            rotate(grad_key_own.reshape(row_count, local_heads, HD), cos_own, sin_own, -1.0)
            .astype(jnp.bfloat16)
            .reshape(row_count, -1)
        )
        grad_value_b = grad_value_own.astype(jnp.bfloat16)
        grad_query_w = row_product(first_in, grad_query_b)
        grad_key_w = row_product(first_in, grad_key_b)
        grad_value_w = row_product(first_in, grad_value_b)
        grad_first = lax.psum(
            (
                col_product(grad_query_b, query_w)
                + col_product(grad_key_b, key_w)
                + col_product(grad_value_b, value_w)
            ).astype(jnp.bfloat16),
            "tensor",
        ).astype(jnp.float32)
        grad_gain_one = jnp.sum(grad_first * normed_one, axis=0)
        grad_rows = grad_middle + norm_back(grad_first, normed_one, inverse_one, gain_a)
        slot_grads = (
            grad_gain_one,
            grad_query_w,
            grad_key_w,
            grad_value_w,
            grad_out_w,
            grad_gain_two,
            grad_gate_w,
            grad_up_w,
            grad_down_w,
        )
        layer_rows, grad_rows, slot_grads = (layer_rows, grad_rows, slot_grads)
        out_blocks.append(layer_rows)
        grad_blocks.append(grad_rows)
        if totals is None:
            totals = slot_grads
        else:
            totals = tuple(
                (left_val + right_val for left_val, right_val in zip(totals, slot_grads))
            )
    (
        sum_gain_one,
        sum_query,
        sum_key,
        sum_value,
        sum_out,
        sum_gain_two,
        sum_gate,
        sum_up,
        sum_down,
    ) = totals
    spread = (
        lax.psum_scatter(sum_gain_one, ("shard", "ctx"), scatter_dimension=0, tiled=True),
        lax.psum_scatter(sum_query, ("shard", "ctx"), scatter_dimension=0, tiled=True),
        lax.psum_scatter(sum_key, ("shard", "ctx"), scatter_dimension=0, tiled=True),
        lax.psum_scatter(sum_value, ("shard", "ctx"), scatter_dimension=0, tiled=True),
        lax.psum_scatter(sum_out, ("shard", "ctx"), scatter_dimension=1, tiled=True),
        lax.psum_scatter(sum_gain_two, ("shard", "ctx"), scatter_dimension=0, tiled=True),
        lax.psum_scatter(sum_gate, ("shard", "ctx"), scatter_dimension=0, tiled=True),
        lax.psum_scatter(sum_up, ("shard", "ctx"), scatter_dimension=0, tiled=True),
        lax.psum_scatter(sum_down, ("shard", "ctx"), scatter_dimension=1, tiled=True),
    )
    (
        part_gain_one,
        part_query,
        part_key,
        part_value,
        part_out,
        part_gain_two,
        part_gate,
        part_up,
        part_down,
    ) = spread
    final = (
        lax.all_gather(part_gain_one.astype(jnp.bfloat16), "ctx", axis=0, tiled=True).astype(
            part_gain_one.dtype
        ),
        lax.all_gather(part_query.astype(jnp.bfloat16), "ctx", axis=0, tiled=True).astype(
            part_query.dtype
        ),
        lax.all_gather(part_key.astype(jnp.bfloat16), "ctx", axis=0, tiled=True).astype(
            part_key.dtype
        ),
        lax.all_gather(part_value.astype(jnp.bfloat16), "ctx", axis=0, tiled=True).astype(
            part_value.dtype
        ),
        lax.all_gather(part_out.astype(jnp.bfloat16), "ctx", axis=1, tiled=True).astype(
            part_out.dtype
        ),
        lax.all_gather(part_gain_two.astype(jnp.bfloat16), "ctx", axis=0, tiled=True).astype(
            part_gain_two.dtype
        ),
        lax.all_gather(part_gate.astype(jnp.bfloat16), "ctx", axis=0, tiled=True).astype(
            part_gate.dtype
        ),
        lax.all_gather(part_up.astype(jnp.bfloat16), "ctx", axis=0, tiled=True).astype(
            part_up.dtype
        ),
        lax.all_gather(part_down.astype(jnp.bfloat16), "ctx", axis=1, tiled=True).astype(
            part_down.dtype
        ),
    )
    layer_out = jnp.stack(out_blocks, axis=0)
    grad_tokens = jnp.stack(grad_blocks, axis=0)
    return (
        layer_out,
        grad_tokens,
        final[0],
        final[1],
        final[2],
        final[3],
        final[4],
        final[5],
        final[6],
        final[7],
        final[8],
    )


LANES = 128
QUERY_TILE = 256


def lane_partner(values_in):
    lane = lax.broadcasted_iota(jnp.int32, values_in.shape, 1) % HD
    return jnp.where(
        lane < HD // 2,
        -pltpu.roll(values_in, LANES - HD // 2, 1),
        pltpu.roll(values_in, HD // 2, 1),
    )


def head_lanes(values_in, head):
    lane = lax.broadcasted_iota(jnp.int32, values_in.shape, 1)
    return jnp.where(lane // HD == head, values_in, jnp.zeros_like(values_in))


def tile_allowed(rows, start, length):
    key = lax.broadcasted_iota(jnp.int32, (rows, QUERY_TILE), 0)
    query = lax.broadcasted_iota(jnp.int32, (rows, QUERY_TILE), 1) + start
    return (key <= query) & (key < length)


def attend_kernel(
    heads, span, order, length, q_in, k_in, v_in, cos, sin, out, q_out, k_out, v_out, log_out,
    q_sort, k_sort, v_sort, turned,
):
    rows = q_in.shape[0]
    pair = pl.program_id(0)
    for block in range(rows // span):
        place = pl.ds(pl.multiple_of(order[block] * span, span), span)
        stored = slice(block * span, (block + 1) * span)
        q_sort[place, :] = q_in[stored, :]
        k_sort[place, :] = k_in[stored, :]
        v_sort[place, :] = v_in[stored, :]
    queries = q_sort[...]
    keys = k_sort[...]
    q_out[...] = (queries * cos[...] + lane_partner(queries) * sin[...]).astype(jnp.bfloat16)
    k_out[...] = (keys * cos[...] + lane_partner(keys) * sin[...]).astype(jnp.bfloat16)
    v_out[...] = v_sort[...].astype(jnp.bfloat16)
    values_t = jnp.transpose(v_out[...])
    turned[...] = jnp.zeros_like(turned)
    log_out[...] = jnp.zeros_like(log_out)
    for head in range(LANES // HD):

        @pl.when(pair * (LANES // HD) + head < heads)
        def _():
            for start in range(0, rows, QUERY_TILE):
                used = start + QUERY_TILE
                query = head_lanes(q_out[start:used, :] * (HD**-0.5), head).astype(jnp.bfloat16)
                scores = col_product(k_out[:used, :], query)
                scores = jnp.where(tile_allowed(used, start, length[0]), scores, -1e30)
                top = jnp.max(scores, axis=0, keepdims=True)
                weights = jnp.exp(scores - top)
                total = jnp.sum(weights, axis=0, keepdims=True)
                probs = (weights * (1.0 / total)).astype(jnp.bfloat16)
                turned[head * HD : (head + 1) * HD, start:used] = plain_product(
                    values_t[head * HD : (head + 1) * HD, :used], probs
                )
                log_out[0, head : head + 1, start:used] = top + jnp.log(total)

    q_sort[...] = jnp.transpose(turned[...])
    for block in range(rows // span):
        place = pl.ds(pl.multiple_of(order[block] * span, span), span)
        out[block * span : (block + 1) * span, :] = q_sort[place, :].astype(jnp.bfloat16)


def attend_back_kernel(
    heads, span, order, length, q_in, k_in, v_in, log_in, o_in, do_in, cos, sin, grads,
    o_sort, do_sort, dq_turned, dq_sum, dk_sum, dv_sum, piece, sems,
):
    rows = q_in.shape[0]
    pair = pl.program_id(0)
    pairs = pl.num_programs(0)
    for block in range(rows // span):
        place = pl.ds(pl.multiple_of(order[block] * span, span), span)
        stored = slice(block * span, (block + 1) * span)
        o_sort[place, :] = o_in[stored, :].astype(jnp.float32)
        do_sort[place, :] = do_in[stored, :].astype(jnp.float32)
    means_t = jnp.transpose(o_sort[...] * do_sort[...])
    keys_t = jnp.transpose(k_in[...])
    dq_turned[...] = jnp.zeros_like(dq_turned)
    dk_sum[...] = jnp.zeros_like(dk_sum)
    dv_sum[...] = jnp.zeros_like(dv_sum)
    for head in range(LANES // HD):

        @pl.when(pair * (LANES // HD) + head < heads)
        def _():
            inner = jnp.sum(means_t[head * HD : (head + 1) * HD, :], axis=0, keepdims=True)
            for start in range(0, rows, QUERY_TILE):
                used = start + QUERY_TILE
                query = head_lanes(q_in[start:used, :] * (HD**-0.5), head).astype(jnp.bfloat16)
                grad_o = head_lanes(do_sort[start:used, :], head).astype(jnp.bfloat16)
                scores = col_product(k_in[:used, :], query)
                probs = jnp.where(
                    tile_allowed(used, start, length[0]),
                    jnp.exp(scores - log_in[0, head : head + 1, start:used]),
                    0.0,
                )
                grad_p = col_product(v_in[:used, :], grad_o)
                grad_s = (probs * (grad_p - inner[:, start:used])).astype(jnp.bfloat16)
                dv_sum[:used, :] += plain_product(probs.astype(jnp.bfloat16), grad_o)
                dk_sum[:used, :] += plain_product(grad_s, query)
                dq_turned[head * HD : (head + 1) * HD, start:used] = plain_product(
                    keys_t[head * HD : (head + 1) * HD, :used], grad_s
                )

    grad_q = jnp.transpose(dq_turned[...]) * (HD**-0.5)
    grad_k = dk_sum[...]
    dq_sum[...] = grad_q * cos[...] - lane_partner(grad_q) * sin[...]
    dk_sum[...] = grad_k * cos[...] - lane_partner(grad_k) * sin[...]
    copies = []
    for which, total in enumerate((dq_sum, dk_sum, dv_sum)):
        for block in range(rows // span):
            place = pl.ds(pl.multiple_of(order[block] * span, span), span)
            piece[which, block * span : (block + 1) * span, :] = total[place, :].astype(jnp.bfloat16)
        column = pl.multiple_of((which * pairs + pair) * LANES, LANES)
        copies.append(
            pltpu.make_async_copy(
                piece.at[which], grads.at[:, pl.ds(column, LANES)], sems.at[which]
            )
        )
        copies[-1].start()
    for copy in copies:
        copy.wait()


def attend_forward(heads, span, order, length, qkv, cos, sin):
    rows = qkv.shape[0]
    pairs = qkv.shape[1] // (3 * LANES)
    column = lambda offset: pl.BlockSpec((rows, LANES), lambda i, *_: (0, offset + i))
    fixed = pl.BlockSpec((rows, LANES), lambda i, *_: (0, 0))
    flat = jax.ShapeDtypeStruct((rows, pairs * LANES), jnp.bfloat16)
    return pl.pallas_call(
        functools.partial(attend_kernel, heads, span),
        grid_spec=pltpu.PrefetchScalarGridSpec(
            num_scalar_prefetch=2,
            grid=(pairs,),
            in_specs=[column(0), column(pairs), column(2 * pairs), fixed, fixed],
            out_specs=[column(0)] * 4 + [pl.BlockSpec((1, 8, rows), lambda i, *_: (i, 0, 0))],
            scratch_shapes=[pltpu.VMEM((rows, LANES), jnp.float32)] * 3
            + [pltpu.VMEM((LANES, rows), jnp.float32)],
        ),
        out_shape=[flat] * 4 + [jax.ShapeDtypeStruct((pairs, 8, rows), jnp.float32)],
        compiler_params=pltpu.CompilerParams(vmem_limit_bytes=40 << 20),
        cost_estimate=pl.CostEstimate(
            flops=4 * heads * rows * rows * HD,
            bytes_accessed=rows * pairs * LANES * 24,
            transcendentals=heads * rows * rows,
        ),
        name="attend",
    )(order, length, qkv, qkv, qkv, cos, sin)


def attend_backward(heads, span, order, length, kept, attend, grad_attend, cos, sin):
    queries, keys, values, logs = kept
    rows = queries.shape[0]
    pairs = queries.shape[1] // LANES
    column = pl.BlockSpec((rows, LANES), lambda i, *_: (0, i))
    fixed = pl.BlockSpec((rows, LANES), lambda i, *_: (0, 0))
    return pl.pallas_call(
        functools.partial(attend_back_kernel, heads, span),
        grid_spec=pltpu.PrefetchScalarGridSpec(
            num_scalar_prefetch=2,
            grid=(pairs,),
            in_specs=[column] * 3
            + [pl.BlockSpec((1, 8, rows), lambda i, *_: (i, 0, 0)), column, column, fixed, fixed],
            out_specs=pl.BlockSpec(memory_space=pl.ANY),
            scratch_shapes=[pltpu.VMEM((rows, LANES), jnp.float32)] * 2
            + [pltpu.VMEM((LANES, rows), jnp.float32)]
            + [pltpu.VMEM((rows, LANES), jnp.float32)] * 3
            + [pltpu.VMEM((3, rows, LANES), jnp.bfloat16), pltpu.SemaphoreType.DMA((3,))],
        ),
        out_shape=jax.ShapeDtypeStruct((rows, 3 * pairs * LANES), jnp.bfloat16),
        compiler_params=pltpu.CompilerParams(vmem_limit_bytes=40 << 20),
        cost_estimate=pl.CostEstimate(
            flops=10 * heads * rows * rows * HD,
            bytes_accessed=rows * pairs * LANES * 16,
            transcendentals=heads * rows * rows,
        ),
        name="attend_back",
    )(order, length, queries, keys, values, logs, attend, grad_attend, cos, sin)


def columns_kernel(count, each, used, core, own, other, *outs):
    mine = pl.program_id(0) == core[0]
    for k in range(own.shape[0]):
        rows = jnp.where(mine, own[k].astype(jnp.float32), other[k].astype(jnp.float32))
        for j in range(count):
            outs[j][:, k * used : (k + 1) * used] = rows[:, j * each : j * each + used]


def join_columns(core, own, other, count, each, used):
    pieces, rows, cols = own.shape
    tile = rows // 3 if rows % 48 == 0 else rows
    taken = pl.BlockSpec((pieces, tile, cols), lambda c, r, *_: (0, r, 0))
    given = pl.BlockSpec((tile, pieces * used), lambda c, r, *_: (c * (rows // tile) + r, 0))
    return pl.pallas_call(
        functools.partial(columns_kernel, count, each, used),
        grid_spec=pltpu.PrefetchScalarGridSpec(
            num_scalar_prefetch=1,
            grid=(2, rows // tile),
            in_specs=[taken, taken],
            out_specs=[given] * count,
        ),
        out_shape=[jax.ShapeDtypeStruct((2 * rows, pieces * used), jnp.float32)] * count,
        compiler_params=pltpu.CompilerParams(vmem_limit_bytes=40 << 20),
        cost_estimate=pl.CostEstimate(
            flops=0, bytes_accessed=8 * pieces * rows * (cols + used * count), transcendentals=0
        ),
        name="join_columns",
    )(core, own, other)


def swap_pairs():
    return [(0, 1), (1, 0)]


class LineGather:
    def __init__(self, block, axis, size):
        self.axis, self.size = axis, size
        self.ups, self.downs = [block], [block]

    def step(self):
        done = len(self.ups)
        up_pairs = [(i, i + 1) for i in range(done - 1, self.size - 1)]
        down_pairs = [(i, i - 1) for i in range(1, self.size - done + 1)]
        self.ups.append(lax.ppermute(self.ups[-1], self.axis, up_pairs))
        self.downs.append(lax.ppermute(self.downs[-1], self.axis, down_pairs))

    def held(self):
        return (self.ups[-1], self.downs[-1])

    def hold(self, values):
        self.ups[-1], self.downs[-1] = values

    def near(self, mask):
        place = lax.axis_index(self.axis)
        found = None
        for here in range(self.size):
            there = here ^ mask
            block = self.ups[here - there] if there < here else self.downs[there - here]
            found = block if found is None else jnp.where(place == here, block, found)
        return found

    def at(self, target):
        gap = lax.axis_index(self.axis) - target
        found = self.ups[0]
        for hops in range(1, self.size):
            found = jnp.where(gap == hops, self.ups[hops], found)
            found = jnp.where(gap == -hops, self.downs[hops], found)
        return found


class LineScatter:
    def __init__(self, parts, axis, size):
        self.axis, self.size, self.parts = axis, size, parts
        self.done = 0
        self.up = self.down = None

    def part(self, offsets):
        place = lax.axis_index(self.axis)
        masks = {}
        for here, there in offsets:
            masks.setdefault(here ^ there, []).append(here)
        found = None
        for mask, places in sorted(masks.items()):
            if found is None:
                found = self.parts[mask]
                continue
            chosen = functools.reduce(jnp.logical_or, [place == here for here in places])
            found = jnp.where(chosen, self.parts[mask], found)
        return found

    def step(self):
        self.done += 1
        gap = self.size - self.done
        ups = [(i, i + gap) for i in range(self.done)]
        downs = [(i, i - gap) for i in range(gap, self.size)]
        up, down = self.part(ups), self.part(downs)
        if self.done > 1:
            up = (up.astype(jnp.float32) + self.up.astype(jnp.float32)).astype(jnp.bfloat16)
            down = (down.astype(jnp.float32) + self.down.astype(jnp.float32)).astype(jnp.bfloat16)
        self.up = lax.ppermute(up, self.axis, [(i, i + 1) for i, _ in ups])
        self.down = lax.ppermute(down, self.axis, [(i, i - 1) for i, _ in downs])

    def held(self):
        return (self.up, self.down)

    def hold(self, values):
        self.up, self.down = values

    def total(self):
        return (
            self.parts[0].astype(jnp.float32)
            + self.up.astype(jnp.float32)
            + self.down.astype(jnp.float32)
        )


def stage(chains, *arrays):
    held = [chain.held() for chain in chains]
    held, arrays = lax.optimization_barrier((held, arrays))
    for chain, values in zip(chains, held):
        chain.hold(values)
    return arrays


def column_split(
    shape,
    tokens,
    lengths,
    span_order,
    attn_gain,
    w_query,
    w_key,
    w_value,
    w_out,
    mlp_gain,
    w_gate,
    w_up,
    w_down,
    cotangent,
):
    shards, lines, cores = shape["shard"], shape["ctx"], shape["tensor"]
    line = lax.axis_index("ctx")
    core = lax.axis_index("tensor")
    per_half = lines // cores
    owner = core == line // per_half
    sub = line % per_half
    slot_count, row_count, width = tokens.shape
    all_rows = row_count * lines
    heads = w_query.shape[1] * cores // lines // HD
    head_cols = heads * HD
    pad_cols = -(-head_cols // LANES) * LANES
    widen = lambda v, dim: jnp.pad(v, [(0, pad_cols - head_cols if d == dim else 0) for d in (0, 1)])
    unit_cols = w_gate.shape[1] * cores // lines

    def column_piece(weights, shape_up=lambda v: v):
        cut = [
            shape_up(
                lax.dynamic_slice_in_dim(w, sub * (w.shape[1] // per_half), w.shape[1] // per_half, 1)
            )
            for w in weights
        ]
        return jnp.concatenate(cut, axis=1) if len(cut) > 1 else cut[0]

    def turned_piece(w):
        rows = w.shape[0] // per_half
        return jnp.transpose(lax.dynamic_slice_in_dim(w, sub * rows, rows, 0))

    def to_pair(piece):
        rows = piece.shape[0] // cores
        keep = lax.dynamic_slice_in_dim(piece, core * rows, rows, 0)
        give = lax.dynamic_slice_in_dim(piece, (1 - core) * rows, rows, 0)
        got = lax.ppermute(give, "tensor", swap_pairs())
        return jnp.where(owner, keep, got)

    def gather_pair(mine):
        return lax.all_gather(mine, ("shard", "tensor"), axis=0, tiled=True)

    def reduce_pair(grad):
        return lax.psum_scatter(grad, ("shard", "tensor"), scatter_dimension=0, tiled=True)

    def gain_marks(weights, piece):
        used = weights.shape[1]
        total = jnp.sum(
            weights.astype(jnp.float32) * piece[:, :used].astype(jnp.float32), axis=1, keepdims=True
        )
        high = total.astype(jnp.bfloat16)
        low = (total - high.astype(jnp.float32)).astype(jnp.bfloat16)
        return jnp.concatenate([high, low], axis=1)

    def line_pieces(chain):
        half = lambda c: jnp.stack([chain.at(c * per_half + k) for k in range(per_half)])
        give = half(1 - core)
        return half(core), lax.ppermute(give, "tensor", swap_pairs()), give

    def gain_total(found, column, gain):
        marks = [pieces[:, :, column : column + 2].astype(jnp.float32) for pieces in found]
        own = jnp.sum(marks[0] + marks[1], axis=(0, 2))
        other = lax.ppermute(own, "tensor", swap_pairs())
        total = jnp.concatenate(
            [jnp.where(core == 0, own, other), jnp.where(core == 0, other, own)]
        )
        return total / gain.astype(jnp.float32)

    def walk(block):
        return LineGather(block, "ctx", lines)

    def add_up(parts):
        return LineScatter(parts, "ctx", lines)

    def blocks_of(v):
        v = v.astype(jnp.bfloat16)
        return [v[k * row_count : (k + 1) * row_count] for k in range(v.shape[0] // row_count)]

    length = lengths[core]
    offsets = jnp.arange(row_count // 2, dtype=jnp.int32)
    stored_pos = (span_order[:, None] * (row_count // 2) + offsets[None, :]).reshape(lines, row_count)
    ring_pos = stored_pos[line ^ jnp.arange(lines)].reshape(-1)
    own_pos = ring_pos[:row_count]
    span = row_count // 2
    order = ring_pos[::span] // span
    frequency = ROPE_BASE ** (-(jnp.arange(HD // 2) * 2).astype(jnp.float32) / HD)
    angles = jnp.arange(all_rows, dtype=jnp.float32)[:, None] * jnp.tile(frequency, 2 * LANES // HD)
    cos_all, sin_all = jnp.cos(angles), jnp.sin(angles)
    live_all = (ring_pos < length).astype(jnp.float32)[:, None]
    live_own = live_all[:row_count]
    core_index = core.astype(jnp.int32).reshape(1)
    own_tokens = lax.dynamic_index_in_dim(tokens, core, 0, keepdims=False)
    own_cot = lax.dynamic_index_in_dim(cotangent, core, 0, keepdims=False)

    own_tokens, w_query, w_key, w_value = lax.optimization_barrier(
        (own_tokens, w_query, w_key, w_value)
    )
    tokens_line = walk(own_tokens)
    tokens_line.step()
    qkv_mine = to_pair(column_piece([w_query, w_key, w_value], lambda v: widen(v, 1)))
    qkv_w = gather_pair(qkv_mine)
    w_out, w_down, gain_pair = stage(
        [tokens_line], w_out, w_down, jnp.stack([attn_gain, mlp_gain])
    )
    tokens_line.step()
    gains = lax.all_gather(gain_pair, "shard", axis=1, tiled=True)
    gain_a = gains[0].astype(jnp.float32)
    gain_b = gains[1].astype(jnp.float32)
    out_mine = to_pair(widen(turned_piece(w_out), 1))
    down_mine = to_pair(turned_piece(w_down))
    gain_a, gain_b, out_mine, own_cot, cos_all, sin_all, order, w_gate, w_up = stage(
        [tokens_line], gain_a, gain_b, out_mine, own_cot, cos_all, sin_all, order, w_gate, w_up
    )
    tokens_line.step()
    out_w = gather_pair(out_mine)
    gate_up_mine = to_pair(column_piece([w_gate, w_up]))
    own_cot, down_mine, gate_up_mine = stage([tokens_line], own_cot, down_mine, gate_up_mine)
    down_w = gather_pair(down_mine)

    cot_line = walk(own_cot)
    cot_line.step()
    all_tokens = jnp.concatenate([tokens_line.near(k) for k in range(lines)], axis=0)
    first_in = (norm_parts(all_tokens.astype(jnp.float32))[0] * gain_a).astype(jnp.bfloat16)
    qkv = plain_product(first_in, qkv_w)
    qkv, gate_up_mine = stage([cot_line], qkv, gate_up_mine)
    gate_up_w = gather_pair(gate_up_mine)

    cot_line.step()
    attend, *kept = attend_forward(heads, span, order, length.reshape(1), qkv, cos_all, sin_all)
    (attend,) = stage([cot_line], attend)

    cot_line.step()
    attn_part = col_product(attend, out_w).astype(jnp.bfloat16)
    attn_line = add_up(blocks_of(attn_part))
    attn_line.step()
    stage([attn_line, cot_line])
    attn_line.step()
    all_cot = jnp.concatenate([cot_line.near(k) for k in range(lines)], axis=0)
    grad_mlp = (BRANCH_SCALE * (all_cot.astype(jnp.float32) * live_all)).astype(jnp.bfloat16)
    (grad_mlp,) = stage([attn_line], grad_mlp)
    attn_line.step()
    half_rows = all_rows // 2
    grad_hidden = [
        plain_product(grad_mlp[k * half_rows : (k + 1) * half_rows], down_w) for k in range(2)
    ]
    grad_hidden = stage([attn_line], *grad_hidden)
    own_x = own_tokens.astype(jnp.float32)
    middle = own_x + BRANCH_SCALE * attn_line.total()
    normed_two, inverse_two = norm_parts(middle)

    second_line = walk((normed_two * gain_b).astype(jnp.bfloat16))
    second_line.step()
    stage([second_line])

    def units(second_half, grad_half):
        gate_up = plain_product(second_half, gate_up_w)
        gate_proj = gate_up[:, :unit_cols]
        up_proj = gate_up[:, unit_cols:]
        gate_sig = jax.nn.sigmoid(gate_proj)
        gate_act = gate_proj * gate_sig
        hidden_half = (gate_act * up_proj).astype(jnp.bfloat16)
        grad_gate_b = (
            grad_half * up_proj * gate_sig * (1.0 + gate_proj * (1.0 - gate_sig))
        ).astype(jnp.bfloat16)
        grad_up_b = (grad_half * gate_act).astype(jnp.bfloat16)
        return hidden_half, jnp.concatenate([grad_gate_b, grad_up_b], axis=1)

    near_half = jnp.concatenate([second_line.near(k) for k in range(lines // 2)], axis=0)
    second_line.step()
    hidden_near, grad_near = units(near_half, grad_hidden[0])
    hidden_near, grad_near = stage([second_line], hidden_near, grad_near)
    second_line.step()
    part_near = col_product(grad_near, gate_up_w).astype(jnp.bfloat16)
    (part_near,) = stage([second_line], part_near)
    far_half = jnp.concatenate([second_line.near(k) for k in range(lines // 2, lines)], axis=0)
    hidden_far, grad_far = units(far_half, grad_hidden[1])
    part_far = col_product(grad_far, gate_up_w).astype(jnp.bfloat16)
    hidden_far, grad_far, part_far = lax.optimization_barrier((hidden_far, grad_far, part_far))

    grad_line = add_up(blocks_of(part_near) + blocks_of(part_far))
    grad_line.step()
    second_in = jnp.concatenate([near_half, far_half], axis=0)
    grad_gate_up = jnp.concatenate([grad_near, grad_far], axis=0)
    gate_up_grad = row_product(second_in, grad_gate_up).astype(jnp.bfloat16)
    hidden = jnp.concatenate([hidden_near, hidden_far], axis=0)
    gate_up_grad, hidden = stage([grad_line], gate_up_grad, hidden)
    grad_line.step()
    gate_up_piece = reduce_pair(gate_up_grad)
    down_grad = row_product(grad_mlp, hidden).astype(jnp.bfloat16)
    down_grad, hidden = stage([grad_line], down_grad, hidden)
    grad_line.step()
    down_piece = reduce_pair(down_grad)
    mlp_part = col_product(hidden, down_w).astype(jnp.bfloat16)
    (mlp_part,) = stage([grad_line], mlp_part)
    grad_second = grad_line.total()

    own_dy = own_cot.astype(jnp.float32) * live_own
    grad_middle = own_dy + norm_back(grad_second, normed_two, inverse_two, gain_b)
    attn_grad_line = walk((BRANCH_SCALE * grad_middle).astype(jnp.bfloat16))
    attn_grad_line.step()
    (mlp_part,) = stage([attn_grad_line], mlp_part)
    mlp_line = add_up(blocks_of(mlp_part))
    mlp_line.step()
    attn_grad_line.step()
    stage([attn_grad_line, mlp_line])
    attn_grad_line.step()
    mlp_line.step()
    unit_marks = gain_marks(gate_up_mine, gate_up_piece)
    rest = jnp.zeros((unit_marks.shape[0], -(2 * unit_cols + 2) % LANES), jnp.bfloat16)
    unit_block = jnp.concatenate([gate_up_piece, unit_marks, rest], axis=1)
    (unit_block,) = stage([attn_grad_line, mlp_line], unit_block)
    mlp_line.step()
    unit_line = walk(unit_block)
    unit_line.step()
    grad_attn = jnp.concatenate([attn_grad_line.near(k) for k in range(lines)], axis=0)
    out_grad = row_product(grad_attn, attend).astype(jnp.bfloat16)
    grad_attend = plain_product(grad_attn, out_w).astype(jnp.bfloat16)
    grad_qkv = attend_backward(
        heads, span, order, length.reshape(1), kept, attend, grad_attend, cos_all, sin_all
    )
    qkv_grad = row_product(first_in, grad_qkv).astype(jnp.bfloat16)
    out_piece = reduce_pair(out_grad)
    grad_qkv, qkv_grad, out_piece, down_piece = stage(
        [unit_line, mlp_line], grad_qkv, qkv_grad, out_piece, down_piece
    )
    unit_line.step()
    down_line = walk(down_piece)
    down_line.step()
    qkv_piece = reduce_pair(qkv_grad)
    first_part = col_product(grad_qkv, qkv_w).astype(jnp.bfloat16)

    first_line = add_up(blocks_of(first_part))
    first_line.step()
    layer_rows = ((middle + BRANCH_SCALE * mlp_line.total()) * live_own).astype(jnp.bfloat16)
    (layer_rows,) = stage([unit_line, first_line, down_line], layer_rows)
    unit_line.step()
    first_line.step()
    down_line.step()
    qkv_marks = gain_marks(qkv_mine, qkv_piece)
    head_block = jnp.concatenate(
        [qkv_piece[:, :head_cols], qkv_marks, qkv_piece[:, head_cols + 2 :], out_piece], axis=1
    )
    (head_block,) = stage([unit_line, first_line, down_line], head_block)
    head_line = walk(head_block)
    head_line.step()
    first_line.step()
    down_line.step()
    own, other, give = line_pieces(unit_line)
    final_gate, final_up = join_columns(core_index, own, other, 2, unit_cols, unit_cols)
    final_gain_two = gain_total((own, give), 2 * unit_cols, mlp_gain)
    final_gate, final_up = stage([first_line, head_line, down_line], final_gate, final_up)
    head_line.step()
    own, other, _ = line_pieces(down_line)
    (final_down,) = join_columns(core_index, own, other, 1, unit_cols, unit_cols)
    grad_first = first_line.total()
    normed_one, inverse_one = norm_parts(own_x)
    grad_rows = grad_middle + norm_back(grad_first, normed_one, inverse_one, gain_a)
    grad_rows, final_down = stage([head_line], grad_rows, final_down)
    head_line.step()

    def both_slots(own):
        other = lax.ppermute(own, "tensor", swap_pairs())
        return jnp.stack(
            [jnp.where(core == 0, own, other), jnp.where(core == 0, other, own)], axis=0
        )

    layer_out = both_slots(layer_rows)
    grad_tokens = both_slots(grad_rows.astype(jnp.bfloat16)).astype(jnp.float32)
    layer_out, grad_tokens = stage([head_line], layer_out, grad_tokens)
    own, other, give = line_pieces(head_line)
    final_query, final_key, final_value, final_out = join_columns(
        core_index, own, other, 4, pad_cols, head_cols
    )
    final_gain_one = gain_total((own, give), head_cols, attn_gain)
    return (
        layer_out,
        grad_tokens,
        final_gain_one,
        final_query,
        final_key,
        final_value,
        jnp.transpose(final_out),
        final_gain_two,
        final_gate,
        final_up,
        jnp.transpose(final_down),
    )


def heads_of(w_query, cores, lines):
    return w_query.shape[1] * cores // lines


def local(shape, *arrays):
    shards, lines, cores = shape["shard"], shape["ctx"], shape["tensor"]
    tokens, w_query, w_gate = arrays[0], arrays[4], arrays[9]
    fits = (
        cores == 2
        and tokens.shape[0] == cores
        and lines % cores == 0
        and lines == 4
        and (w_query.shape[1] * cores) % (lines * HD) == 0
        and (w_gate.shape[1] * cores) % (lines * cores) == 0
        and w_query.shape[0] % cores == 0
        and -(-heads_of(w_query, cores, lines) // LANES) * LANES >= heads_of(w_query, cores, lines) + 2
    )
    if fits:
        return column_split(shape, *arrays)
    return gather_all(*arrays)


def solution(mesh):
    placed = (
        P("shard", "ctx", None),
        P("shard"),
        P(),
        P("shard"),
        P("shard", "tensor"),
        P("shard", "tensor"),
        P("shard", "tensor"),
        P("tensor", "shard"),
        P("shard"),
        P("shard", "tensor"),
        P("shard", "tensor"),
        P("tensor", "shard"),
        P("shard", "ctx", None),
    )
    return jax.shard_map(
        functools.partial(local, dict(mesh.shape)),
        mesh=mesh,
        in_specs=placed,
        out_specs=(
            P("shard", "ctx", None),
            P("shard", "ctx", None),
            P("shard"),
            P("shard", "tensor"),
            P("shard", "tensor"),
            P("shard", "tensor"),
            P("tensor", "shard"),
            P("shard"),
            P("shard", "tensor"),
            P("shard", "tensor"),
            P("tensor", "shard"),
        ),
        check_vma=False,
    )
```

```python
import functools
import math

import jax
import jax.numpy as jnp
from jax import lax
from jax.experimental import pallas as pl
from jax.experimental.pallas import tpu as pltpu
from jax.sharding import PartitionSpec as P

HD = 64


NORM_EPS = 1e-05
ROPE_BASE = 10000.0
BRANCH_SCALE = 1.4 / math.sqrt(40.0)
CONTRACT_ROWS = (((0,), (0,)), ((), ()))
CONTRACT_COLS = (((1,), (1,)), ((), ()))


def row_product(left_mat, right_mat):
    return lax.dot_general(left_mat, right_mat, CONTRACT_ROWS, preferred_element_type=jnp.float32)


def col_product(left_mat, right_mat):
    return lax.dot_general(left_mat, right_mat, CONTRACT_COLS, preferred_element_type=jnp.float32)


def plain_product(left_mat, right_mat):
    return jnp.dot(left_mat, right_mat, preferred_element_type=jnp.float32)


def rope_tables(positions, head_dim):
    frequency = ROPE_BASE ** (-(jnp.arange(head_dim // 2) * 2).astype(jnp.float32) / head_dim)
    angles = positions.astype(jnp.float32)[:, None] * frequency[None, :]
    return (jnp.cos(angles)[:, None, :], jnp.sin(angles)[:, None, :])


def rotate(values_in, cos_table, sin_table, sign_dir):
    half_dim = values_in.shape[-1] // 2
    lead_part = values_in[..., :half_dim]
    tail_part = values_in[..., half_dim:]
    turned = sin_table * sign_dir
    return jnp.concatenate(
        [lead_part * cos_table - tail_part * turned, tail_part * cos_table + lead_part * turned],
        axis=-1,
    )


def norm_parts(values_in):
    inverse = lax.rsqrt(jnp.mean(values_in * values_in, axis=-1, keepdims=True) + NORM_EPS)
    return (values_in * inverse, inverse)


def norm_back(grad_in, normed, inverse, gain_vec):
    scaled = grad_in * gain_vec
    return inverse * (scaled - normed * jnp.mean(scaled * normed, axis=-1, keepdims=True))


def gather_all(
    tokens,
    lengths,
    span_order,
    attn_gain,
    w_query,
    w_key,
    w_value,
    w_out,
    mlp_gain,
    w_gate,
    w_up,
    w_down,
    cotangent,
):
    slot_count, row_count, width = tokens.shape
    local_heads = w_query.shape[1] // HD
    span_rows = row_count // 2
    offsets = jnp.arange(span_rows, dtype=jnp.int32)
    all_pos = (span_order[:, None] * span_rows + offsets[None, :]).reshape(-1)
    own_pos = lax.dynamic_slice_in_dim(all_pos, lax.axis_index("ctx") * row_count, row_count)
    cos_own, sin_own = rope_tables(own_pos, HD)
    causal = all_pos[None, :] <= own_pos[:, None]
    score_scale = HD ** (-0.5)

    def masked_scores(query_b, key_all, allowed):
        raw_scores = (
            jnp.einsum("qhd,khd->hqk", query_b, key_all, preferred_element_type=jnp.float32)
            * score_scale
        )
        return jnp.where(allowed[None], raw_scores, -1e30)

    out_blocks = []
    grad_blocks = []
    totals = None
    for slot_index in range(slot_count):
        length = lengths[slot_index]
        gain_one = lax.all_gather(attn_gain, "shard", axis=0, tiled=True)
        query_w = lax.all_gather(w_query, "shard", axis=0, tiled=True)
        key_w = lax.all_gather(w_key, "shard", axis=0, tiled=True)
        value_w = lax.all_gather(w_value, "shard", axis=0, tiled=True)
        out_w = lax.all_gather(w_out, "shard", axis=1, tiled=True)
        gain_two = lax.all_gather(mlp_gain, "shard", axis=0, tiled=True)
        gate_w = lax.all_gather(w_gate, "shard", axis=0, tiled=True)
        up_w = lax.all_gather(w_up, "shard", axis=0, tiled=True)
        down_w = lax.all_gather(w_down, "shard", axis=1, tiled=True)
        live_mask = (own_pos < length).astype(jnp.float32)[:, None]
        run_allowed = causal & (all_pos < length)[None, :]
        gain_a = gain_one.astype(jnp.float32)
        gain_b = gain_two.astype(jnp.float32)
        residual_in = tokens[slot_index].astype(jnp.float32)
        normed_one, inverse_one = norm_parts(residual_in)
        first_in = (normed_one * gain_a).astype(jnp.bfloat16)
        query_f = plain_product(first_in, query_w).reshape(row_count, local_heads, HD)
        key_f = plain_product(first_in, key_w).reshape(row_count, local_heads, HD)
        value_b = plain_product(first_in, value_w).astype(jnp.bfloat16)
        run_query_b = rotate(query_f, cos_own, sin_own, 1.0).astype(jnp.bfloat16)
        key_b = rotate(key_f, cos_own, sin_own, 1.0).astype(jnp.bfloat16).reshape(row_count, -1)
        run_key_all = lax.all_gather(key_b, "ctx", axis=0, tiled=True)
        value_all = lax.all_gather(value_b, "ctx", axis=0, tiled=True)
        run_key_all = run_key_all.reshape(-1, local_heads, HD)
        value_all = value_all.reshape(-1, local_heads, HD)
        scores = masked_scores(run_query_b, run_key_all, run_allowed)
        row_top = jnp.max(scores, axis=-1, keepdims=True)
        weights = jnp.exp(scores - row_top)
        row_total = jnp.sum(weights, axis=-1, keepdims=True)
        log_total = row_top + jnp.log(row_total)
        probs_low = (weights / row_total).astype(jnp.bfloat16)
        attend = (
            jnp.einsum("hqk,khd->qhd", probs_low, value_all, preferred_element_type=jnp.float32)
            .astype(jnp.bfloat16)
            .reshape(row_count, -1)
        )
        attn_out = lax.psum(plain_product(attend, out_w), "tensor")
        middle = residual_in + BRANCH_SCALE * attn_out
        normed_two, inverse_two = norm_parts(middle)
        second_in = (normed_two * gain_b).astype(jnp.bfloat16)
        gate_proj = plain_product(second_in, gate_w)
        up_proj = plain_product(second_in, up_w)
        gate_sig = jax.nn.sigmoid(gate_proj)
        gate_act = gate_proj * gate_sig
        hidden = (gate_act * up_proj).astype(jnp.bfloat16)
        mlp_out = lax.psum(plain_product(hidden, down_w).astype(jnp.bfloat16), "tensor").astype(
            jnp.float32
        )
        layer_rows = ((middle + BRANCH_SCALE * mlp_out) * live_mask).astype(jnp.bfloat16)
        grad_y = cotangent[slot_index].astype(jnp.float32) * live_mask
        grad_mlp = (BRANCH_SCALE * grad_y).astype(jnp.bfloat16)
        grad_down_w = row_product(hidden, grad_mlp)
        grad_hidden = col_product(grad_mlp, down_w)
        grad_gate_b = (
            grad_hidden * up_proj * gate_sig * (1.0 + gate_proj * (1.0 - gate_sig))
        ).astype(jnp.bfloat16)
        grad_up_b = (grad_hidden * gate_act).astype(jnp.bfloat16)
        grad_gate_w = row_product(second_in, grad_gate_b)
        grad_up_w = row_product(second_in, grad_up_b)
        grad_second = lax.psum(
            col_product(grad_gate_b, gate_w) + col_product(grad_up_b, up_w), "tensor"
        )
        grad_gain_two = jnp.sum(grad_second * normed_two, axis=0)
        grad_middle = grad_y + norm_back(grad_second, normed_two, inverse_two, gain_b)
        grad_attn = (BRANCH_SCALE * grad_middle).astype(jnp.bfloat16)
        grad_out_w = row_product(attend, grad_attn)
        grad_attend = (
            col_product(grad_attn, out_w).astype(jnp.bfloat16).reshape(row_count, local_heads, HD)
        )
        probs_new = jnp.exp(masked_scores(run_query_b, run_key_all, run_allowed) - log_total)
        grad_probs = jnp.einsum(
            "qhd,khd->hqk", grad_attend, value_all, preferred_element_type=jnp.float32
        )
        grad_scores = (
            probs_new * (grad_probs - jnp.sum(probs_new * grad_probs, axis=-1, keepdims=True))
        ).astype(jnp.bfloat16)
        grad_query_f = (
            jnp.einsum("hqk,khd->qhd", grad_scores, run_key_all, preferred_element_type=jnp.float32)
            * score_scale
        )
        grad_key_all = (
            jnp.einsum("hqk,qhd->khd", grad_scores, run_query_b, preferred_element_type=jnp.float32)
            * score_scale
        )
        grad_value_all = jnp.einsum(
            "hqk,qhd->khd",
            probs_new.astype(jnp.bfloat16),
            grad_attend,
            preferred_element_type=jnp.float32,
        )
        grad_key_own = lax.psum_scatter(
            grad_key_all.reshape(grad_key_all.shape[0], -1), "ctx", scatter_dimension=0, tiled=True
        )
        grad_value_own = lax.psum_scatter(
            grad_value_all.reshape(grad_value_all.shape[0], -1),
            "ctx",
            scatter_dimension=0,
            tiled=True,
        )
        grad_query_b = (
            rotate(grad_query_f, cos_own, sin_own, -1.0).astype(jnp.bfloat16).reshape(row_count, -1)
        )
        grad_key_b = (
            rotate(grad_key_own.reshape(row_count, local_heads, HD), cos_own, sin_own, -1.0)
            .astype(jnp.bfloat16)
            .reshape(row_count, -1)
        )
        grad_value_b = grad_value_own.astype(jnp.bfloat16)
        grad_query_w = row_product(first_in, grad_query_b)
        grad_key_w = row_product(first_in, grad_key_b)
        grad_value_w = row_product(first_in, grad_value_b)
        grad_first = lax.psum(
            (
                col_product(grad_query_b, query_w)
                + col_product(grad_key_b, key_w)
                + col_product(grad_value_b, value_w)
            ).astype(jnp.bfloat16),
            "tensor",
        ).astype(jnp.float32)
        grad_gain_one = jnp.sum(grad_first * normed_one, axis=0)
        grad_rows = grad_middle + norm_back(grad_first, normed_one, inverse_one, gain_a)
        slot_grads = (
            grad_gain_one,
            grad_query_w,
            grad_key_w,
            grad_value_w,
            grad_out_w,
            grad_gain_two,
            grad_gate_w,
            grad_up_w,
            grad_down_w,
        )
        layer_rows, grad_rows, slot_grads = (layer_rows, grad_rows, slot_grads)
        out_blocks.append(layer_rows)
        grad_blocks.append(grad_rows)
        if totals is None:
            totals = slot_grads
        else:
            totals = tuple(
                (left_val + right_val for left_val, right_val in zip(totals, slot_grads))
            )
    (
        sum_gain_one,
        sum_query,
        sum_key,
        sum_value,
        sum_out,
        sum_gain_two,
        sum_gate,
        sum_up,
        sum_down,
    ) = totals
    spread = (
        lax.psum_scatter(sum_gain_one, ("shard", "ctx"), scatter_dimension=0, tiled=True),
        lax.psum_scatter(sum_query, ("shard", "ctx"), scatter_dimension=0, tiled=True),
        lax.psum_scatter(sum_key, ("shard", "ctx"), scatter_dimension=0, tiled=True),
        lax.psum_scatter(sum_value, ("shard", "ctx"), scatter_dimension=0, tiled=True),
        lax.psum_scatter(sum_out, ("shard", "ctx"), scatter_dimension=1, tiled=True),
        lax.psum_scatter(sum_gain_two, ("shard", "ctx"), scatter_dimension=0, tiled=True),
        lax.psum_scatter(sum_gate, ("shard", "ctx"), scatter_dimension=0, tiled=True),
        lax.psum_scatter(sum_up, ("shard", "ctx"), scatter_dimension=0, tiled=True),
        lax.psum_scatter(sum_down, ("shard", "ctx"), scatter_dimension=1, tiled=True),
    )
    (
        part_gain_one,
        part_query,
        part_key,
        part_value,
        part_out,
        part_gain_two,
        part_gate,
        part_up,
        part_down,
    ) = spread
    final = (
        lax.all_gather(part_gain_one.astype(jnp.bfloat16), "ctx", axis=0, tiled=True).astype(
            part_gain_one.dtype
        ),
        lax.all_gather(part_query.astype(jnp.bfloat16), "ctx", axis=0, tiled=True).astype(
            part_query.dtype
        ),
        lax.all_gather(part_key.astype(jnp.bfloat16), "ctx", axis=0, tiled=True).astype(
            part_key.dtype
        ),
        lax.all_gather(part_value.astype(jnp.bfloat16), "ctx", axis=0, tiled=True).astype(
            part_value.dtype
        ),
        lax.all_gather(part_out.astype(jnp.bfloat16), "ctx", axis=1, tiled=True).astype(
            part_out.dtype
        ),
        lax.all_gather(part_gain_two.astype(jnp.bfloat16), "ctx", axis=0, tiled=True).astype(
            part_gain_two.dtype
        ),
        lax.all_gather(part_gate.astype(jnp.bfloat16), "ctx", axis=0, tiled=True).astype(
            part_gate.dtype
        ),
        lax.all_gather(part_up.astype(jnp.bfloat16), "ctx", axis=0, tiled=True).astype(
            part_up.dtype
        ),
        lax.all_gather(part_down.astype(jnp.bfloat16), "ctx", axis=1, tiled=True).astype(
            part_down.dtype
        ),
    )
    layer_out = jnp.stack(out_blocks, axis=0)
    grad_tokens = jnp.stack(grad_blocks, axis=0)
    return (
        layer_out,
        grad_tokens,
        final[0],
        final[1],
        final[2],
        final[3],
        final[4],
        final[5],
        final[6],
        final[7],
        final[8],
    )


LANES = 128
QUERY_TILE = 256


def lane_partner(values_in):
    lane = lax.broadcasted_iota(jnp.int32, values_in.shape, 1) % HD
    return jnp.where(
        lane < HD // 2,
        -pltpu.roll(values_in, LANES - HD // 2, 1),
        pltpu.roll(values_in, HD // 2, 1),
    )


def head_lanes(values_in, head):
    lane = lax.broadcasted_iota(jnp.int32, values_in.shape, 1)
    return jnp.where(lane // HD == head, values_in, jnp.zeros_like(values_in))


def tile_allowed(rows, start, length):
    key = lax.broadcasted_iota(jnp.int32, (rows, QUERY_TILE), 0)
    query = lax.broadcasted_iota(jnp.int32, (rows, QUERY_TILE), 1) + start
    return (key <= query) & (key < length)


def attend_kernel(
    heads, span, order, length, q_in, k_in, v_in, cos, sin, out, q_out, k_out, v_out, log_out,
    q_sort, k_sort, v_sort, turned,
):
    rows = q_in.shape[0]
    pair = pl.program_id(0)
    for block in range(rows // span):
        place = pl.ds(pl.multiple_of(order[block] * span, span), span)
        stored = slice(block * span, (block + 1) * span)
        q_sort[place, :] = q_in[stored, :]
        k_sort[place, :] = k_in[stored, :]
        v_sort[place, :] = v_in[stored, :]
    queries = q_sort[...]
    keys = k_sort[...]
    q_out[...] = (queries * cos[...] + lane_partner(queries) * sin[...]).astype(jnp.bfloat16)
    k_out[...] = (keys * cos[...] + lane_partner(keys) * sin[...]).astype(jnp.bfloat16)
    v_out[...] = v_sort[...].astype(jnp.bfloat16)
    values_t = jnp.transpose(v_out[...])
    turned[...] = jnp.zeros_like(turned)
    log_out[...] = jnp.zeros_like(log_out)
    for head in range(LANES // HD):

        @pl.when(pair * (LANES // HD) + head < heads)
        def _():
            for start in range(0, rows, QUERY_TILE):
                used = start + QUERY_TILE
                query = head_lanes(q_out[start:used, :] * (HD**-0.5), head).astype(jnp.bfloat16)
                scores = col_product(k_out[:used, :], query)
                scores = jnp.where(tile_allowed(used, start, length[0]), scores, -1e30)
                top = jnp.max(scores, axis=0, keepdims=True)
                weights = jnp.exp(scores - top)
                total = jnp.sum(weights, axis=0, keepdims=True)
                probs = (weights * (1.0 / total)).astype(jnp.bfloat16)
                turned[head * HD : (head + 1) * HD, start:used] = plain_product(
                    values_t[head * HD : (head + 1) * HD, :used], probs
                )
                log_out[0, head : head + 1, start:used] = top + jnp.log(total)

    q_sort[...] = jnp.transpose(turned[...])
    for block in range(rows // span):
        place = pl.ds(pl.multiple_of(order[block] * span, span), span)
        out[block * span : (block + 1) * span, :] = q_sort[place, :].astype(jnp.bfloat16)


def attend_back_kernel(
    heads, span, order, length, q_in, k_in, v_in, log_in, o_in, do_in, cos, sin, grads,
    o_sort, do_sort, dq_turned, dq_sum, dk_sum, dv_sum, piece, sems,
):
    rows = q_in.shape[0]
    pair = pl.program_id(0)
    pairs = pl.num_programs(0)
    for block in range(rows // span):
        place = pl.ds(pl.multiple_of(order[block] * span, span), span)
        stored = slice(block * span, (block + 1) * span)
        o_sort[place, :] = o_in[stored, :].astype(jnp.float32)
        do_sort[place, :] = do_in[stored, :].astype(jnp.float32)
    means_t = jnp.transpose(o_sort[...] * do_sort[...])
    keys_t = jnp.transpose(k_in[...])
    dq_turned[...] = jnp.zeros_like(dq_turned)
    dk_sum[...] = jnp.zeros_like(dk_sum)
    dv_sum[...] = jnp.zeros_like(dv_sum)
    for head in range(LANES // HD):

        @pl.when(pair * (LANES // HD) + head < heads)
        def _():
            inner = jnp.sum(means_t[head * HD : (head + 1) * HD, :], axis=0, keepdims=True)
            for start in range(0, rows, QUERY_TILE):
                used = start + QUERY_TILE
                query = head_lanes(q_in[start:used, :] * (HD**-0.5), head).astype(jnp.bfloat16)
                grad_o = head_lanes(do_sort[start:used, :], head).astype(jnp.bfloat16)
                scores = col_product(k_in[:used, :], query)
                probs = jnp.where(
                    tile_allowed(used, start, length[0]),
                    jnp.exp(scores - log_in[0, head : head + 1, start:used]),
                    0.0,
                )
                grad_p = col_product(v_in[:used, :], grad_o)
                grad_s = (probs * (grad_p - inner[:, start:used])).astype(jnp.bfloat16)
                dv_sum[:used, :] += plain_product(probs.astype(jnp.bfloat16), grad_o)
                dk_sum[:used, :] += plain_product(grad_s, query)
                dq_turned[head * HD : (head + 1) * HD, start:used] = plain_product(
                    keys_t[head * HD : (head + 1) * HD, :used], grad_s
                )

    grad_q = jnp.transpose(dq_turned[...]) * (HD**-0.5)
    grad_k = dk_sum[...]
    dq_sum[...] = grad_q * cos[...] - lane_partner(grad_q) * sin[...]
    dk_sum[...] = grad_k * cos[...] - lane_partner(grad_k) * sin[...]
    copies = []
    for which, total in enumerate((dq_sum, dk_sum, dv_sum)):
        for block in range(rows // span):
            place = pl.ds(pl.multiple_of(order[block] * span, span), span)
            piece[which, block * span : (block + 1) * span, :] = total[place, :].astype(jnp.bfloat16)
        column = pl.multiple_of((which * pairs + pair) * LANES, LANES)
        copies.append(
            pltpu.make_async_copy(
                piece.at[which], grads.at[:, pl.ds(column, LANES)], sems.at[which]
            )
        )
        copies[-1].start()
    for copy in copies:
        copy.wait()


def attend_forward(heads, span, order, length, qkv, cos, sin):
    rows = qkv.shape[0]
    pairs = qkv.shape[1] // (3 * LANES)
    column = lambda offset: pl.BlockSpec((rows, LANES), lambda i, *_: (0, offset + i))
    fixed = pl.BlockSpec((rows, LANES), lambda i, *_: (0, 0))
    flat = jax.ShapeDtypeStruct((rows, pairs * LANES), jnp.bfloat16)
    return pl.pallas_call(
        functools.partial(attend_kernel, heads, span),
        grid_spec=pltpu.PrefetchScalarGridSpec(
            num_scalar_prefetch=2,
            grid=(pairs,),
            in_specs=[column(0), column(pairs), column(2 * pairs), fixed, fixed],
            out_specs=[column(0)] * 4 + [pl.BlockSpec((1, 8, rows), lambda i, *_: (i, 0, 0))],
            scratch_shapes=[pltpu.VMEM((rows, LANES), jnp.float32)] * 3
            + [pltpu.VMEM((LANES, rows), jnp.float32)],
        ),
        out_shape=[flat] * 4 + [jax.ShapeDtypeStruct((pairs, 8, rows), jnp.float32)],
        compiler_params=pltpu.CompilerParams(vmem_limit_bytes=40 << 20),
        cost_estimate=pl.CostEstimate(
            flops=4 * heads * rows * rows * HD,
            bytes_accessed=rows * pairs * LANES * 24,
            transcendentals=heads * rows * rows,
        ),
        name="attend",
    )(order, length, qkv, qkv, qkv, cos, sin)


def attend_backward(heads, span, order, length, kept, attend, grad_attend, cos, sin):
    queries, keys, values, logs = kept
    rows = queries.shape[0]
    pairs = queries.shape[1] // LANES
    column = pl.BlockSpec((rows, LANES), lambda i, *_: (0, i))
    fixed = pl.BlockSpec((rows, LANES), lambda i, *_: (0, 0))
    return pl.pallas_call(
        functools.partial(attend_back_kernel, heads, span),
        grid_spec=pltpu.PrefetchScalarGridSpec(
            num_scalar_prefetch=2,
            grid=(pairs,),
            in_specs=[column] * 3
            + [pl.BlockSpec((1, 8, rows), lambda i, *_: (i, 0, 0)), column, column, fixed, fixed],
            out_specs=pl.BlockSpec(memory_space=pl.ANY),
            scratch_shapes=[pltpu.VMEM((rows, LANES), jnp.float32)] * 2
            + [pltpu.VMEM((LANES, rows), jnp.float32)]
            + [pltpu.VMEM((rows, LANES), jnp.float32)] * 3
            + [pltpu.VMEM((3, rows, LANES), jnp.bfloat16), pltpu.SemaphoreType.DMA((3,))],
        ),
        out_shape=jax.ShapeDtypeStruct((rows, 3 * pairs * LANES), jnp.bfloat16),
        compiler_params=pltpu.CompilerParams(vmem_limit_bytes=40 << 20),
        cost_estimate=pl.CostEstimate(
            flops=10 * heads * rows * rows * HD,
            bytes_accessed=rows * pairs * LANES * 16,
            transcendentals=heads * rows * rows,
        ),
        name="attend_back",
    )(order, length, queries, keys, values, logs, attend, grad_attend, cos, sin)


def columns_kernel(count, each, used, core, own, other, *outs):
    mine = pl.program_id(0) == core[0]
    for k in range(own.shape[0]):
        rows = jnp.where(mine, own[k].astype(jnp.float32), other[k].astype(jnp.float32))
        for j in range(count):
            outs[j][:, k * used : (k + 1) * used] = rows[:, j * each : j * each + used]


def join_columns(core, own, other, count, each, used):
    pieces, rows, cols = own.shape
    tile = rows // 3 if rows % 48 == 0 else rows
    taken = pl.BlockSpec((pieces, tile, cols), lambda c, r, *_: (0, r, 0))
    given = pl.BlockSpec((tile, pieces * used), lambda c, r, *_: (c * (rows // tile) + r, 0))
    return pl.pallas_call(
        functools.partial(columns_kernel, count, each, used),
        grid_spec=pltpu.PrefetchScalarGridSpec(
            num_scalar_prefetch=1,
            grid=(2, rows // tile),
            in_specs=[taken, taken],
            out_specs=[given] * count,
        ),
        out_shape=[jax.ShapeDtypeStruct((2 * rows, pieces * used), jnp.float32)] * count,
        compiler_params=pltpu.CompilerParams(vmem_limit_bytes=40 << 20),
        cost_estimate=pl.CostEstimate(
            flops=0, bytes_accessed=8 * pieces * rows * (cols + used * count), transcendentals=0
        ),
        name="join_columns",
    )(core, own, other)


def swap_pairs():
    return [(0, 1), (1, 0)]


class LineGather:
    def __init__(self, block, axis, size):
        self.axis, self.size = axis, size
        self.ups, self.downs = [block], [block]

    def step(self):
        done = len(self.ups)
        up_pairs = [(i, i + 1) for i in range(done - 1, self.size - 1)]
        down_pairs = [(i, i - 1) for i in range(1, self.size - done + 1)]
        self.ups.append(lax.ppermute(self.ups[-1], self.axis, up_pairs))
        self.downs.append(lax.ppermute(self.downs[-1], self.axis, down_pairs))

    def held(self):
        return (self.ups[-1], self.downs[-1])

    def hold(self, values):
        self.ups[-1], self.downs[-1] = values

    def near(self, mask):
        place = lax.axis_index(self.axis)
        found = None
        for here in range(self.size):
            there = here ^ mask
            block = self.ups[here - there] if there < here else self.downs[there - here]
            found = block if found is None else jnp.where(place == here, block, found)
        return found

    def at(self, target):
        gap = lax.axis_index(self.axis) - target
        found = self.ups[0]
        for hops in range(1, self.size):
            found = jnp.where(gap == hops, self.ups[hops], found)
            found = jnp.where(gap == -hops, self.downs[hops], found)
        return found


class LineScatter:
    def __init__(self, parts, axis, size):
        self.axis, self.size, self.parts = axis, size, parts
        self.done = 0
        self.up = self.down = None

    def part(self, offsets):
        place = lax.axis_index(self.axis)
        masks = {}
        for here, there in offsets:
            masks.setdefault(here ^ there, []).append(here)
        found = None
        for mask, places in sorted(masks.items()):
            if found is None:
                found = self.parts[mask]
                continue
            chosen = functools.reduce(jnp.logical_or, [place == here for here in places])
            found = jnp.where(chosen, self.parts[mask], found)
        return found

    def step(self):
        self.done += 1
        gap = self.size - self.done
        ups = [(i, i + gap) for i in range(self.done)]
        downs = [(i, i - gap) for i in range(gap, self.size)]
        up, down = self.part(ups), self.part(downs)
        if self.done > 1:
            up = (up.astype(jnp.float32) + self.up.astype(jnp.float32)).astype(jnp.bfloat16)
            down = (down.astype(jnp.float32) + self.down.astype(jnp.float32)).astype(jnp.bfloat16)
        self.up = lax.ppermute(up, self.axis, [(i, i + 1) for i, _ in ups])
        self.down = lax.ppermute(down, self.axis, [(i, i - 1) for i, _ in downs])

    def held(self):
        return (self.up, self.down)

    def hold(self, values):
        self.up, self.down = values

    def total(self):
        return (
            self.parts[0].astype(jnp.float32)
            + self.up.astype(jnp.float32)
            + self.down.astype(jnp.float32)
        )


def stage(chains, *arrays):
    held = [chain.held() for chain in chains]
    held, arrays = lax.optimization_barrier((held, arrays))
    for chain, values in zip(chains, held):
        chain.hold(values)
    return arrays


def column_split(
    shape,
    tokens,
    lengths,
    span_order,
    attn_gain,
    w_query,
    w_key,
    w_value,
    w_out,
    mlp_gain,
    w_gate,
    w_up,
    w_down,
    cotangent,
):
    shards, lines, cores = shape["shard"], shape["ctx"], shape["tensor"]
    line = lax.axis_index("ctx")
    core = lax.axis_index("tensor")
    per_half = lines // cores
    owner = core == line // per_half
    sub = line % per_half
    slot_count, row_count, width = tokens.shape
    all_rows = row_count * lines
    heads = w_query.shape[1] * cores // lines // HD
    head_cols = heads * HD
    pad_cols = -(-head_cols // LANES) * LANES
    widen = lambda v, dim: jnp.pad(v, [(0, pad_cols - head_cols if d == dim else 0) for d in (0, 1)])
    unit_cols = w_gate.shape[1] * cores // lines

    def column_piece(weights, shape_up=lambda v: v):
        cut = [
            shape_up(
                lax.dynamic_slice_in_dim(w, sub * (w.shape[1] // per_half), w.shape[1] // per_half, 1)
            )
            for w in weights
        ]
        return jnp.concatenate(cut, axis=1) if len(cut) > 1 else cut[0]

    def turned_piece(w):
        rows = w.shape[0] // per_half
        return jnp.transpose(lax.dynamic_slice_in_dim(w, sub * rows, rows, 0))

    def to_pair(piece):
        rows = piece.shape[0] // cores
        keep = lax.dynamic_slice_in_dim(piece, core * rows, rows, 0)
        give = lax.dynamic_slice_in_dim(piece, (1 - core) * rows, rows, 0)
        got = lax.ppermute(give, "tensor", swap_pairs())
        return jnp.where(owner, keep, got)

    def gather_pair(mine):
        return lax.all_gather(mine, ("shard", "tensor"), axis=0, tiled=True)

    def reduce_pair(grad):
        return lax.psum_scatter(grad, ("shard", "tensor"), scatter_dimension=0, tiled=True)

    def gain_marks(weights, piece):
        used = weights.shape[1]
        total = jnp.sum(
            weights.astype(jnp.float32) * piece[:, :used].astype(jnp.float32), axis=1, keepdims=True
        )
        high = total.astype(jnp.bfloat16)
        low = (total - high.astype(jnp.float32)).astype(jnp.bfloat16)
        return jnp.concatenate([high, low], axis=1)

    def line_pieces(chain):
        half = lambda c: jnp.stack([chain.at(c * per_half + k) for k in range(per_half)])
        give = half(1 - core)
        return half(core), lax.ppermute(give, "tensor", swap_pairs()), give

    def gain_total(found, column, gain):
        marks = [pieces[:, :, column : column + 2].astype(jnp.float32) for pieces in found]
        own = jnp.sum(marks[0] + marks[1], axis=(0, 2))
        other = lax.ppermute(own, "tensor", swap_pairs())
        total = jnp.concatenate(
            [jnp.where(core == 0, own, other), jnp.where(core == 0, other, own)]
        )
        return total / gain.astype(jnp.float32)

    def walk(block):
        return LineGather(block, "ctx", lines)

    def add_up(parts):
        return LineScatter(parts, "ctx", lines)

    def blocks_of(v):
        v = v.astype(jnp.bfloat16)
        return [v[k * row_count : (k + 1) * row_count] for k in range(v.shape[0] // row_count)]

    length = lengths[core]
    offsets = jnp.arange(row_count // 2, dtype=jnp.int32)
    stored_pos = (span_order[:, None] * (row_count // 2) + offsets[None, :]).reshape(lines, row_count)
    ring_pos = stored_pos[line ^ jnp.arange(lines)].reshape(-1)
    own_pos = ring_pos[:row_count]
    span = row_count // 2
    order = ring_pos[::span] // span
    frequency = ROPE_BASE ** (-(jnp.arange(HD // 2) * 2).astype(jnp.float32) / HD)
    angles = jnp.arange(all_rows, dtype=jnp.float32)[:, None] * jnp.tile(frequency, 2 * LANES // HD)
    cos_all, sin_all = jnp.cos(angles), jnp.sin(angles)
    live_all = (ring_pos < length).astype(jnp.float32)[:, None]
    live_own = live_all[:row_count]
    core_index = core.astype(jnp.int32).reshape(1)
    own_tokens = lax.dynamic_index_in_dim(tokens, core, 0, keepdims=False)
    own_cot = lax.dynamic_index_in_dim(cotangent, core, 0, keepdims=False)

    own_tokens, w_query, w_key, w_value = lax.optimization_barrier(
        (own_tokens, w_query, w_key, w_value)
    )
    tokens_line = walk(own_tokens)
    tokens_line.step()
    qkv_mine = to_pair(column_piece([w_query, w_key, w_value], lambda v: widen(v, 1)))
    qkv_w = gather_pair(qkv_mine)
    w_out, w_down, gain_pair = stage(
        [tokens_line], w_out, w_down, jnp.stack([attn_gain, mlp_gain])
    )
    tokens_line.step()
    gains = lax.all_gather(gain_pair, "shard", axis=1, tiled=True)
    gain_a = gains[0].astype(jnp.float32)
    gain_b = gains[1].astype(jnp.float32)
    out_mine = to_pair(widen(turned_piece(w_out), 1))
    down_mine = to_pair(turned_piece(w_down))
    gain_a, gain_b, out_mine, own_cot, cos_all, sin_all, order, w_gate, w_up = stage(
        [tokens_line], gain_a, gain_b, out_mine, own_cot, cos_all, sin_all, order, w_gate, w_up
    )
    tokens_line.step()
    out_w = gather_pair(out_mine)
    gate_up_mine = to_pair(column_piece([w_gate, w_up]))
    own_cot, down_mine, gate_up_mine = stage([tokens_line], own_cot, down_mine, gate_up_mine)
    down_w = gather_pair(down_mine)

    cot_line = walk(own_cot)
    cot_line.step()
    all_tokens = jnp.concatenate([tokens_line.near(k) for k in range(lines)], axis=0)
    first_in = (norm_parts(all_tokens.astype(jnp.float32))[0] * gain_a).astype(jnp.bfloat16)
    qkv = plain_product(first_in, qkv_w)
    qkv, gate_up_mine = stage([cot_line], qkv, gate_up_mine)
    gate_up_w = gather_pair(gate_up_mine)

    cot_line.step()
    attend, *kept = attend_forward(heads, span, order, length.reshape(1), qkv, cos_all, sin_all)
    (attend,) = stage([cot_line], attend)

    cot_line.step()
    attn_part = col_product(attend, out_w).astype(jnp.bfloat16)
    attn_line = add_up(blocks_of(attn_part))
    attn_line.step()
    stage([attn_line, cot_line])
    attn_line.step()
    all_cot = jnp.concatenate([cot_line.near(k) for k in range(lines)], axis=0)
    grad_mlp = (BRANCH_SCALE * (all_cot.astype(jnp.float32) * live_all)).astype(jnp.bfloat16)
    (grad_mlp,) = stage([attn_line], grad_mlp)
    attn_line.step()
    half_rows = all_rows // 2
    grad_hidden = [
        plain_product(grad_mlp[k * half_rows : (k + 1) * half_rows], down_w) for k in range(2)
    ]
    grad_hidden = stage([attn_line], *grad_hidden)
    own_x = own_tokens.astype(jnp.float32)
    middle = own_x + BRANCH_SCALE * attn_line.total()
    normed_two, inverse_two = norm_parts(middle)

    second_line = walk((normed_two * gain_b).astype(jnp.bfloat16))
    second_line.step()
    stage([second_line])

    def units(second_half, grad_half):
        gate_up = plain_product(second_half, gate_up_w)
        gate_proj = gate_up[:, :unit_cols]
        up_proj = gate_up[:, unit_cols:]
        gate_sig = jax.nn.sigmoid(gate_proj)
        gate_act = gate_proj * gate_sig
        hidden_half = (gate_act * up_proj).astype(jnp.bfloat16)
        grad_gate_b = (
            grad_half * up_proj * gate_sig * (1.0 + gate_proj * (1.0 - gate_sig))
        ).astype(jnp.bfloat16)
        grad_up_b = (grad_half * gate_act).astype(jnp.bfloat16)
        return hidden_half, jnp.concatenate([grad_gate_b, grad_up_b], axis=1)

    near_half = jnp.concatenate([second_line.near(k) for k in range(lines // 2)], axis=0)
    second_line.step()
    hidden_near, grad_near = units(near_half, grad_hidden[0])
    hidden_near, grad_near = stage([second_line], hidden_near, grad_near)
    second_line.step()
    part_near = col_product(grad_near, gate_up_w).astype(jnp.bfloat16)
    (part_near,) = stage([second_line], part_near)
    far_half = jnp.concatenate([second_line.near(k) for k in range(lines // 2, lines)], axis=0)
    hidden_far, grad_far = units(far_half, grad_hidden[1])
    part_far = col_product(grad_far, gate_up_w).astype(jnp.bfloat16)
    hidden_far, grad_far, part_far = lax.optimization_barrier((hidden_far, grad_far, part_far))

    grad_line = add_up(blocks_of(part_near) + blocks_of(part_far))
    grad_line.step()
    second_in = jnp.concatenate([near_half, far_half], axis=0)
    grad_gate_up = jnp.concatenate([grad_near, grad_far], axis=0)
    gate_up_grad = row_product(second_in, grad_gate_up).astype(jnp.bfloat16)
    hidden = jnp.concatenate([hidden_near, hidden_far], axis=0)
    gate_up_grad, hidden = stage([grad_line], gate_up_grad, hidden)
    grad_line.step()
    gate_up_piece = reduce_pair(gate_up_grad)
    down_grad = row_product(grad_mlp, hidden).astype(jnp.bfloat16)
    down_grad, hidden = stage([grad_line], down_grad, hidden)
    grad_line.step()
    down_piece = reduce_pair(down_grad)
    mlp_part = col_product(hidden, down_w).astype(jnp.bfloat16)
    (mlp_part,) = stage([grad_line], mlp_part)
    grad_second = grad_line.total()

    own_dy = own_cot.astype(jnp.float32) * live_own
    grad_middle = own_dy + norm_back(grad_second, normed_two, inverse_two, gain_b)
    attn_grad_line = walk((BRANCH_SCALE * grad_middle).astype(jnp.bfloat16))
    attn_grad_line.step()
    (mlp_part,) = stage([attn_grad_line], mlp_part)
    mlp_line = add_up(blocks_of(mlp_part))
    mlp_line.step()
    attn_grad_line.step()
    stage([attn_grad_line, mlp_line])
    attn_grad_line.step()
    mlp_line.step()
    unit_marks = gain_marks(gate_up_mine, gate_up_piece)
    rest = jnp.zeros((unit_marks.shape[0], -(3 * unit_cols + 2) % LANES), jnp.bfloat16)
    (unit_marks,) = stage([attn_grad_line, mlp_line], unit_marks)
    mlp_line.step()
    grad_attn = jnp.concatenate([attn_grad_line.near(k) for k in range(lines)], axis=0)
    out_grad = row_product(grad_attn, attend).astype(jnp.bfloat16)
    grad_attend = plain_product(grad_attn, out_w).astype(jnp.bfloat16)
    grad_attend, out_grad, gate_up_piece = lax.optimization_barrier(
        (grad_attend, out_grad, gate_up_piece)
    )
    unit_block = jnp.concatenate([gate_up_piece, down_piece, unit_marks, rest], axis=1)
    out_grad, grad_attend, unit_block = stage([mlp_line], out_grad, grad_attend, unit_block)
    out_piece = reduce_pair(out_grad)
    unit_line = walk(unit_block)
    unit_line.step()
    grad_qkv = attend_backward(
        heads, span, order, length.reshape(1), kept, attend, grad_attend, cos_all, sin_all
    )
    qkv_grad = row_product(first_in, grad_qkv).astype(jnp.bfloat16)
    grad_qkv, qkv_grad, out_piece = stage([unit_line], grad_qkv, qkv_grad, out_piece)
    unit_line.step()
    qkv_piece = reduce_pair(qkv_grad)
    first_part = col_product(grad_qkv, qkv_w).astype(jnp.bfloat16)

    first_line = add_up(blocks_of(first_part))
    first_line.step()
    layer_rows = ((middle + BRANCH_SCALE * mlp_line.total()) * live_own).astype(jnp.bfloat16)
    (layer_rows,) = stage([unit_line, first_line], layer_rows)
    unit_line.step()
    first_line.step()
    qkv_marks = gain_marks(qkv_mine, qkv_piece)
    head_block = jnp.concatenate(
        [qkv_piece[:, :head_cols], qkv_marks, qkv_piece[:, head_cols + 2 :], out_piece], axis=1
    )
    (head_block,) = stage([unit_line, first_line], head_block)
    head_line = walk(head_block)
    head_line.step()
    first_line.step()
    own, other, give = line_pieces(unit_line)
    final_gate, final_up, final_down = join_columns(
        core_index, own, other, 3, unit_cols, unit_cols
    )
    final_gain_two = gain_total((own, give), 3 * unit_cols, mlp_gain)
    final_gate, final_up, final_down = stage(
        [first_line, head_line], final_gate, final_up, final_down
    )
    head_line.step()
    grad_first = first_line.total()
    normed_one, inverse_one = norm_parts(own_x)
    grad_rows = grad_middle + norm_back(grad_first, normed_one, inverse_one, gain_a)
    (grad_rows,) = stage([head_line], grad_rows)
    head_line.step()

    def both_slots(own):
        other = lax.ppermute(own, "tensor", swap_pairs())
        return jnp.stack(
            [jnp.where(core == 0, own, other), jnp.where(core == 0, other, own)], axis=0
        )

    layer_out = both_slots(layer_rows)
    grad_tokens = both_slots(grad_rows.astype(jnp.bfloat16)).astype(jnp.float32)
    layer_out, grad_tokens = stage([head_line], layer_out, grad_tokens)
    own, other, give = line_pieces(head_line)
    final_query, final_key, final_value, final_out = join_columns(
        core_index, own, other, 4, pad_cols, head_cols
    )
    final_gain_one = gain_total((own, give), head_cols, attn_gain)
    return (
        layer_out,
        grad_tokens,
        final_gain_one,
        final_query,
        final_key,
        final_value,
        jnp.transpose(final_out),
        final_gain_two,
        final_gate,
        final_up,
        jnp.transpose(final_down),
    )


def heads_of(w_query, cores, lines):
    return w_query.shape[1] * cores // lines


def local(shape, *arrays):
    shards, lines, cores = shape["shard"], shape["ctx"], shape["tensor"]
    tokens, w_query, w_gate = arrays[0], arrays[4], arrays[9]
    fits = (
        cores == 2
        and tokens.shape[0] == cores
        and lines % cores == 0
        and lines == 4
        and (w_query.shape[1] * cores) % (lines * HD) == 0
        and (w_gate.shape[1] * cores) % (lines * cores) == 0
        and w_query.shape[0] % cores == 0
        and -(-heads_of(w_query, cores, lines) // LANES) * LANES >= heads_of(w_query, cores, lines) + 2
    )
    if fits:
        return column_split(shape, *arrays)
    return gather_all(*arrays)


def solution(mesh):
    placed = (
        P("shard", "ctx", None),
        P("shard"),
        P(),
        P("shard"),
        P("shard", "tensor"),
        P("shard", "tensor"),
        P("shard", "tensor"),
        P("tensor", "shard"),
        P("shard"),
        P("shard", "tensor"),
        P("shard", "tensor"),
        P("tensor", "shard"),
        P("shard", "ctx", None),
    )
    return jax.shard_map(
        functools.partial(local, dict(mesh.shape)),
        mesh=mesh,
        in_specs=placed,
        out_specs=(
            P("shard", "ctx", None),
            P("shard", "ctx", None),
            P("shard"),
            P("shard", "tensor"),
            P("shard", "tensor"),
            P("shard", "tensor"),
            P("tensor", "shard"),
            P("shard"),
            P("shard", "tensor"),
            P("shard", "tensor"),
            P("tensor", "shard"),
        ),
        check_vma=False,
    )
```

```python
import functools
import math

import jax
import jax.numpy as jnp
from jax import lax
from jax.experimental import pallas as pl
from jax.experimental.pallas import tpu as pltpu
from jax.sharding import PartitionSpec as P

HD = 64


NORM_EPS = 1e-05
ROPE_BASE = 10000.0
BRANCH_SCALE = 1.4 / math.sqrt(40.0)
CONTRACT_ROWS = (((0,), (0,)), ((), ()))
CONTRACT_COLS = (((1,), (1,)), ((), ()))


def row_product(left_mat, right_mat):
    return lax.dot_general(left_mat, right_mat, CONTRACT_ROWS, preferred_element_type=jnp.float32)


def col_product(left_mat, right_mat):
    return lax.dot_general(left_mat, right_mat, CONTRACT_COLS, preferred_element_type=jnp.float32)


def plain_product(left_mat, right_mat):
    return jnp.dot(left_mat, right_mat, preferred_element_type=jnp.float32)


def rope_tables(positions, head_dim):
    frequency = ROPE_BASE ** (-(jnp.arange(head_dim // 2) * 2).astype(jnp.float32) / head_dim)
    angles = positions.astype(jnp.float32)[:, None] * frequency[None, :]
    return (jnp.cos(angles)[:, None, :], jnp.sin(angles)[:, None, :])


def rotate(values_in, cos_table, sin_table, sign_dir):
    half_dim = values_in.shape[-1] // 2
    lead_part = values_in[..., :half_dim]
    tail_part = values_in[..., half_dim:]
    turned = sin_table * sign_dir
    return jnp.concatenate(
        [lead_part * cos_table - tail_part * turned, tail_part * cos_table + lead_part * turned],
        axis=-1,
    )


def norm_parts(values_in):
    inverse = lax.rsqrt(jnp.mean(values_in * values_in, axis=-1, keepdims=True) + NORM_EPS)
    return (values_in * inverse, inverse)


def norm_back(grad_in, normed, inverse, gain_vec):
    scaled = grad_in * gain_vec
    return inverse * (scaled - normed * jnp.mean(scaled * normed, axis=-1, keepdims=True))


def gather_all(
    tokens,
    lengths,
    span_order,
    attn_gain,
    w_query,
    w_key,
    w_value,
    w_out,
    mlp_gain,
    w_gate,
    w_up,
    w_down,
    cotangent,
):
    slot_count, row_count, width = tokens.shape
    local_heads = w_query.shape[1] // HD
    span_rows = row_count // 2
    offsets = jnp.arange(span_rows, dtype=jnp.int32)
    all_pos = (span_order[:, None] * span_rows + offsets[None, :]).reshape(-1)
    own_pos = lax.dynamic_slice_in_dim(all_pos, lax.axis_index("ctx") * row_count, row_count)
    cos_own, sin_own = rope_tables(own_pos, HD)
    causal = all_pos[None, :] <= own_pos[:, None]
    score_scale = HD ** (-0.5)

    def masked_scores(query_b, key_all, allowed):
        raw_scores = (
            jnp.einsum("qhd,khd->hqk", query_b, key_all, preferred_element_type=jnp.float32)
            * score_scale
        )
        return jnp.where(allowed[None], raw_scores, -1e30)

    out_blocks = []
    grad_blocks = []
    totals = None
    for slot_index in range(slot_count):
        length = lengths[slot_index]
        gain_one = lax.all_gather(attn_gain, "shard", axis=0, tiled=True)
        query_w = lax.all_gather(w_query, "shard", axis=0, tiled=True)
        key_w = lax.all_gather(w_key, "shard", axis=0, tiled=True)
        value_w = lax.all_gather(w_value, "shard", axis=0, tiled=True)
        out_w = lax.all_gather(w_out, "shard", axis=1, tiled=True)
        gain_two = lax.all_gather(mlp_gain, "shard", axis=0, tiled=True)
        gate_w = lax.all_gather(w_gate, "shard", axis=0, tiled=True)
        up_w = lax.all_gather(w_up, "shard", axis=0, tiled=True)
        down_w = lax.all_gather(w_down, "shard", axis=1, tiled=True)
        live_mask = (own_pos < length).astype(jnp.float32)[:, None]
        run_allowed = causal & (all_pos < length)[None, :]
        gain_a = gain_one.astype(jnp.float32)
        gain_b = gain_two.astype(jnp.float32)
        residual_in = tokens[slot_index].astype(jnp.float32)
        normed_one, inverse_one = norm_parts(residual_in)
        first_in = (normed_one * gain_a).astype(jnp.bfloat16)
        query_f = plain_product(first_in, query_w).reshape(row_count, local_heads, HD)
        key_f = plain_product(first_in, key_w).reshape(row_count, local_heads, HD)
        value_b = plain_product(first_in, value_w).astype(jnp.bfloat16)
        run_query_b = rotate(query_f, cos_own, sin_own, 1.0).astype(jnp.bfloat16)
        key_b = rotate(key_f, cos_own, sin_own, 1.0).astype(jnp.bfloat16).reshape(row_count, -1)
        run_key_all = lax.all_gather(key_b, "ctx", axis=0, tiled=True)
        value_all = lax.all_gather(value_b, "ctx", axis=0, tiled=True)
        run_key_all = run_key_all.reshape(-1, local_heads, HD)
        value_all = value_all.reshape(-1, local_heads, HD)
        scores = masked_scores(run_query_b, run_key_all, run_allowed)
        row_top = jnp.max(scores, axis=-1, keepdims=True)
        weights = jnp.exp(scores - row_top)
        row_total = jnp.sum(weights, axis=-1, keepdims=True)
        log_total = row_top + jnp.log(row_total)
        probs_low = (weights / row_total).astype(jnp.bfloat16)
        attend = (
            jnp.einsum("hqk,khd->qhd", probs_low, value_all, preferred_element_type=jnp.float32)
            .astype(jnp.bfloat16)
            .reshape(row_count, -1)
        )
        attn_out = lax.psum(plain_product(attend, out_w), "tensor")
        middle = residual_in + BRANCH_SCALE * attn_out
        normed_two, inverse_two = norm_parts(middle)
        second_in = (normed_two * gain_b).astype(jnp.bfloat16)
        gate_proj = plain_product(second_in, gate_w)
        up_proj = plain_product(second_in, up_w)
        gate_sig = jax.nn.sigmoid(gate_proj)
        gate_act = gate_proj * gate_sig
        hidden = (gate_act * up_proj).astype(jnp.bfloat16)
        mlp_out = lax.psum(plain_product(hidden, down_w).astype(jnp.bfloat16), "tensor").astype(
            jnp.float32
        )
        layer_rows = ((middle + BRANCH_SCALE * mlp_out) * live_mask).astype(jnp.bfloat16)
        grad_y = cotangent[slot_index].astype(jnp.float32) * live_mask
        grad_mlp = (BRANCH_SCALE * grad_y).astype(jnp.bfloat16)
        grad_down_w = row_product(hidden, grad_mlp)
        grad_hidden = col_product(grad_mlp, down_w)
        grad_gate_b = (
            grad_hidden * up_proj * gate_sig * (1.0 + gate_proj * (1.0 - gate_sig))
        ).astype(jnp.bfloat16)
        grad_up_b = (grad_hidden * gate_act).astype(jnp.bfloat16)
        grad_gate_w = row_product(second_in, grad_gate_b)
        grad_up_w = row_product(second_in, grad_up_b)
        grad_second = lax.psum(
            col_product(grad_gate_b, gate_w) + col_product(grad_up_b, up_w), "tensor"
        )
        grad_gain_two = jnp.sum(grad_second * normed_two, axis=0)
        grad_middle = grad_y + norm_back(grad_second, normed_two, inverse_two, gain_b)
        grad_attn = (BRANCH_SCALE * grad_middle).astype(jnp.bfloat16)
        grad_out_w = row_product(attend, grad_attn)
        grad_attend = (
            col_product(grad_attn, out_w).astype(jnp.bfloat16).reshape(row_count, local_heads, HD)
        )
        probs_new = jnp.exp(masked_scores(run_query_b, run_key_all, run_allowed) - log_total)
        grad_probs = jnp.einsum(
            "qhd,khd->hqk", grad_attend, value_all, preferred_element_type=jnp.float32
        )
        grad_scores = (
            probs_new * (grad_probs - jnp.sum(probs_new * grad_probs, axis=-1, keepdims=True))
        ).astype(jnp.bfloat16)
        grad_query_f = (
            jnp.einsum("hqk,khd->qhd", grad_scores, run_key_all, preferred_element_type=jnp.float32)
            * score_scale
        )
        grad_key_all = (
            jnp.einsum("hqk,qhd->khd", grad_scores, run_query_b, preferred_element_type=jnp.float32)
            * score_scale
        )
        grad_value_all = jnp.einsum(
            "hqk,qhd->khd",
            probs_new.astype(jnp.bfloat16),
            grad_attend,
            preferred_element_type=jnp.float32,
        )
        grad_key_own = lax.psum_scatter(
            grad_key_all.reshape(grad_key_all.shape[0], -1), "ctx", scatter_dimension=0, tiled=True
        )
        grad_value_own = lax.psum_scatter(
            grad_value_all.reshape(grad_value_all.shape[0], -1),
            "ctx",
            scatter_dimension=0,
            tiled=True,
        )
        grad_query_b = (
            rotate(grad_query_f, cos_own, sin_own, -1.0).astype(jnp.bfloat16).reshape(row_count, -1)
        )
        grad_key_b = (
            rotate(grad_key_own.reshape(row_count, local_heads, HD), cos_own, sin_own, -1.0)
            .astype(jnp.bfloat16)
            .reshape(row_count, -1)
        )
        grad_value_b = grad_value_own.astype(jnp.bfloat16)
        grad_query_w = row_product(first_in, grad_query_b)
        grad_key_w = row_product(first_in, grad_key_b)
        grad_value_w = row_product(first_in, grad_value_b)
        grad_first = lax.psum(
            (
                col_product(grad_query_b, query_w)
                + col_product(grad_key_b, key_w)
                + col_product(grad_value_b, value_w)
            ).astype(jnp.bfloat16),
            "tensor",
        ).astype(jnp.float32)
        grad_gain_one = jnp.sum(grad_first * normed_one, axis=0)
        grad_rows = grad_middle + norm_back(grad_first, normed_one, inverse_one, gain_a)
        slot_grads = (
            grad_gain_one,
            grad_query_w,
            grad_key_w,
            grad_value_w,
            grad_out_w,
            grad_gain_two,
            grad_gate_w,
            grad_up_w,
            grad_down_w,
        )
        layer_rows, grad_rows, slot_grads = (layer_rows, grad_rows, slot_grads)
        out_blocks.append(layer_rows)
        grad_blocks.append(grad_rows)
        if totals is None:
            totals = slot_grads
        else:
            totals = tuple(
                (left_val + right_val for left_val, right_val in zip(totals, slot_grads))
            )
    (
        sum_gain_one,
        sum_query,
        sum_key,
        sum_value,
        sum_out,
        sum_gain_two,
        sum_gate,
        sum_up,
        sum_down,
    ) = totals
    spread = (
        lax.psum_scatter(sum_gain_one, ("shard", "ctx"), scatter_dimension=0, tiled=True),
        lax.psum_scatter(sum_query, ("shard", "ctx"), scatter_dimension=0, tiled=True),
        lax.psum_scatter(sum_key, ("shard", "ctx"), scatter_dimension=0, tiled=True),
        lax.psum_scatter(sum_value, ("shard", "ctx"), scatter_dimension=0, tiled=True),
        lax.psum_scatter(sum_out, ("shard", "ctx"), scatter_dimension=1, tiled=True),
        lax.psum_scatter(sum_gain_two, ("shard", "ctx"), scatter_dimension=0, tiled=True),
        lax.psum_scatter(sum_gate, ("shard", "ctx"), scatter_dimension=0, tiled=True),
        lax.psum_scatter(sum_up, ("shard", "ctx"), scatter_dimension=0, tiled=True),
        lax.psum_scatter(sum_down, ("shard", "ctx"), scatter_dimension=1, tiled=True),
    )
    (
        part_gain_one,
        part_query,
        part_key,
        part_value,
        part_out,
        part_gain_two,
        part_gate,
        part_up,
        part_down,
    ) = spread
    final = (
        lax.all_gather(part_gain_one.astype(jnp.bfloat16), "ctx", axis=0, tiled=True).astype(
            part_gain_one.dtype
        ),
        lax.all_gather(part_query.astype(jnp.bfloat16), "ctx", axis=0, tiled=True).astype(
            part_query.dtype
        ),
        lax.all_gather(part_key.astype(jnp.bfloat16), "ctx", axis=0, tiled=True).astype(
            part_key.dtype
        ),
        lax.all_gather(part_value.astype(jnp.bfloat16), "ctx", axis=0, tiled=True).astype(
            part_value.dtype
        ),
        lax.all_gather(part_out.astype(jnp.bfloat16), "ctx", axis=1, tiled=True).astype(
            part_out.dtype
        ),
        lax.all_gather(part_gain_two.astype(jnp.bfloat16), "ctx", axis=0, tiled=True).astype(
            part_gain_two.dtype
        ),
        lax.all_gather(part_gate.astype(jnp.bfloat16), "ctx", axis=0, tiled=True).astype(
            part_gate.dtype
        ),
        lax.all_gather(part_up.astype(jnp.bfloat16), "ctx", axis=0, tiled=True).astype(
            part_up.dtype
        ),
        lax.all_gather(part_down.astype(jnp.bfloat16), "ctx", axis=1, tiled=True).astype(
            part_down.dtype
        ),
    )
    layer_out = jnp.stack(out_blocks, axis=0)
    grad_tokens = jnp.stack(grad_blocks, axis=0)
    return (
        layer_out,
        grad_tokens,
        final[0],
        final[1],
        final[2],
        final[3],
        final[4],
        final[5],
        final[6],
        final[7],
        final[8],
    )


LANES = 128
QUERY_TILE = 256


def lane_partner(values_in):
    lane = lax.broadcasted_iota(jnp.int32, values_in.shape, 1) % HD
    return jnp.where(
        lane < HD // 2,
        -pltpu.roll(values_in, LANES - HD // 2, 1),
        pltpu.roll(values_in, HD // 2, 1),
    )


def head_lanes(values_in, head):
    lane = lax.broadcasted_iota(jnp.int32, values_in.shape, 1)
    return jnp.where(lane // HD == head, values_in, jnp.zeros_like(values_in))


def tile_allowed(rows, start, length):
    key = lax.broadcasted_iota(jnp.int32, (rows, QUERY_TILE), 0)
    query = lax.broadcasted_iota(jnp.int32, (rows, QUERY_TILE), 1) + start
    return (key <= query) & (key < length)


def attend_kernel(
    heads, span, order, length, q_near, k_near, v_near, q_far, k_far, v_far, cos, sin,
    out, q_out, k_out, v_out, log_out, q_sort, k_sort, v_sort, turned,
):
    rows = q_out.shape[0]
    pair = pl.program_id(0)
    for block in range(rows // span):
        place = pl.ds(pl.multiple_of(order[block] * span, span), span)
        start = block * span
        near = start < q_near.shape[0]
        start -= 0 if near else q_near.shape[0]
        stored = slice(start, start + span)
        q_sort[place, :] = (q_near if near else q_far)[stored, :]
        k_sort[place, :] = (k_near if near else k_far)[stored, :]
        v_sort[place, :] = (v_near if near else v_far)[stored, :]
    queries = q_sort[...]
    keys = k_sort[...]
    q_out[...] = (queries * cos[...] + lane_partner(queries) * sin[...]).astype(jnp.bfloat16)
    k_out[...] = (keys * cos[...] + lane_partner(keys) * sin[...]).astype(jnp.bfloat16)
    v_out[...] = v_sort[...].astype(jnp.bfloat16)
    values_t = jnp.transpose(v_out[...])
    turned[...] = jnp.zeros_like(turned)
    log_out[...] = jnp.zeros_like(log_out)
    for head in range(LANES // HD):

        @pl.when(pair * (LANES // HD) + head < heads)
        def _():
            for start in range(0, rows, QUERY_TILE):
                used = start + QUERY_TILE
                query = head_lanes(q_out[start:used, :] * (HD**-0.5), head).astype(jnp.bfloat16)
                scores = col_product(k_out[:used, :], query)
                scores = jnp.where(tile_allowed(used, start, length[0]), scores, -1e30)
                top = jnp.max(scores, axis=0, keepdims=True)
                weights = jnp.exp(scores - top)
                total = jnp.sum(weights, axis=0, keepdims=True)
                probs = (weights * (1.0 / total)).astype(jnp.bfloat16)
                turned[head * HD : (head + 1) * HD, start:used] = plain_product(
                    values_t[head * HD : (head + 1) * HD, :used], probs
                )
                log_out[0, head : head + 1, start:used] = top + jnp.log(total)

    q_sort[...] = jnp.transpose(turned[...])
    for block in range(rows // span):
        place = pl.ds(pl.multiple_of(order[block] * span, span), span)
        out[block * span : (block + 1) * span, :] = q_sort[place, :].astype(jnp.bfloat16)


def attend_back_kernel(
    heads, span, order, length, q_in, k_in, v_in, log_in, o_in, do_in, cos, sin, grads,
    o_sort, do_sort, dq_turned, dq_sum, dk_sum, dv_sum, piece, sems,
):
    rows = q_in.shape[0]
    pair = pl.program_id(0)
    pairs = pl.num_programs(0)
    for block in range(rows // span):
        place = pl.ds(pl.multiple_of(order[block] * span, span), span)
        stored = slice(block * span, (block + 1) * span)
        o_sort[place, :] = o_in[stored, :].astype(jnp.float32)
        do_sort[place, :] = do_in[stored, :].astype(jnp.float32)
    means_t = jnp.transpose(o_sort[...] * do_sort[...])
    keys_t = jnp.transpose(k_in[...])
    dq_turned[...] = jnp.zeros_like(dq_turned)
    dk_sum[...] = jnp.zeros_like(dk_sum)
    dv_sum[...] = jnp.zeros_like(dv_sum)
    for head in range(LANES // HD):

        @pl.when(pair * (LANES // HD) + head < heads)
        def _():
            inner = jnp.sum(means_t[head * HD : (head + 1) * HD, :], axis=0, keepdims=True)
            for start in range(0, rows, QUERY_TILE):
                used = start + QUERY_TILE
                query = head_lanes(q_in[start:used, :] * (HD**-0.5), head).astype(jnp.bfloat16)
                grad_o = head_lanes(do_sort[start:used, :], head).astype(jnp.bfloat16)
                scores = col_product(k_in[:used, :], query)
                probs = jnp.where(
                    tile_allowed(used, start, length[0]),
                    jnp.exp(scores - log_in[0, head : head + 1, start:used]),
                    0.0,
                )
                grad_p = col_product(v_in[:used, :], grad_o)
                grad_s = (probs * (grad_p - inner[:, start:used])).astype(jnp.bfloat16)
                dv_sum[:used, :] += plain_product(probs.astype(jnp.bfloat16), grad_o)
                dk_sum[:used, :] += plain_product(grad_s, query)
                dq_turned[head * HD : (head + 1) * HD, start:used] = plain_product(
                    keys_t[head * HD : (head + 1) * HD, :used], grad_s
                )

    grad_q = jnp.transpose(dq_turned[...]) * (HD**-0.5)
    grad_k = dk_sum[...]
    dq_sum[...] = grad_q * cos[...] - lane_partner(grad_q) * sin[...]
    dk_sum[...] = grad_k * cos[...] - lane_partner(grad_k) * sin[...]
    copies = []
    for which, total in enumerate((dq_sum, dk_sum, dv_sum)):
        for block in range(rows // span):
            place = pl.ds(pl.multiple_of(order[block] * span, span), span)
            piece[which, block * span : (block + 1) * span, :] = total[place, :].astype(jnp.bfloat16)
        column = pl.multiple_of((which * pairs + pair) * LANES, LANES)
        copies.append(
            pltpu.make_async_copy(
                piece.at[which], grads.at[:, pl.ds(column, LANES)], sems.at[which]
            )
        )
        copies[-1].start()
    for copy in copies:
        copy.wait()


def attend_forward(heads, span, order, length, near, far, cos, sin):
    rows = near.shape[0] + far.shape[0]
    pairs = near.shape[1] // (3 * LANES)
    column = lambda v, offset: pl.BlockSpec((v.shape[0], LANES), lambda i, *_: (0, offset + i))
    fixed = pl.BlockSpec((rows, LANES), lambda i, *_: (0, 0))
    flat = jax.ShapeDtypeStruct((rows, pairs * LANES), jnp.bfloat16)
    return pl.pallas_call(
        functools.partial(attend_kernel, heads, span),
        grid_spec=pltpu.PrefetchScalarGridSpec(
            num_scalar_prefetch=2,
            grid=(pairs,),
            in_specs=[column(v, k * pairs) for v in (near, far) for k in range(3)] + [fixed, fixed],
            out_specs=[column(cos, 0)] * 4 + [pl.BlockSpec((1, 8, rows), lambda i, *_: (i, 0, 0))],
            scratch_shapes=[pltpu.VMEM((rows, LANES), jnp.float32)] * 3
            + [pltpu.VMEM((LANES, rows), jnp.float32)],
        ),
        out_shape=[flat] * 4 + [jax.ShapeDtypeStruct((pairs, 8, rows), jnp.float32)],
        compiler_params=pltpu.CompilerParams(vmem_limit_bytes=40 << 20),
        cost_estimate=pl.CostEstimate(
            flops=4 * heads * rows * rows * HD,
            bytes_accessed=rows * pairs * LANES * 24,
            transcendentals=heads * rows * rows,
        ),
        name="attend",
    )(order, length, near, near, near, far, far, far, cos, sin)


def attend_backward(heads, span, order, length, kept, attend, grad_attend, cos, sin):
    queries, keys, values, logs = kept
    rows = queries.shape[0]
    pairs = queries.shape[1] // LANES
    column = pl.BlockSpec((rows, LANES), lambda i, *_: (0, i))
    fixed = pl.BlockSpec((rows, LANES), lambda i, *_: (0, 0))
    return pl.pallas_call(
        functools.partial(attend_back_kernel, heads, span),
        grid_spec=pltpu.PrefetchScalarGridSpec(
            num_scalar_prefetch=2,
            grid=(pairs,),
            in_specs=[column] * 3
            + [pl.BlockSpec((1, 8, rows), lambda i, *_: (i, 0, 0)), column, column, fixed, fixed],
            out_specs=pl.BlockSpec(memory_space=pl.ANY),
            scratch_shapes=[pltpu.VMEM((rows, LANES), jnp.float32)] * 2
            + [pltpu.VMEM((LANES, rows), jnp.float32)]
            + [pltpu.VMEM((rows, LANES), jnp.float32)] * 3
            + [pltpu.VMEM((3, rows, LANES), jnp.bfloat16), pltpu.SemaphoreType.DMA((3,))],
        ),
        out_shape=jax.ShapeDtypeStruct((rows, 3 * pairs * LANES), jnp.bfloat16),
        compiler_params=pltpu.CompilerParams(vmem_limit_bytes=40 << 20),
        cost_estimate=pl.CostEstimate(
            flops=10 * heads * rows * rows * HD,
            bytes_accessed=rows * pairs * LANES * 16,
            transcendentals=heads * rows * rows,
        ),
        name="attend_back",
    )(order, length, queries, keys, values, logs, attend, grad_attend, cos, sin)


def columns_kernel(count, each, used, core, own, other, *outs):
    mine = pl.program_id(0) == core[0]
    for k in range(own.shape[0]):
        rows = jnp.where(mine, own[k].astype(jnp.float32), other[k].astype(jnp.float32))
        for j in range(count):
            outs[j][:, k * used : (k + 1) * used] = rows[:, j * each : j * each + used]


def join_columns(core, own, other, count, each, used):
    pieces, rows, cols = own.shape
    tile = rows // 3 if rows % 48 == 0 else rows
    taken = pl.BlockSpec((pieces, tile, cols), lambda c, r, *_: (0, r, 0))
    given = pl.BlockSpec((tile, pieces * used), lambda c, r, *_: (c * (rows // tile) + r, 0))
    return pl.pallas_call(
        functools.partial(columns_kernel, count, each, used),
        grid_spec=pltpu.PrefetchScalarGridSpec(
            num_scalar_prefetch=1,
            grid=(2, rows // tile),
            in_specs=[taken, taken],
            out_specs=[given] * count,
        ),
        out_shape=[jax.ShapeDtypeStruct((2 * rows, pieces * used), jnp.float32)] * count,
        compiler_params=pltpu.CompilerParams(vmem_limit_bytes=40 << 20),
        cost_estimate=pl.CostEstimate(
            flops=0, bytes_accessed=8 * pieces * rows * (cols + used * count), transcendentals=0
        ),
        name="join_columns",
    )(core, own, other)


def swap_pairs():
    return [(0, 1), (1, 0)]


class LineGather:
    def __init__(self, block, axis, size):
        self.axis, self.size = axis, size
        self.ups, self.downs = [block], [block]

    def step(self):
        done = len(self.ups)
        up_pairs = [(i, i + 1) for i in range(done - 1, self.size - 1)]
        down_pairs = [(i, i - 1) for i in range(1, self.size - done + 1)]
        self.ups.append(lax.ppermute(self.ups[-1], self.axis, up_pairs))
        self.downs.append(lax.ppermute(self.downs[-1], self.axis, down_pairs))

    def held(self):
        return (self.ups[-1], self.downs[-1])

    def hold(self, values):
        self.ups[-1], self.downs[-1] = values

    def near(self, mask):
        place = lax.axis_index(self.axis)
        found = None
        for here in range(self.size):
            there = here ^ mask
            block = self.ups[here - there] if there < here else self.downs[there - here]
            found = block if found is None else jnp.where(place == here, block, found)
        return found

    def at(self, target):
        gap = lax.axis_index(self.axis) - target
        found = self.ups[0]
        for hops in range(1, self.size):
            found = jnp.where(gap == hops, self.ups[hops], found)
            found = jnp.where(gap == -hops, self.downs[hops], found)
        return found


class LineScatter:
    def __init__(self, parts, axis, size):
        self.axis, self.size, self.parts = axis, size, parts
        self.done = 0
        self.up = self.down = None

    def part(self, offsets):
        place = lax.axis_index(self.axis)
        masks = {}
        for here, there in offsets:
            masks.setdefault(here ^ there, []).append(here)
        found = None
        for mask, places in sorted(masks.items()):
            if found is None:
                found = self.parts[mask]
                continue
            chosen = functools.reduce(jnp.logical_or, [place == here for here in places])
            found = jnp.where(chosen, self.parts[mask], found)
        return found

    def step(self):
        self.done += 1
        gap = self.size - self.done
        ups = [(i, i + gap) for i in range(self.done)]
        downs = [(i, i - gap) for i in range(gap, self.size)]
        up, down = self.part(ups), self.part(downs)
        if self.done > 1:
            up = (up.astype(jnp.float32) + self.up.astype(jnp.float32)).astype(jnp.bfloat16)
            down = (down.astype(jnp.float32) + self.down.astype(jnp.float32)).astype(jnp.bfloat16)
        self.up = lax.ppermute(up, self.axis, [(i, i + 1) for i, _ in ups])
        self.down = lax.ppermute(down, self.axis, [(i, i - 1) for i, _ in downs])

    def held(self):
        return (self.up, self.down)

    def hold(self, values):
        self.up, self.down = values

    def total(self):
        return (
            self.parts[0].astype(jnp.float32)
            + self.up.astype(jnp.float32)
            + self.down.astype(jnp.float32)
        )


def stage(chains, *arrays):
    held = [chain.held() for chain in chains]
    held, arrays = lax.optimization_barrier((held, arrays))
    for chain, values in zip(chains, held):
        chain.hold(values)
    return arrays


def column_split(
    shape,
    tokens,
    lengths,
    span_order,
    attn_gain,
    w_query,
    w_key,
    w_value,
    w_out,
    mlp_gain,
    w_gate,
    w_up,
    w_down,
    cotangent,
):
    shards, lines, cores = shape["shard"], shape["ctx"], shape["tensor"]
    line = lax.axis_index("ctx")
    core = lax.axis_index("tensor")
    per_half = lines // cores
    owner = core == line // per_half
    sub = line % per_half
    slot_count, row_count, width = tokens.shape
    all_rows = row_count * lines
    heads = w_query.shape[1] * cores // lines // HD
    head_cols = heads * HD
    pad_cols = -(-head_cols // LANES) * LANES
    widen = lambda v, dim: jnp.pad(v, [(0, pad_cols - head_cols if d == dim else 0) for d in (0, 1)])
    unit_cols = w_gate.shape[1] * cores // lines

    def column_piece(weights, shape_up=lambda v: v):
        cut = [
            shape_up(
                lax.dynamic_slice_in_dim(w, sub * (w.shape[1] // per_half), w.shape[1] // per_half, 1)
            )
            for w in weights
        ]
        return jnp.concatenate(cut, axis=1) if len(cut) > 1 else cut[0]

    def turned_piece(w):
        rows = w.shape[0] // per_half
        return jnp.transpose(lax.dynamic_slice_in_dim(w, sub * rows, rows, 0))

    def to_pair(piece):
        rows = piece.shape[0] // cores
        keep = lax.dynamic_slice_in_dim(piece, core * rows, rows, 0)
        give = lax.dynamic_slice_in_dim(piece, (1 - core) * rows, rows, 0)
        got = lax.ppermute(give, "tensor", swap_pairs())
        return jnp.where(owner, keep, got)

    def gather_pair(mine):
        return lax.all_gather(mine, ("shard", "tensor"), axis=0, tiled=True)

    def reduce_pair(grad):
        return lax.psum_scatter(grad, ("shard", "tensor"), scatter_dimension=0, tiled=True)

    def gain_marks(weights, piece):
        used = weights.shape[1]
        total = jnp.sum(
            weights.astype(jnp.float32) * piece[:, :used].astype(jnp.float32), axis=1, keepdims=True
        )
        high = total.astype(jnp.bfloat16)
        low = (total - high.astype(jnp.float32)).astype(jnp.bfloat16)
        return jnp.concatenate([high, low], axis=1)

    def line_pieces(chain):
        half = lambda c: jnp.stack([chain.at(c * per_half + k) for k in range(per_half)])
        give = half(1 - core)
        return half(core), lax.ppermute(give, "tensor", swap_pairs()), give

    def gain_total(found, column, gain):
        marks = [pieces[:, :, column : column + 2].astype(jnp.float32) for pieces in found]
        own = jnp.sum(marks[0] + marks[1], axis=(0, 2))
        other = lax.ppermute(own, "tensor", swap_pairs())
        total = jnp.concatenate(
            [jnp.where(core == 0, own, other), jnp.where(core == 0, other, own)]
        )
        return total / gain.astype(jnp.float32)

    def walk(block):
        return LineGather(block, "ctx", lines)

    def add_up(parts):
        return LineScatter(parts, "ctx", lines)

    def blocks_of(v):
        v = v.astype(jnp.bfloat16)
        return [v[k * row_count : (k + 1) * row_count] for k in range(v.shape[0] // row_count)]

    length = lengths[core]
    offsets = jnp.arange(row_count // 2, dtype=jnp.int32)
    stored_pos = (span_order[:, None] * (row_count // 2) + offsets[None, :]).reshape(lines, row_count)
    ring_pos = stored_pos[line ^ jnp.arange(lines)].reshape(-1)
    own_pos = ring_pos[:row_count]
    span = row_count // 2
    order = ring_pos[::span] // span
    frequency = ROPE_BASE ** (-(jnp.arange(HD // 2) * 2).astype(jnp.float32) / HD)
    angles = jnp.arange(all_rows, dtype=jnp.float32)[:, None] * jnp.tile(frequency, 2 * LANES // HD)
    cos_all, sin_all = jnp.cos(angles), jnp.sin(angles)
    live_all = (ring_pos < length).astype(jnp.float32)[:, None]
    live_own = live_all[:row_count]
    core_index = core.astype(jnp.int32).reshape(1)
    own_tokens = lax.dynamic_index_in_dim(tokens, core, 0, keepdims=False)
    own_cot = lax.dynamic_index_in_dim(cotangent, core, 0, keepdims=False)

    own_tokens, w_query, w_key, w_value = lax.optimization_barrier(
        (own_tokens, w_query, w_key, w_value)
    )
    tokens_line = walk(own_tokens)
    tokens_line.step()
    qkv_mine = to_pair(column_piece([w_query, w_key, w_value], lambda v: widen(v, 1)))
    qkv_w = gather_pair(qkv_mine)
    w_out, w_down, gain_pair = stage(
        [tokens_line], w_out, w_down, jnp.stack([attn_gain, mlp_gain])
    )
    tokens_line.step()
    gains = lax.all_gather(gain_pair, "shard", axis=1, tiled=True)
    gain_a = gains[0].astype(jnp.float32)
    gain_b = gains[1].astype(jnp.float32)
    out_mine = to_pair(widen(turned_piece(w_out), 1))
    down_mine = to_pair(turned_piece(w_down))
    gain_a, gain_b, out_mine, own_cot, cos_all, sin_all, order, w_gate, w_up = stage(
        [tokens_line], gain_a, gain_b, out_mine, own_cot, cos_all, sin_all, order, w_gate, w_up
    )
    tokens_line.step()
    out_w = gather_pair(out_mine)
    gate_up_mine = to_pair(column_piece([w_gate, w_up]))

    def first_rows(masks):
        rows = jnp.concatenate([tokens_line.near(k) for k in masks], axis=0)
        return (norm_parts(rows.astype(jnp.float32))[0] * gain_a).astype(jnp.bfloat16)

    first_near = first_rows(range(lines // 2))
    qkv_near = plain_product(first_near, qkv_w)
    own_cot, down_mine, gate_up_mine, qkv_near = stage(
        [tokens_line], own_cot, down_mine, gate_up_mine, qkv_near
    )
    down_w = gather_pair(down_mine)

    cot_line = walk(own_cot)
    cot_line.step()
    first_far = first_rows(range(lines // 2, lines))
    qkv_far = plain_product(first_far, qkv_w)
    qkv_far, gate_up_mine = lax.optimization_barrier((qkv_far, gate_up_mine))
    gate_up_w = gather_pair(gate_up_mine)
    first_in = jnp.concatenate([first_near, first_far], axis=0)
    attend, *kept = attend_forward(
        heads, span, order, length.reshape(1), qkv_near, qkv_far, cos_all, sin_all
    )
    attn_part = col_product(attend, out_w).astype(jnp.bfloat16)
    (attn_part,) = stage([cot_line], attn_part)

    attn_line = add_up(blocks_of(attn_part))
    attn_line.step()
    cot_line.step()
    stage([attn_line, cot_line])
    attn_line.step()
    cot_line.step()
    stage([attn_line, cot_line])
    attn_line.step()
    all_cot = jnp.concatenate([cot_line.near(k) for k in range(lines)], axis=0)
    grad_mlp = (BRANCH_SCALE * (all_cot.astype(jnp.float32) * live_all)).astype(jnp.bfloat16)
    half_rows = all_rows // 2
    grad_hidden = [
        plain_product(grad_mlp[k * half_rows : (k + 1) * half_rows], down_w) for k in range(2)
    ]
    grad_hidden = stage([attn_line], *grad_hidden)
    own_x = own_tokens.astype(jnp.float32)
    middle = own_x + BRANCH_SCALE * attn_line.total()
    normed_two, inverse_two = norm_parts(middle)

    second_line = walk((normed_two * gain_b).astype(jnp.bfloat16))
    second_line.step()
    stage([second_line])

    def units(second_half, grad_half):
        gate_up = plain_product(second_half, gate_up_w)
        gate_proj = gate_up[:, :unit_cols]
        up_proj = gate_up[:, unit_cols:]
        gate_sig = jax.nn.sigmoid(gate_proj)
        gate_act = gate_proj * gate_sig
        hidden_half = (gate_act * up_proj).astype(jnp.bfloat16)
        grad_gate_b = (
            grad_half * up_proj * gate_sig * (1.0 + gate_proj * (1.0 - gate_sig))
        ).astype(jnp.bfloat16)
        grad_up_b = (grad_half * gate_act).astype(jnp.bfloat16)
        return hidden_half, jnp.concatenate([grad_gate_b, grad_up_b], axis=1)

    near_half = jnp.concatenate([second_line.near(k) for k in range(lines // 2)], axis=0)
    second_line.step()
    hidden_near, grad_near = units(near_half, grad_hidden[0])
    hidden_near, grad_near = stage([second_line], hidden_near, grad_near)
    second_line.step()
    part_near = col_product(grad_near, gate_up_w).astype(jnp.bfloat16)
    (part_near,) = stage([second_line], part_near)
    far_half = jnp.concatenate([second_line.near(k) for k in range(lines // 2, lines)], axis=0)
    hidden_far, grad_far = units(far_half, grad_hidden[1])
    part_far = col_product(grad_far, gate_up_w).astype(jnp.bfloat16)
    hidden_far, grad_far, part_far = lax.optimization_barrier((hidden_far, grad_far, part_far))

    grad_line = add_up(blocks_of(part_near) + blocks_of(part_far))
    grad_line.step()
    second_in = jnp.concatenate([near_half, far_half], axis=0)
    grad_gate_up = jnp.concatenate([grad_near, grad_far], axis=0)
    gate_up_grad = row_product(second_in, grad_gate_up).astype(jnp.bfloat16)
    hidden = jnp.concatenate([hidden_near, hidden_far], axis=0)
    gate_up_grad, hidden = stage([grad_line], gate_up_grad, hidden)
    grad_line.step()
    gate_up_piece = reduce_pair(gate_up_grad)
    down_grad = row_product(grad_mlp, hidden).astype(jnp.bfloat16)
    down_grad, hidden = stage([grad_line], down_grad, hidden)
    grad_line.step()
    down_piece = reduce_pair(down_grad)
    mlp_part = col_product(hidden, down_w).astype(jnp.bfloat16)
    (mlp_part,) = stage([grad_line], mlp_part)
    grad_second = grad_line.total()

    own_dy = own_cot.astype(jnp.float32) * live_own
    grad_middle = own_dy + norm_back(grad_second, normed_two, inverse_two, gain_b)
    attn_grad_line = walk((BRANCH_SCALE * grad_middle).astype(jnp.bfloat16))
    attn_grad_line.step()
    (mlp_part,) = stage([attn_grad_line], mlp_part)
    mlp_line = add_up(blocks_of(mlp_part))
    mlp_line.step()
    attn_grad_line.step()
    stage([attn_grad_line, mlp_line])
    attn_grad_line.step()
    mlp_line.step()
    unit_marks = gain_marks(gate_up_mine, gate_up_piece)
    rest = jnp.zeros((unit_marks.shape[0], -(3 * unit_cols + 2) % LANES), jnp.bfloat16)
    (unit_marks,) = stage([attn_grad_line, mlp_line], unit_marks)
    mlp_line.step()
    grad_attn = jnp.concatenate([attn_grad_line.near(k) for k in range(lines)], axis=0)
    out_grad = row_product(grad_attn, attend).astype(jnp.bfloat16)
    grad_attend = plain_product(grad_attn, out_w).astype(jnp.bfloat16)
    grad_attend, out_grad, gate_up_piece = lax.optimization_barrier(
        (grad_attend, out_grad, gate_up_piece)
    )
    unit_block = jnp.concatenate([gate_up_piece, down_piece, unit_marks, rest], axis=1)
    out_grad, grad_attend, unit_block = stage([mlp_line], out_grad, grad_attend, unit_block)
    out_piece = reduce_pair(out_grad)
    unit_line = walk(unit_block)
    unit_line.step()
    grad_qkv = attend_backward(
        heads, span, order, length.reshape(1), kept, attend, grad_attend, cos_all, sin_all
    )
    qkv_grad = row_product(first_in, grad_qkv).astype(jnp.bfloat16)
    grad_qkv, qkv_grad, out_piece = stage([unit_line], grad_qkv, qkv_grad, out_piece)
    unit_line.step()
    qkv_piece = reduce_pair(qkv_grad)
    first_part = col_product(grad_qkv, qkv_w).astype(jnp.bfloat16)

    first_line = add_up(blocks_of(first_part))
    first_line.step()
    layer_rows = ((middle + BRANCH_SCALE * mlp_line.total()) * live_own).astype(jnp.bfloat16)
    (layer_rows,) = stage([unit_line, first_line], layer_rows)
    unit_line.step()
    first_line.step()
    qkv_marks = gain_marks(qkv_mine, qkv_piece)
    head_block = jnp.concatenate(
        [qkv_piece[:, :head_cols], qkv_marks, qkv_piece[:, head_cols + 2 :], out_piece], axis=1
    )
    (head_block,) = stage([unit_line, first_line], head_block)
    head_line = walk(head_block)
    head_line.step()
    first_line.step()
    own, other, give = line_pieces(unit_line)
    final_gate, final_up, final_down = join_columns(
        core_index, own, other, 3, unit_cols, unit_cols
    )
    final_gain_two = gain_total((own, give), 3 * unit_cols, mlp_gain)
    final_gate, final_up, final_down = stage(
        [first_line, head_line], final_gate, final_up, final_down
    )
    head_line.step()
    grad_first = first_line.total()
    normed_one, inverse_one = norm_parts(own_x)
    grad_rows = grad_middle + norm_back(grad_first, normed_one, inverse_one, gain_a)
    (grad_rows,) = stage([head_line], grad_rows)
    head_line.step()

    def both_slots(own):
        other = lax.ppermute(own, "tensor", swap_pairs())
        return jnp.stack(
            [jnp.where(core == 0, own, other), jnp.where(core == 0, other, own)], axis=0
        )

    layer_out = both_slots(layer_rows)
    grad_tokens = both_slots(grad_rows.astype(jnp.bfloat16)).astype(jnp.float32)
    layer_out, grad_tokens = stage([head_line], layer_out, grad_tokens)
    own, other, give = line_pieces(head_line)
    final_query, final_key, final_value, final_out = join_columns(
        core_index, own, other, 4, pad_cols, head_cols
    )
    final_gain_one = gain_total((own, give), head_cols, attn_gain)
    return (
        layer_out,
        grad_tokens,
        final_gain_one,
        final_query,
        final_key,
        final_value,
        jnp.transpose(final_out),
        final_gain_two,
        final_gate,
        final_up,
        jnp.transpose(final_down),
    )


def heads_of(w_query, cores, lines):
    return w_query.shape[1] * cores // lines


def local(shape, *arrays):
    shards, lines, cores = shape["shard"], shape["ctx"], shape["tensor"]
    tokens, w_query, w_gate = arrays[0], arrays[4], arrays[9]
    fits = (
        cores == 2
        and tokens.shape[0] == cores
        and lines % cores == 0
        and lines == 4
        and (w_query.shape[1] * cores) % (lines * HD) == 0
        and (w_gate.shape[1] * cores) % (lines * cores) == 0
        and w_query.shape[0] % cores == 0
        and -(-heads_of(w_query, cores, lines) // LANES) * LANES >= heads_of(w_query, cores, lines) + 2
    )
    if fits:
        return column_split(shape, *arrays)
    return gather_all(*arrays)


def solution(mesh):
    placed = (
        P("shard", "ctx", None),
        P("shard"),
        P(),
        P("shard"),
        P("shard", "tensor"),
        P("shard", "tensor"),
        P("shard", "tensor"),
        P("tensor", "shard"),
        P("shard"),
        P("shard", "tensor"),
        P("shard", "tensor"),
        P("tensor", "shard"),
        P("shard", "ctx", None),
    )
    return jax.shard_map(
        functools.partial(local, dict(mesh.shape)),
        mesh=mesh,
        in_specs=placed,
        out_specs=(
            P("shard", "ctx", None),
            P("shard", "ctx", None),
            P("shard"),
            P("shard", "tensor"),
            P("shard", "tensor"),
            P("shard", "tensor"),
            P("tensor", "shard"),
            P("shard"),
            P("shard", "tensor"),
            P("shard", "tensor"),
            P("tensor", "shard"),
        ),
        check_vma=False,
    )
```

```python
import functools
import math

import jax
import jax.numpy as jnp
from jax import lax
from jax.experimental import pallas as pl
from jax.experimental.pallas import tpu as pltpu
from jax.sharding import PartitionSpec as P

HD = 64


NORM_EPS = 1e-05
ROPE_BASE = 10000.0
BRANCH_SCALE = 1.4 / math.sqrt(40.0)
CONTRACT_ROWS = (((0,), (0,)), ((), ()))
CONTRACT_COLS = (((1,), (1,)), ((), ()))


def row_product(left_mat, right_mat):
    return lax.dot_general(left_mat, right_mat, CONTRACT_ROWS, preferred_element_type=jnp.float32)


def col_product(left_mat, right_mat):
    return lax.dot_general(left_mat, right_mat, CONTRACT_COLS, preferred_element_type=jnp.float32)


def plain_product(left_mat, right_mat):
    return jnp.dot(left_mat, right_mat, preferred_element_type=jnp.float32)


def rope_tables(positions, head_dim):
    frequency = ROPE_BASE ** (-(jnp.arange(head_dim // 2) * 2).astype(jnp.float32) / head_dim)
    angles = positions.astype(jnp.float32)[:, None] * frequency[None, :]
    return (jnp.cos(angles)[:, None, :], jnp.sin(angles)[:, None, :])


def rotate(values_in, cos_table, sin_table, sign_dir):
    half_dim = values_in.shape[-1] // 2
    lead_part = values_in[..., :half_dim]
    tail_part = values_in[..., half_dim:]
    turned = sin_table * sign_dir
    return jnp.concatenate(
        [lead_part * cos_table - tail_part * turned, tail_part * cos_table + lead_part * turned],
        axis=-1,
    )


def norm_parts(values_in):
    inverse = lax.rsqrt(jnp.mean(values_in * values_in, axis=-1, keepdims=True) + NORM_EPS)
    return (values_in * inverse, inverse)


def norm_back(grad_in, normed, inverse, gain_vec):
    scaled = grad_in * gain_vec
    return inverse * (scaled - normed * jnp.mean(scaled * normed, axis=-1, keepdims=True))


def gather_all(
    tokens,
    lengths,
    span_order,
    attn_gain,
    w_query,
    w_key,
    w_value,
    w_out,
    mlp_gain,
    w_gate,
    w_up,
    w_down,
    cotangent,
):
    slot_count, row_count, width = tokens.shape
    local_heads = w_query.shape[1] // HD
    span_rows = row_count // 2
    offsets = jnp.arange(span_rows, dtype=jnp.int32)
    all_pos = (span_order[:, None] * span_rows + offsets[None, :]).reshape(-1)
    own_pos = lax.dynamic_slice_in_dim(all_pos, lax.axis_index("ctx") * row_count, row_count)
    cos_own, sin_own = rope_tables(own_pos, HD)
    causal = all_pos[None, :] <= own_pos[:, None]
    score_scale = HD ** (-0.5)

    def masked_scores(query_b, key_all, allowed):
        raw_scores = (
            jnp.einsum("qhd,khd->hqk", query_b, key_all, preferred_element_type=jnp.float32)
            * score_scale
        )
        return jnp.where(allowed[None], raw_scores, -1e30)

    out_blocks = []
    grad_blocks = []
    totals = None
    for slot_index in range(slot_count):
        length = lengths[slot_index]
        gain_one = lax.all_gather(attn_gain, "shard", axis=0, tiled=True)
        query_w = lax.all_gather(w_query, "shard", axis=0, tiled=True)
        key_w = lax.all_gather(w_key, "shard", axis=0, tiled=True)
        value_w = lax.all_gather(w_value, "shard", axis=0, tiled=True)
        out_w = lax.all_gather(w_out, "shard", axis=1, tiled=True)
        gain_two = lax.all_gather(mlp_gain, "shard", axis=0, tiled=True)
        gate_w = lax.all_gather(w_gate, "shard", axis=0, tiled=True)
        up_w = lax.all_gather(w_up, "shard", axis=0, tiled=True)
        down_w = lax.all_gather(w_down, "shard", axis=1, tiled=True)
        live_mask = (own_pos < length).astype(jnp.float32)[:, None]
        run_allowed = causal & (all_pos < length)[None, :]
        gain_a = gain_one.astype(jnp.float32)
        gain_b = gain_two.astype(jnp.float32)
        residual_in = tokens[slot_index].astype(jnp.float32)
        normed_one, inverse_one = norm_parts(residual_in)
        first_in = (normed_one * gain_a).astype(jnp.bfloat16)
        query_f = plain_product(first_in, query_w).reshape(row_count, local_heads, HD)
        key_f = plain_product(first_in, key_w).reshape(row_count, local_heads, HD)
        value_b = plain_product(first_in, value_w).astype(jnp.bfloat16)
        run_query_b = rotate(query_f, cos_own, sin_own, 1.0).astype(jnp.bfloat16)
        key_b = rotate(key_f, cos_own, sin_own, 1.0).astype(jnp.bfloat16).reshape(row_count, -1)
        run_key_all = lax.all_gather(key_b, "ctx", axis=0, tiled=True)
        value_all = lax.all_gather(value_b, "ctx", axis=0, tiled=True)
        run_key_all = run_key_all.reshape(-1, local_heads, HD)
        value_all = value_all.reshape(-1, local_heads, HD)
        scores = masked_scores(run_query_b, run_key_all, run_allowed)
        row_top = jnp.max(scores, axis=-1, keepdims=True)
        weights = jnp.exp(scores - row_top)
        row_total = jnp.sum(weights, axis=-1, keepdims=True)
        log_total = row_top + jnp.log(row_total)
        probs_low = (weights / row_total).astype(jnp.bfloat16)
        attend = (
            jnp.einsum("hqk,khd->qhd", probs_low, value_all, preferred_element_type=jnp.float32)
            .astype(jnp.bfloat16)
            .reshape(row_count, -1)
        )
        attn_out = lax.psum(plain_product(attend, out_w), "tensor")
        middle = residual_in + BRANCH_SCALE * attn_out
        normed_two, inverse_two = norm_parts(middle)
        second_in = (normed_two * gain_b).astype(jnp.bfloat16)
        gate_proj = plain_product(second_in, gate_w)
        up_proj = plain_product(second_in, up_w)
        gate_sig = jax.nn.sigmoid(gate_proj)
        gate_act = gate_proj * gate_sig
        hidden = (gate_act * up_proj).astype(jnp.bfloat16)
        mlp_out = lax.psum(plain_product(hidden, down_w).astype(jnp.bfloat16), "tensor").astype(
            jnp.float32
        )
        layer_rows = ((middle + BRANCH_SCALE * mlp_out) * live_mask).astype(jnp.bfloat16)
        grad_y = cotangent[slot_index].astype(jnp.float32) * live_mask
        grad_mlp = (BRANCH_SCALE * grad_y).astype(jnp.bfloat16)
        grad_down_w = row_product(hidden, grad_mlp)
        grad_hidden = col_product(grad_mlp, down_w)
        grad_gate_b = (
            grad_hidden * up_proj * gate_sig * (1.0 + gate_proj * (1.0 - gate_sig))
        ).astype(jnp.bfloat16)
        grad_up_b = (grad_hidden * gate_act).astype(jnp.bfloat16)
        grad_gate_w = row_product(second_in, grad_gate_b)
        grad_up_w = row_product(second_in, grad_up_b)
        grad_second = lax.psum(
            col_product(grad_gate_b, gate_w) + col_product(grad_up_b, up_w), "tensor"
        )
        grad_gain_two = jnp.sum(grad_second * normed_two, axis=0)
        grad_middle = grad_y + norm_back(grad_second, normed_two, inverse_two, gain_b)
        grad_attn = (BRANCH_SCALE * grad_middle).astype(jnp.bfloat16)
        grad_out_w = row_product(attend, grad_attn)
        grad_attend = (
            col_product(grad_attn, out_w).astype(jnp.bfloat16).reshape(row_count, local_heads, HD)
        )
        probs_new = jnp.exp(masked_scores(run_query_b, run_key_all, run_allowed) - log_total)
        grad_probs = jnp.einsum(
            "qhd,khd->hqk", grad_attend, value_all, preferred_element_type=jnp.float32
        )
        grad_scores = (
            probs_new * (grad_probs - jnp.sum(probs_new * grad_probs, axis=-1, keepdims=True))
        ).astype(jnp.bfloat16)
        grad_query_f = (
            jnp.einsum("hqk,khd->qhd", grad_scores, run_key_all, preferred_element_type=jnp.float32)
            * score_scale
        )
        grad_key_all = (
            jnp.einsum("hqk,qhd->khd", grad_scores, run_query_b, preferred_element_type=jnp.float32)
            * score_scale
        )
        grad_value_all = jnp.einsum(
            "hqk,qhd->khd",
            probs_new.astype(jnp.bfloat16),
            grad_attend,
            preferred_element_type=jnp.float32,
        )
        grad_key_own = lax.psum_scatter(
            grad_key_all.reshape(grad_key_all.shape[0], -1), "ctx", scatter_dimension=0, tiled=True
        )
        grad_value_own = lax.psum_scatter(
            grad_value_all.reshape(grad_value_all.shape[0], -1),
            "ctx",
            scatter_dimension=0,
            tiled=True,
        )
        grad_query_b = (
            rotate(grad_query_f, cos_own, sin_own, -1.0).astype(jnp.bfloat16).reshape(row_count, -1)
        )
        grad_key_b = (
            rotate(grad_key_own.reshape(row_count, local_heads, HD), cos_own, sin_own, -1.0)
            .astype(jnp.bfloat16)
            .reshape(row_count, -1)
        )
        grad_value_b = grad_value_own.astype(jnp.bfloat16)
        grad_query_w = row_product(first_in, grad_query_b)
        grad_key_w = row_product(first_in, grad_key_b)
        grad_value_w = row_product(first_in, grad_value_b)
        grad_first = lax.psum(
            (
                col_product(grad_query_b, query_w)
                + col_product(grad_key_b, key_w)
                + col_product(grad_value_b, value_w)
            ).astype(jnp.bfloat16),
            "tensor",
        ).astype(jnp.float32)
        grad_gain_one = jnp.sum(grad_first * normed_one, axis=0)
        grad_rows = grad_middle + norm_back(grad_first, normed_one, inverse_one, gain_a)
        slot_grads = (
            grad_gain_one,
            grad_query_w,
            grad_key_w,
            grad_value_w,
            grad_out_w,
            grad_gain_two,
            grad_gate_w,
            grad_up_w,
            grad_down_w,
        )
        layer_rows, grad_rows, slot_grads = (layer_rows, grad_rows, slot_grads)
        out_blocks.append(layer_rows)
        grad_blocks.append(grad_rows)
        if totals is None:
            totals = slot_grads
        else:
            totals = tuple(
                (left_val + right_val for left_val, right_val in zip(totals, slot_grads))
            )
    (
        sum_gain_one,
        sum_query,
        sum_key,
        sum_value,
        sum_out,
        sum_gain_two,
        sum_gate,
        sum_up,
        sum_down,
    ) = totals
    spread = (
        lax.psum_scatter(sum_gain_one, ("shard", "ctx"), scatter_dimension=0, tiled=True),
        lax.psum_scatter(sum_query, ("shard", "ctx"), scatter_dimension=0, tiled=True),
        lax.psum_scatter(sum_key, ("shard", "ctx"), scatter_dimension=0, tiled=True),
        lax.psum_scatter(sum_value, ("shard", "ctx"), scatter_dimension=0, tiled=True),
        lax.psum_scatter(sum_out, ("shard", "ctx"), scatter_dimension=1, tiled=True),
        lax.psum_scatter(sum_gain_two, ("shard", "ctx"), scatter_dimension=0, tiled=True),
        lax.psum_scatter(sum_gate, ("shard", "ctx"), scatter_dimension=0, tiled=True),
        lax.psum_scatter(sum_up, ("shard", "ctx"), scatter_dimension=0, tiled=True),
        lax.psum_scatter(sum_down, ("shard", "ctx"), scatter_dimension=1, tiled=True),
    )
    (
        part_gain_one,
        part_query,
        part_key,
        part_value,
        part_out,
        part_gain_two,
        part_gate,
        part_up,
        part_down,
    ) = spread
    final = (
        lax.all_gather(part_gain_one.astype(jnp.bfloat16), "ctx", axis=0, tiled=True).astype(
            part_gain_one.dtype
        ),
        lax.all_gather(part_query.astype(jnp.bfloat16), "ctx", axis=0, tiled=True).astype(
            part_query.dtype
        ),
        lax.all_gather(part_key.astype(jnp.bfloat16), "ctx", axis=0, tiled=True).astype(
            part_key.dtype
        ),
        lax.all_gather(part_value.astype(jnp.bfloat16), "ctx", axis=0, tiled=True).astype(
            part_value.dtype
        ),
        lax.all_gather(part_out.astype(jnp.bfloat16), "ctx", axis=1, tiled=True).astype(
            part_out.dtype
        ),
        lax.all_gather(part_gain_two.astype(jnp.bfloat16), "ctx", axis=0, tiled=True).astype(
            part_gain_two.dtype
        ),
        lax.all_gather(part_gate.astype(jnp.bfloat16), "ctx", axis=0, tiled=True).astype(
            part_gate.dtype
        ),
        lax.all_gather(part_up.astype(jnp.bfloat16), "ctx", axis=0, tiled=True).astype(
            part_up.dtype
        ),
        lax.all_gather(part_down.astype(jnp.bfloat16), "ctx", axis=1, tiled=True).astype(
            part_down.dtype
        ),
    )
    layer_out = jnp.stack(out_blocks, axis=0)
    grad_tokens = jnp.stack(grad_blocks, axis=0)
    return (
        layer_out,
        grad_tokens,
        final[0],
        final[1],
        final[2],
        final[3],
        final[4],
        final[5],
        final[6],
        final[7],
        final[8],
    )


LANES = 128
QUERY_TILE = 256


def lane_partner(values_in):
    lane = lax.broadcasted_iota(jnp.int32, values_in.shape, 1) % HD
    return jnp.where(
        lane < HD // 2,
        -pltpu.roll(values_in, LANES - HD // 2, 1),
        pltpu.roll(values_in, HD // 2, 1),
    )


def head_lanes(values_in, head):
    lane = lax.broadcasted_iota(jnp.int32, values_in.shape, 1)
    return jnp.where(lane // HD == head, values_in, jnp.zeros_like(values_in))


def tile_allowed(rows, start, length):
    key = lax.broadcasted_iota(jnp.int32, (rows, QUERY_TILE), 0)
    query = lax.broadcasted_iota(jnp.int32, (rows, QUERY_TILE), 1) + start
    return (key <= query) & (key < length)


def attend_kernel(
    heads, span, order, length, q_near, k_near, v_near, q_far, k_far, v_far, cos, sin,
    out, q_out, k_out, v_out, log_out, q_sort, k_sort, v_sort, turned,
):
    rows = q_out.shape[0]
    pair = pl.program_id(0)
    for block in range(rows // span):
        place = pl.ds(pl.multiple_of(order[block] * span, span), span)
        start = block * span
        near = start < q_near.shape[0]
        start -= 0 if near else q_near.shape[0]
        stored = slice(start, start + span)
        q_sort[place, :] = (q_near if near else q_far)[stored, :]
        k_sort[place, :] = (k_near if near else k_far)[stored, :]
        v_sort[place, :] = (v_near if near else v_far)[stored, :]
    queries = q_sort[...]
    keys = k_sort[...]
    q_out[...] = (queries * cos[...] + lane_partner(queries) * sin[...]).astype(jnp.bfloat16)
    k_out[...] = (keys * cos[...] + lane_partner(keys) * sin[...]).astype(jnp.bfloat16)
    v_out[...] = v_sort[...].astype(jnp.bfloat16)
    values_t = jnp.transpose(v_out[...])
    turned[...] = jnp.zeros_like(turned)
    log_out[...] = jnp.zeros_like(log_out)
    for head in range(LANES // HD):

        @pl.when(pair * (LANES // HD) + head < heads)
        def _():
            for start in range(0, rows, QUERY_TILE):
                used = start + QUERY_TILE
                query = head_lanes(q_out[start:used, :] * (HD**-0.5), head).astype(jnp.bfloat16)
                scores = col_product(k_out[:used, :], query)
                scores = jnp.where(tile_allowed(used, start, length[0]), scores, -1e30)
                top = jnp.max(scores, axis=0, keepdims=True)
                weights = jnp.exp(scores - top)
                total = jnp.sum(weights, axis=0, keepdims=True)
                probs = (weights * (1.0 / total)).astype(jnp.bfloat16)
                turned[head * HD : (head + 1) * HD, start:used] = plain_product(
                    values_t[head * HD : (head + 1) * HD, :used], probs
                )
                log_out[0, head : head + 1, start:used] = top + jnp.log(total)

    q_sort[...] = jnp.transpose(turned[...])
    for block in range(rows // span):
        place = pl.ds(pl.multiple_of(order[block] * span, span), span)
        out[block * span : (block + 1) * span, :] = q_sort[place, :].astype(jnp.bfloat16)


def attend_back_kernel(
    heads, span, order, length, q_in, k_in, v_in, log_in, o_in, do_in, cos, sin, grads,
    o_sort, do_sort, dq_turned, dq_sum, dk_sum, dv_sum, piece, sems,
):
    rows = q_in.shape[0]
    pair = pl.program_id(0)
    pairs = pl.num_programs(0)
    for block in range(rows // span):
        place = pl.ds(pl.multiple_of(order[block] * span, span), span)
        stored = slice(block * span, (block + 1) * span)
        o_sort[place, :] = o_in[stored, :].astype(jnp.float32)
        do_sort[place, :] = do_in[stored, :].astype(jnp.float32)
    means_t = jnp.transpose(o_sort[...] * do_sort[...])
    keys_t = jnp.transpose(k_in[...])
    dq_turned[...] = jnp.zeros_like(dq_turned)
    dk_sum[...] = jnp.zeros_like(dk_sum)
    dv_sum[...] = jnp.zeros_like(dv_sum)
    for head in range(LANES // HD):

        @pl.when(pair * (LANES // HD) + head < heads)
        def _():
            inner = jnp.sum(means_t[head * HD : (head + 1) * HD, :], axis=0, keepdims=True)
            for start in range(0, rows, QUERY_TILE):
                used = start + QUERY_TILE
                query = head_lanes(q_in[start:used, :] * (HD**-0.5), head).astype(jnp.bfloat16)
                grad_o = head_lanes(do_sort[start:used, :], head).astype(jnp.bfloat16)
                scores = col_product(k_in[:used, :], query)
                probs = jnp.where(
                    tile_allowed(used, start, length[0]),
                    jnp.exp(scores - log_in[0, head : head + 1, start:used]),
                    0.0,
                )
                grad_p = col_product(v_in[:used, :], grad_o)
                grad_s = (probs * (grad_p - inner[:, start:used])).astype(jnp.bfloat16)
                dv_sum[:used, :] += plain_product(probs.astype(jnp.bfloat16), grad_o)
                dk_sum[:used, :] += plain_product(grad_s, query)
                dq_turned[head * HD : (head + 1) * HD, start:used] = plain_product(
                    keys_t[head * HD : (head + 1) * HD, :used], grad_s
                )

    grad_q = jnp.transpose(dq_turned[...]) * (HD**-0.5)
    grad_k = dk_sum[...]
    dq_sum[...] = grad_q * cos[...] - lane_partner(grad_q) * sin[...]
    dk_sum[...] = grad_k * cos[...] - lane_partner(grad_k) * sin[...]
    copies = []
    for which, total in enumerate((dq_sum, dk_sum, dv_sum)):
        for block in range(rows // span):
            place = pl.ds(pl.multiple_of(order[block] * span, span), span)
            piece[which, block * span : (block + 1) * span, :] = total[place, :].astype(jnp.bfloat16)
        column = pl.multiple_of((which * pairs + pair) * LANES, LANES)
        copies.append(
            pltpu.make_async_copy(
                piece.at[which], grads.at[:, pl.ds(column, LANES)], sems.at[which]
            )
        )
        copies[-1].start()
    for copy in copies:
        copy.wait()


def attend_forward(heads, span, order, length, near, far, cos, sin):
    rows = near.shape[0] + far.shape[0]
    pairs = near.shape[1] // (3 * LANES)
    column = lambda v, offset: pl.BlockSpec((v.shape[0], LANES), lambda i, *_: (0, offset + i))
    fixed = pl.BlockSpec((rows, LANES), lambda i, *_: (0, 0))
    flat = jax.ShapeDtypeStruct((rows, pairs * LANES), jnp.bfloat16)
    return pl.pallas_call(
        functools.partial(attend_kernel, heads, span),
        grid_spec=pltpu.PrefetchScalarGridSpec(
            num_scalar_prefetch=2,
            grid=(pairs,),
            in_specs=[column(v, k * pairs) for v in (near, far) for k in range(3)] + [fixed, fixed],
            out_specs=[column(cos, 0)] * 4 + [pl.BlockSpec((1, 8, rows), lambda i, *_: (i, 0, 0))],
            scratch_shapes=[pltpu.VMEM((rows, LANES), jnp.float32)] * 3
            + [pltpu.VMEM((LANES, rows), jnp.float32)],
        ),
        out_shape=[flat] * 4 + [jax.ShapeDtypeStruct((pairs, 8, rows), jnp.float32)],
        compiler_params=pltpu.CompilerParams(vmem_limit_bytes=40 << 20),
        cost_estimate=pl.CostEstimate(
            flops=4 * heads * rows * rows * HD,
            bytes_accessed=rows * pairs * LANES * 24,
            transcendentals=heads * rows * rows,
        ),
        name="attend",
    )(order, length, near, near, near, far, far, far, cos, sin)


def attend_backward(heads, span, order, length, kept, attend, grad_attend, cos, sin):
    queries, keys, values, logs = kept
    rows = queries.shape[0]
    pairs = queries.shape[1] // LANES
    column = pl.BlockSpec((rows, LANES), lambda i, *_: (0, i))
    fixed = pl.BlockSpec((rows, LANES), lambda i, *_: (0, 0))
    return pl.pallas_call(
        functools.partial(attend_back_kernel, heads, span),
        grid_spec=pltpu.PrefetchScalarGridSpec(
            num_scalar_prefetch=2,
            grid=(pairs,),
            in_specs=[column] * 3
            + [pl.BlockSpec((1, 8, rows), lambda i, *_: (i, 0, 0)), column, column, fixed, fixed],
            out_specs=pl.BlockSpec(memory_space=pl.ANY),
            scratch_shapes=[pltpu.VMEM((rows, LANES), jnp.float32)] * 2
            + [pltpu.VMEM((LANES, rows), jnp.float32)]
            + [pltpu.VMEM((rows, LANES), jnp.float32)] * 3
            + [pltpu.VMEM((3, rows, LANES), jnp.bfloat16), pltpu.SemaphoreType.DMA((3,))],
        ),
        out_shape=jax.ShapeDtypeStruct((rows, 3 * pairs * LANES), jnp.bfloat16),
        compiler_params=pltpu.CompilerParams(vmem_limit_bytes=40 << 20),
        cost_estimate=pl.CostEstimate(
            flops=10 * heads * rows * rows * HD,
            bytes_accessed=rows * pairs * LANES * 16,
            transcendentals=heads * rows * rows,
        ),
        name="attend_back",
    )(order, length, queries, keys, values, logs, attend, grad_attend, cos, sin)


def columns_kernel(count, each, used, core, own, other, *outs):
    mine = pl.program_id(0) == core[0]
    for k in range(own.shape[0]):
        rows = jnp.where(mine, own[k].astype(jnp.float32), other[k].astype(jnp.float32))
        for j in range(count):
            outs[j][:, k * used : (k + 1) * used] = rows[:, j * each : j * each + used]


def join_columns(core, own, other, count, each, used):
    pieces, rows, cols = own.shape
    tile = rows // 3 if rows % 48 == 0 else rows
    taken = pl.BlockSpec((pieces, tile, cols), lambda c, r, *_: (0, r, 0))
    given = pl.BlockSpec((tile, pieces * used), lambda c, r, *_: (c * (rows // tile) + r, 0))
    return pl.pallas_call(
        functools.partial(columns_kernel, count, each, used),
        grid_spec=pltpu.PrefetchScalarGridSpec(
            num_scalar_prefetch=1,
            grid=(2, rows // tile),
            in_specs=[taken, taken],
            out_specs=[given] * count,
        ),
        out_shape=[jax.ShapeDtypeStruct((2 * rows, pieces * used), jnp.float32)] * count,
        compiler_params=pltpu.CompilerParams(vmem_limit_bytes=40 << 20),
        cost_estimate=pl.CostEstimate(
            flops=0, bytes_accessed=8 * pieces * rows * (cols + used * count), transcendentals=0
        ),
        name="join_columns",
    )(core, own, other)


def swap_pairs():
    return [(0, 1), (1, 0)]


class LineGather:
    def __init__(self, block, axis, size):
        self.axis, self.size = axis, size
        self.ups, self.downs = [block], [block]

    def step(self):
        done = len(self.ups)
        up_pairs = [(i, i + 1) for i in range(done - 1, self.size - 1)]
        down_pairs = [(i, i - 1) for i in range(1, self.size - done + 1)]
        self.ups.append(lax.ppermute(self.ups[-1], self.axis, up_pairs))
        self.downs.append(lax.ppermute(self.downs[-1], self.axis, down_pairs))

    def held(self):
        return (self.ups[-1], self.downs[-1])

    def hold(self, values):
        self.ups[-1], self.downs[-1] = values

    def near(self, mask):
        place = lax.axis_index(self.axis)
        found = None
        for here in range(self.size):
            there = here ^ mask
            block = self.ups[here - there] if there < here else self.downs[there - here]
            found = block if found is None else jnp.where(place == here, block, found)
        return found

    def at(self, target):
        gap = lax.axis_index(self.axis) - target
        found = self.ups[0]
        for hops in range(1, self.size):
            found = jnp.where(gap == hops, self.ups[hops], found)
            found = jnp.where(gap == -hops, self.downs[hops], found)
        return found


class LineScatter:
    def __init__(self, parts, axis, size):
        self.axis, self.size, self.parts = axis, size, parts
        self.done = 0
        self.up = self.down = None

    def part(self, offsets):
        place = lax.axis_index(self.axis)
        masks = {}
        for here, there in offsets:
            masks.setdefault(here ^ there, []).append(here)
        found = None
        for mask, places in sorted(masks.items()):
            if found is None:
                found = self.parts[mask]
                continue
            chosen = functools.reduce(jnp.logical_or, [place == here for here in places])
            found = jnp.where(chosen, self.parts[mask], found)
        return found

    def step(self):
        self.done += 1
        gap = self.size - self.done
        ups = [(i, i + gap) for i in range(self.done)]
        downs = [(i, i - gap) for i in range(gap, self.size)]
        up, down = self.part(ups), self.part(downs)
        if self.done > 1:
            up = (up.astype(jnp.float32) + self.up.astype(jnp.float32)).astype(jnp.bfloat16)
            down = (down.astype(jnp.float32) + self.down.astype(jnp.float32)).astype(jnp.bfloat16)
        self.up = lax.ppermute(up, self.axis, [(i, i + 1) for i, _ in ups])
        self.down = lax.ppermute(down, self.axis, [(i, i - 1) for i, _ in downs])

    def held(self):
        return (self.up, self.down)

    def hold(self, values):
        self.up, self.down = values

    def total(self):
        return (
            self.parts[0].astype(jnp.float32)
            + self.up.astype(jnp.float32)
            + self.down.astype(jnp.float32)
        )


def stage(chains, *arrays):
    held = [chain.held() for chain in chains]
    held, arrays = lax.optimization_barrier((held, arrays))
    for chain, values in zip(chains, held):
        chain.hold(values)
    return arrays


def column_split(
    shape,
    tokens,
    lengths,
    span_order,
    attn_gain,
    w_query,
    w_key,
    w_value,
    w_out,
    mlp_gain,
    w_gate,
    w_up,
    w_down,
    cotangent,
):
    shards, lines, cores = shape["shard"], shape["ctx"], shape["tensor"]
    line = lax.axis_index("ctx")
    core = lax.axis_index("tensor")
    per_half = lines // cores
    owner = core == line // per_half
    sub = line % per_half
    slot_count, row_count, width = tokens.shape
    all_rows = row_count * lines
    heads = w_query.shape[1] * cores // lines // HD
    head_cols = heads * HD
    pad_cols = -(-head_cols // LANES) * LANES
    widen = lambda v, dim: jnp.pad(v, [(0, pad_cols - head_cols if d == dim else 0) for d in (0, 1)])
    unit_cols = w_gate.shape[1] * cores // lines

    def column_piece(weights, shape_up=lambda v: v):
        cut = [
            shape_up(
                lax.dynamic_slice_in_dim(w, sub * (w.shape[1] // per_half), w.shape[1] // per_half, 1)
            )
            for w in weights
        ]
        return jnp.concatenate(cut, axis=1) if len(cut) > 1 else cut[0]

    def turned_piece(w):
        rows = w.shape[0] // per_half
        return jnp.transpose(lax.dynamic_slice_in_dim(w, sub * rows, rows, 0))

    def to_pair(piece):
        rows = piece.shape[0] // cores
        keep = lax.dynamic_slice_in_dim(piece, core * rows, rows, 0)
        give = lax.dynamic_slice_in_dim(piece, (1 - core) * rows, rows, 0)
        got = lax.ppermute(give, "tensor", swap_pairs())
        return jnp.where(owner, keep, got)

    def gather_pair(mine):
        return lax.all_gather(mine, ("shard", "tensor"), axis=0, tiled=True)

    def reduce_pair(grad):
        return lax.psum_scatter(grad, ("shard", "tensor"), scatter_dimension=0, tiled=True)

    def gain_marks(weights, piece):
        used = weights.shape[1]
        total = jnp.sum(
            weights.astype(jnp.float32) * piece[:, :used].astype(jnp.float32), axis=1, keepdims=True
        )
        high = total.astype(jnp.bfloat16)
        low = (total - high.astype(jnp.float32)).astype(jnp.bfloat16)
        return jnp.concatenate([high, low], axis=1)

    def line_pieces(chain):
        half = lambda c: jnp.stack([chain.at(c * per_half + k) for k in range(per_half)])
        give = half(1 - core)
        return half(core), lax.ppermute(give, "tensor", swap_pairs()), give

    def gain_total(found, column, gain):
        marks = [pieces[:, :, column : column + 2].astype(jnp.float32) for pieces in found]
        own = jnp.sum(marks[0] + marks[1], axis=(0, 2))
        other = lax.ppermute(own, "tensor", swap_pairs())
        total = jnp.concatenate(
            [jnp.where(core == 0, own, other), jnp.where(core == 0, other, own)]
        )
        return total / gain.astype(jnp.float32)

    def walk(block):
        return LineGather(block, "ctx", lines)

    def add_up(parts):
        return LineScatter(parts, "ctx", lines)

    def blocks_of(v):
        v = v.astype(jnp.bfloat16)
        return [v[k * row_count : (k + 1) * row_count] for k in range(v.shape[0] // row_count)]

    length = lengths[core]
    offsets = jnp.arange(row_count // 2, dtype=jnp.int32)
    stored_pos = (span_order[:, None] * (row_count // 2) + offsets[None, :]).reshape(lines, row_count)
    ring_pos = stored_pos[line ^ jnp.arange(lines)].reshape(-1)
    own_pos = ring_pos[:row_count]
    span = row_count // 2
    order = ring_pos[::span] // span
    frequency = ROPE_BASE ** (-(jnp.arange(HD // 2) * 2).astype(jnp.float32) / HD)
    angles = jnp.arange(all_rows, dtype=jnp.float32)[:, None] * jnp.tile(frequency, 2 * LANES // HD)
    cos_all, sin_all = jnp.cos(angles), jnp.sin(angles)
    live_all = (ring_pos < length).astype(jnp.float32)[:, None]
    live_own = live_all[:row_count]
    core_index = core.astype(jnp.int32).reshape(1)
    own_tokens = lax.dynamic_index_in_dim(tokens, core, 0, keepdims=False)
    own_cot = lax.dynamic_index_in_dim(cotangent, core, 0, keepdims=False)

    own_tokens, w_query, w_key, w_value = lax.optimization_barrier(
        (own_tokens, w_query, w_key, w_value)
    )
    tokens_line = walk(own_tokens)
    tokens_line.step()
    qkv_mine = to_pair(column_piece([w_query, w_key, w_value], lambda v: widen(v, 1)))
    qkv_w = gather_pair(qkv_mine)
    w_out, w_down, gain_pair = stage(
        [tokens_line], w_out, w_down, jnp.stack([attn_gain, mlp_gain])
    )
    tokens_line.step()
    gains = lax.all_gather(gain_pair, "shard", axis=1, tiled=True)
    gain_a = gains[0].astype(jnp.float32)
    gain_b = gains[1].astype(jnp.float32)
    out_mine = to_pair(widen(turned_piece(w_out), 1))
    down_mine = to_pair(turned_piece(w_down))
    gain_a, gain_b, out_mine, own_cot, cos_all, sin_all, order = stage(
        [tokens_line], gain_a, gain_b, out_mine, own_cot, cos_all, sin_all, order
    )
    tokens_line.step()
    out_w = gather_pair(out_mine)

    def first_rows(masks):
        rows = jnp.concatenate([tokens_line.near(k) for k in masks], axis=0)
        return (norm_parts(rows.astype(jnp.float32))[0] * gain_a).astype(jnp.bfloat16)

    first_near = first_rows(range(lines // 2))
    qkv_near = plain_product(first_near, qkv_w)
    own_cot, down_mine, qkv_near = stage([tokens_line], own_cot, down_mine, qkv_near)
    down_w = gather_pair(down_mine)

    cot_line = walk(own_cot)
    cot_line.step()
    first_far = first_rows(range(lines // 2, lines))
    qkv_far = plain_product(first_far, qkv_w)
    first_in = jnp.concatenate([first_near, first_far], axis=0)
    attend, *kept = attend_forward(
        heads, span, order, length.reshape(1), qkv_near, qkv_far, cos_all, sin_all
    )
    attn_part = col_product(attend, out_w).astype(jnp.bfloat16)
    attn_part, w_gate, w_up = stage([cot_line], attn_part, w_gate, w_up)
    gate_up_mine = to_pair(column_piece([w_gate, w_up]))
    gate_up_w = gather_pair(gate_up_mine)

    attn_line = add_up(blocks_of(attn_part))
    attn_line.step()
    cot_line.step()
    stage([attn_line, cot_line])
    attn_line.step()
    cot_line.step()
    stage([attn_line, cot_line])
    attn_line.step()
    all_cot = jnp.concatenate([cot_line.near(k) for k in range(lines)], axis=0)
    grad_mlp = (BRANCH_SCALE * (all_cot.astype(jnp.float32) * live_all)).astype(jnp.bfloat16)
    half_rows = all_rows // 2
    grad_hidden = [
        plain_product(grad_mlp[k * half_rows : (k + 1) * half_rows], down_w) for k in range(2)
    ]
    grad_hidden = stage([attn_line], *grad_hidden)
    own_x = own_tokens.astype(jnp.float32)
    middle = own_x + BRANCH_SCALE * attn_line.total()
    normed_two, inverse_two = norm_parts(middle)

    second_line = walk((normed_two * gain_b).astype(jnp.bfloat16))
    second_line.step()
    stage([second_line])

    def units(second_half, grad_half):
        gate_up = plain_product(second_half, gate_up_w)
        gate_proj = gate_up[:, :unit_cols]
        up_proj = gate_up[:, unit_cols:]
        gate_sig = jax.nn.sigmoid(gate_proj)
        gate_act = gate_proj * gate_sig
        hidden_half = (gate_act * up_proj).astype(jnp.bfloat16)
        grad_gate_b = (
            grad_half * up_proj * gate_sig * (1.0 + gate_proj * (1.0 - gate_sig))
        ).astype(jnp.bfloat16)
        grad_up_b = (grad_half * gate_act).astype(jnp.bfloat16)
        return hidden_half, jnp.concatenate([grad_gate_b, grad_up_b], axis=1)

    near_half = jnp.concatenate([second_line.near(k) for k in range(lines // 2)], axis=0)
    second_line.step()
    hidden_near, grad_near = units(near_half, grad_hidden[0])
    hidden_near, grad_near = stage([second_line], hidden_near, grad_near)
    second_line.step()
    part_near = col_product(grad_near, gate_up_w).astype(jnp.bfloat16)
    (part_near,) = stage([second_line], part_near)
    far_half = jnp.concatenate([second_line.near(k) for k in range(lines // 2, lines)], axis=0)
    hidden_far, grad_far = units(far_half, grad_hidden[1])
    part_far = col_product(grad_far, gate_up_w).astype(jnp.bfloat16)
    hidden_far, grad_far, part_far = lax.optimization_barrier((hidden_far, grad_far, part_far))

    grad_line = add_up(blocks_of(part_near) + blocks_of(part_far))
    grad_line.step()
    second_in = jnp.concatenate([near_half, far_half], axis=0)
    grad_gate_up = jnp.concatenate([grad_near, grad_far], axis=0)
    gate_up_grad = row_product(second_in, grad_gate_up).astype(jnp.bfloat16)
    hidden = jnp.concatenate([hidden_near, hidden_far], axis=0)
    gate_up_grad, hidden = stage([grad_line], gate_up_grad, hidden)
    grad_line.step()
    gate_up_piece = reduce_pair(gate_up_grad)
    down_grad = row_product(grad_mlp, hidden).astype(jnp.bfloat16)
    down_grad, hidden = stage([grad_line], down_grad, hidden)
    grad_line.step()
    down_piece = reduce_pair(down_grad)
    mlp_part = col_product(hidden, down_w).astype(jnp.bfloat16)
    (mlp_part,) = stage([grad_line], mlp_part)
    grad_second = grad_line.total()

    own_dy = own_cot.astype(jnp.float32) * live_own
    grad_middle = own_dy + norm_back(grad_second, normed_two, inverse_two, gain_b)
    attn_grad_line = walk((BRANCH_SCALE * grad_middle).astype(jnp.bfloat16))
    attn_grad_line.step()
    (mlp_part,) = stage([attn_grad_line], mlp_part)
    mlp_line = add_up(blocks_of(mlp_part))
    mlp_line.step()
    attn_grad_line.step()
    stage([attn_grad_line, mlp_line])
    attn_grad_line.step()
    mlp_line.step()
    unit_marks = gain_marks(gate_up_mine, gate_up_piece)
    rest = jnp.zeros((unit_marks.shape[0], -(3 * unit_cols + 2) % LANES), jnp.bfloat16)
    (unit_marks,) = stage([attn_grad_line, mlp_line], unit_marks)
    mlp_line.step()
    grad_attn = jnp.concatenate([attn_grad_line.near(k) for k in range(lines)], axis=0)
    out_grad = row_product(grad_attn, attend).astype(jnp.bfloat16)
    grad_attend = plain_product(grad_attn, out_w).astype(jnp.bfloat16)
    grad_attend, out_grad, gate_up_piece = lax.optimization_barrier(
        (grad_attend, out_grad, gate_up_piece)
    )
    unit_block = jnp.concatenate([gate_up_piece, down_piece, unit_marks, rest], axis=1)
    out_grad, grad_attend, unit_block = stage([mlp_line], out_grad, grad_attend, unit_block)
    out_piece = reduce_pair(out_grad)
    unit_line = walk(unit_block)
    unit_line.step()
    grad_qkv = attend_backward(
        heads, span, order, length.reshape(1), kept, attend, grad_attend, cos_all, sin_all
    )
    qkv_grad = row_product(first_in, grad_qkv).astype(jnp.bfloat16)
    grad_qkv, qkv_grad, out_piece = stage([unit_line], grad_qkv, qkv_grad, out_piece)
    unit_line.step()
    qkv_piece = reduce_pair(qkv_grad)
    first_part = col_product(grad_qkv, qkv_w).astype(jnp.bfloat16)

    first_line = add_up(blocks_of(first_part))
    first_line.step()
    layer_rows = ((middle + BRANCH_SCALE * mlp_line.total()) * live_own).astype(jnp.bfloat16)
    (layer_rows,) = stage([unit_line, first_line], layer_rows)
    unit_line.step()
    first_line.step()
    qkv_marks = gain_marks(qkv_mine, qkv_piece)
    head_block = jnp.concatenate(
        [qkv_piece[:, :head_cols], qkv_marks, qkv_piece[:, head_cols + 2 :], out_piece], axis=1
    )
    (head_block,) = stage([unit_line, first_line], head_block)
    head_line = walk(head_block)
    head_line.step()
    first_line.step()
    own, other, give = line_pieces(unit_line)
    final_gate, final_up, final_down = join_columns(
        core_index, own, other, 3, unit_cols, unit_cols
    )
    final_gain_two = gain_total((own, give), 3 * unit_cols, mlp_gain)
    final_gate, final_up, final_down = stage(
        [first_line, head_line], final_gate, final_up, final_down
    )
    head_line.step()
    grad_first = first_line.total()
    normed_one, inverse_one = norm_parts(own_x)
    grad_rows = grad_middle + norm_back(grad_first, normed_one, inverse_one, gain_a)
    (grad_rows,) = stage([head_line], grad_rows)
    head_line.step()

    def both_slots(own):
        other = lax.ppermute(own, "tensor", swap_pairs())
        return jnp.stack(
            [jnp.where(core == 0, own, other), jnp.where(core == 0, other, own)], axis=0
        )

    layer_out = both_slots(layer_rows)
    grad_tokens = both_slots(grad_rows.astype(jnp.bfloat16)).astype(jnp.float32)
    layer_out, grad_tokens = stage([head_line], layer_out, grad_tokens)
    own, other, give = line_pieces(head_line)
    final_query, final_key, final_value, final_out = join_columns(
        core_index, own, other, 4, pad_cols, head_cols
    )
    final_gain_one = gain_total((own, give), head_cols, attn_gain)
    return (
        layer_out,
        grad_tokens,
        final_gain_one,
        final_query,
        final_key,
        final_value,
        jnp.transpose(final_out),
        final_gain_two,
        final_gate,
        final_up,
        jnp.transpose(final_down),
    )


def heads_of(w_query, cores, lines):
    return w_query.shape[1] * cores // lines


def local(shape, *arrays):
    shards, lines, cores = shape["shard"], shape["ctx"], shape["tensor"]
    tokens, w_query, w_gate = arrays[0], arrays[4], arrays[9]
    fits = (
        cores == 2
        and tokens.shape[0] == cores
        and lines % cores == 0
        and lines == 4
        and (w_query.shape[1] * cores) % (lines * HD) == 0
        and (w_gate.shape[1] * cores) % (lines * cores) == 0
        and w_query.shape[0] % cores == 0
        and -(-heads_of(w_query, cores, lines) // LANES) * LANES >= heads_of(w_query, cores, lines) + 2
    )
    if fits:
        return column_split(shape, *arrays)
    return gather_all(*arrays)


def solution(mesh):
    placed = (
        P("shard", "ctx", None),
        P("shard"),
        P(),
        P("shard"),
        P("shard", "tensor"),
        P("shard", "tensor"),
        P("shard", "tensor"),
        P("tensor", "shard"),
        P("shard"),
        P("shard", "tensor"),
        P("shard", "tensor"),
        P("tensor", "shard"),
        P("shard", "ctx", None),
    )
    return jax.shard_map(
        functools.partial(local, dict(mesh.shape)),
        mesh=mesh,
        in_specs=placed,
        out_specs=(
            P("shard", "ctx", None),
            P("shard", "ctx", None),
            P("shard"),
            P("shard", "tensor"),
            P("shard", "tensor"),
            P("shard", "tensor"),
            P("tensor", "shard"),
            P("shard"),
            P("shard", "tensor"),
            P("shard", "tensor"),
            P("tensor", "shard"),
        ),
        check_vma=False,
    )
```
